32 devices in a mesh: dp: 16 (over z, y, x), mp: 2 (over core).
Axes of the slice: x: 2, y: 2, z: 4, core: 2. Of those that a mesh axis runs over, the one named last changes fastest.
Arguments:
- patch_rows: bfloat16 [32, 384, 768], P('dp'), may hold values from -6 to 6
- cotangent: bfloat16 [32, 34, 16, 768], P(None, None, 'dp', 'mp'), may hold values from -6 to 6
- mask_token: bfloat16 [768], P('mp'), may hold values from -6 to 6
- lengths: int32 [32], replicated, may hold values from 66 to 529, as said below
- masked: int32 [32, 529], replicated, may hold values from 0 to 1, as said below
- dealing: int32 [32], replicated, may hold values from 0 to 31, each once
- qkv_master: float32 [2, 884736], P('mp', 'dp'), may hold values from -0.21875 to 0.21875
- qkv_first: float32 [2, 884736], P('mp', 'dp'), may hold values from -48 to 48
- qkv_second: float32 [2, 884736], P('mp', 'dp'), may hold values from 2.94912 to 47.18592
- out_master: float32 [2, 294912], P('mp', 'dp'), may hold values from -3.5 to 3.5
- out_first: float32 [2, 294912], P('mp', 'dp'), may hold values from -6 to 6
- out_second: float32 [2, 294912], P('mp', 'dp'), may hold values from 0.0466944 to 0.73728
- fc1_master: float32 [2, 1179648], P('mp', 'dp'), may hold values from -0.21875 to 0.21875
- fc1_first: float32 [2, 1179648], P('mp', 'dp'), may hold values from -20 to 20
- fc1_second: float32 [2, 1179648], P('mp', 'dp'), may hold values from 0.4153344 to 6.63552
- fc2_master: float32 [2, 1179648], P('mp', 'dp'), may hold values from -0.109375 to 0.109375
- fc2_first: float32 [2, 1179648], P('mp', 'dp'), may hold values from -40 to 40
- fc2_second: float32 [2, 1179648], P('mp', 'dp'), may hold values from 1.65888 to 26.54208
- rep_master: float32 [6, 768], replicated
- rep_first: float32 [6, 768], replicated, may hold values from -64 to 64
- rep_second: float32 [6, 768], replicated, may hold values from 4.608 to 73.728
- split_master: float32 [2, 6, 384], P('mp'), may hold values from -1.2 to 1.2
- split_first: float32 [2, 6, 384], P('mp'), may hold values from -64 to 64
- split_second: float32 [2, 6, 384], P('mp'), may hold values from 4.608 to 73.728
Outputs:
- full_out: bfloat16 [32, 34, 16, 768], P(None, None, 'dp', 'mp')
- input_grad: float32 [32, 384, 768], P('dp')
- mask_grad: float32 [768], P('mp')
- qkv_new: float32 [2, 884736], P('mp', 'dp')
- qkv_first_new: float32 [2, 884736], P('mp', 'dp')
- qkv_second_new: float32 [2, 884736], P('mp', 'dp')
- out_new: float32 [2, 294912], P('mp', 'dp')
- out_first_new: float32 [2, 294912], P('mp', 'dp')
- out_second_new: float32 [2, 294912], P('mp', 'dp')
- fc1_new: float32 [2, 1179648], P('mp', 'dp')
- fc1_first_new: float32 [2, 1179648], P('mp', 'dp')
- fc1_second_new: float32 [2, 1179648], P('mp', 'dp')
- fc2_new: float32 [2, 1179648], P('mp', 'dp')
- fc2_first_new: float32 [2, 1179648], P('mp', 'dp')
- fc2_second_new: float32 [2, 1179648], P('mp', 'dp')
- rep_new: float32 [6, 768], replicated
- rep_first_new: float32 [6, 768], replicated
- rep_second_new: float32 [6, 768], replicated
- split_new: float32 [2, 6, 384], P('mp')
- split_first_new: float32 [2, 6, 384], P('mp')
- split_second_new: float32 [2, 6, 384], P('mp')
The draws below stay inside these ranges and needn't reach their ends.
Inputs may be any that keep to these rules, and one draw needn't show every extreme that they name: `lengths`: some strips have full length 529, at least one in every draw; the others lie between 66 and 396. `masked`: masked positions lie within the text; a strip of length L has max(L - 384, L // 4) of them, so at most 384 of its patches are visible, exactly 384 for a full-length strip. `dealing`: each strip stands in exactly one slot.
All inputs are finite; a program needn't handle non-finite values.
Results may differ from the reference program's by a relative error of at most 0.012.
Values may be sent and summed in bfloat16 or wider, within the bound.
No kernel may reach another device: no remote copies, remote signals or barrier semaphores. Data moves between devices by JAX's collectives and lax.ppermute only.
A program may use at most 960 MiB of HBM per device.

```python
import math
import jax
import jax.numpy as jnp
from jax import lax

D = 768
HEADS = 12
HEAD = 64
FF = 3072
PATCHES = 529
CAP = 384
STEP = 10
STRIPS = 32
PAIRS = 16
POS_DEV = 34
DPART = 384
FPART = 1536
N_DP = 16
N_MP = 2


def strip_plan(key):
    base = jax.random.fold_in(key, 7)
    kind_key, length_key, pick_key = jax.random.split(base, 3)
    dense = jax.random.randint(kind_key, (STRIPS,), 0, 2)
    forced = jax.random.randint(pick_key, (), 0, STRIPS)
    dense = jnp.where(jnp.arange(STRIPS) == forced, 1, dense)
    sparse_length = jax.random.randint(length_key, (STRIPS,), PATCHES // 8, 3 * PATCHES // 4 + 1)
    return jnp.where(dense == 1, PATCHES, sparse_length).astype(jnp.int32)


def draw_lengths(key, part):
    return strip_plan(key)


def draw_masked(key, part):
    lengths = strip_plan(key)
    position = jnp.arange(PATCHES, dtype=jnp.int32)
    score = jax.random.randint(jax.random.fold_in(key, 11), (STRIPS, PATCHES), 0, 1 << 20)
    score = score * 1024 + position[None, :]
    score = jnp.where(position[None, :] < lengths[:, None], score, (1 << 30) + position[None, :])
    order_rank = jnp.argsort(jnp.argsort(score, axis=1), axis=1)
    quota = jnp.maximum(lengths - CAP, lengths // 4)
    return (order_rank < quota[:, None]).astype(jnp.int32)


def draw_rep_master(key, part):
    noise = jax.random.normal(key, (6, D), jnp.float32)
    row_index = jnp.arange(6)[:, None]
    gain_rows = (row_index == 0) | (row_index == 2)
    return jnp.where(gain_rows, 1.0 + 0.15 * noise, 0.2 * noise).astype(jnp.float32)


def levels(own_key, dims, pieces, low, high):
    gain, own = 1.0, jax.random.fold_in(own_key, 6)
    for dim, shards_of in pieces:
        heights = jnp.exp(jax.random.uniform(jax.random.fold_in(own, dim), (shards_of,), jnp.float32, low / len(pieces), high / len(pieces)))
        gain = gain * jnp.repeat(heights, dims[dim] // shards_of).reshape([-1 if axis == dim else 1 for axis in range(len(dims))])
    return gain


def scatter_about(stream_key, extent, width, reach, pieces=(), kind=jnp.bfloat16):
    values = width * jax.random.normal(stream_key, extent, jnp.float32)
    if pieces:
        values = values * levels(stream_key, extent, pieces, -0.22, 0.18)
    return jnp.clip(values, -reach, reach).astype(kind)


def setup_inputs(seed: int = 0) -> dict:
    splits = jax.random.split(jax.random.key(seed), 25)
    return {
        "patch_rows": scatter_about(splits[0], (STRIPS, CAP, D), 1.0, 6.0, ((0, 16),)),
        "cotangent": scatter_about(splits[1], (STRIPS, POS_DEV, N_DP, D), 1.0, 6.0, ((2, 16), (3, 2))),
        "mask_token": scatter_about(splits[2], (D,), 1.0, 6.0, ((0, 2),)),
        "lengths": draw_lengths(jax.random.fold_in(splits[24], 71), 0),
        "masked": draw_masked(jax.random.fold_in(splits[24], 71), 0),
        "dealing": jax.random.permutation(splits[5], STRIPS).astype(jnp.int32),
        "qkv_master": scatter_about(splits[6], (N_MP, 3 * D * DPART), D ** -0.5, 0.21875, ((0, 2), (1, 16)), jnp.float32),
        "qkv_first": scatter_about(splits[7], (N_MP, 3 * D * DPART), (0.077 * (STRIPS * CAP) ** 0.5), 48.0, ((0, 2), (1, 16)), jnp.float32),
        "qkv_second": jnp.clip(jnp.exp(math.log(47.18592) - 2.7725887 * jax.random.uniform(splits[8], (N_MP, 3 * D * DPART), jnp.float32) ** levels(splits[8], (N_MP, 3 * D * DPART), ((0, 2), (1, 16)), -0.2, 0.2)), 2.94912, 47.18592),
        "out_master": scatter_about(splits[9], (N_MP, DPART * D), (D * 3 // (2 * CAP)) ** -0.5, 3.5, ((0, 2), (1, 16)), jnp.float32),
        "out_first": scatter_about(splits[10], (N_MP, DPART * D), (0.0096 * (STRIPS * CAP) ** 0.5), 6.0, ((0, 2), (1, 16)), jnp.float32),
        "out_second": jnp.clip(jnp.exp(math.log(0.73728) - 2.7593435 * jax.random.uniform(splits[11], (N_MP, DPART * D), jnp.float32) ** levels(splits[11], (N_MP, DPART * D), ((0, 2), (1, 16)), -0.2, 0.2)), 0.0466944, 0.73728),
        "fc1_master": scatter_about(splits[12], (N_MP, D * FPART), D ** -0.5, 0.21875, ((0, 2), (1, 16)), jnp.float32),
        "fc1_first": scatter_about(splits[13], (N_MP, D * FPART), (0.029 * (STRIPS * CAP) ** 0.5), 20.0, ((0, 2), (1, 16)), jnp.float32),
        "fc1_second": jnp.clip(jnp.exp(math.log(6.63552) - 2.7711083 * jax.random.uniform(splits[14], (N_MP, D * FPART), jnp.float32) ** levels(splits[14], (N_MP, D * FPART), ((0, 2), (1, 16)), -0.2, 0.2)), 0.4153344, 6.63552),
        "fc2_master": scatter_about(splits[15], (N_MP, FPART * D), FF ** -0.5, 0.109375, ((0, 2), (1, 16)), jnp.float32),
        "fc2_first": scatter_about(splits[16], (N_MP, FPART * D), (0.058 * (STRIPS * CAP) ** 0.5), 40.0, ((0, 2), (1, 16)), jnp.float32),
        "fc2_second": jnp.clip(jnp.exp(math.log(26.54208) - 2.7725887 * jax.random.uniform(splits[17], (N_MP, FPART * D), jnp.float32) ** levels(splits[17], (N_MP, FPART * D), ((0, 2), (1, 16)), -0.2, 0.2)), 1.65888, 26.54208),
        "rep_master": draw_rep_master(jax.random.fold_in(splits[24], 71), 0),
        "rep_first": scatter_about(splits[19], (6, D), (0.096 * (STRIPS * CAP) ** 0.5), 64.0, (), jnp.float32),
        "rep_second": jnp.clip(jnp.exp(jax.random.uniform(splits[20], (6, D), jnp.float32, math.log(4.608), math.log(73.728))), 4.608, 73.728),
        "split_master": scatter_about(splits[21], (N_MP, 2 + FF // D, DPART), 0.2, 1.2, ((0, 2),), jnp.float32),
        "split_first": scatter_about(splits[22], (N_MP, 2 + FF // D, DPART), (0.096 * (STRIPS * CAP) ** 0.5), 64.0, ((0, 2),), jnp.float32),
        "split_second": jnp.clip(jnp.exp(math.log(73.728) - 2.7725887 * jax.random.uniform(splits[23], (N_MP, 2 + FF // D, DPART), jnp.float32) ** levels(splits[23], (N_MP, 2 + FF // D, DPART), ((0, 2),), -0.2, 0.2)), 4.608, 73.728),
    }


@jax.custom_vjp
def low(v):
    return lax.optimization_barrier(v.astype(jnp.bfloat16)).astype(jnp.float32)

@jax.custom_vjp
def low_back(v):
    return v

def low_keep(v):
    return (low(v), None)

def low_pass(kept, grad):
    return (grad,)

def back_keep(v):
    return (v, None)

def back_low(kept, grad):
    return (low(grad),)
low.defvjp(low_keep, low_pass)
low_back.defvjp(back_keep, back_low)
PRECISE = lax.Precision.HIGHEST
NORM_EPS = 1e-06
BETA_ONE = 0.9
BETA_TWO = 0.999
ADAM_EPS = 1e-08
MATRIX_RATE = 0.15
MATRIX_DECAY = 0.05
VECTOR_RATE = 0.6

def layer_norm(signal, norm_gain, norm_shift):
    average = lax.optimization_barrier(jnp.mean(signal, axis=-1, keepdims=True))
    centered = signal - average
    spread = lax.optimization_barrier(jnp.mean(centered * centered, axis=-1, keepdims=True))
    return centered * lax.rsqrt(spread + NORM_EPS) * norm_gain + norm_shift

def rounded_both(signal):
    return low(low_back(signal))

def exact_gelu(signal):
    return jax.nn.gelu(signal, approximate=False)

def project(left, right):
    return jnp.dot(left, right, precision=PRECISE)

def pair_attention(pair_block):
    queries, key_rows, value_rows, valid_rows = pair_block
    length = queries.shape[0]
    head_queries = queries.reshape(length, HEADS, HEAD)
    head_keys = key_rows.reshape(length, HEADS, HEAD)
    head_values = value_rows.reshape(length, HEADS, HEAD)
    scores = jnp.einsum('qhd,khd->hqk', head_queries, head_keys, precision=PRECISE) * HEAD ** (-0.5)
    scores = low_back(scores)
    scores = jnp.where(valid_rows[None, None, :], scores, -1e+30)
    row_max = lax.optimization_barrier(jnp.max(scores, axis=2, keepdims=True))
    lifted = jnp.exp(scores - row_max)
    probability = lifted / lax.optimization_barrier(jnp.sum(lifted, axis=2, keepdims=True))
    attended = jnp.einsum('hqk,khd->qhd', low(probability), head_values, precision=PRECISE)
    return attended.reshape(length, D)

def restore_forward(patch_input, qkv_master, out_master, fc1_master, fc2_master, rep_master, split_master, mask_vector, valid_rows, visible, rank, inverse):
    part_width = D // N_MP
    qkv_blocks = low(qkv_master).reshape(N_MP, D, 3, part_width)
    joined = jnp.transpose(qkv_blocks, (1, 2, 0, 3)).reshape(D, 3, D)
    w_output = low(out_master).reshape(D, D)
    fc_one = jnp.transpose(low(fc1_master).reshape(N_MP, D, FF // N_MP), (1, 0, 2)).reshape(D, FF)
    fc_two = low(fc2_master).reshape(FF, D)
    bias_query = split_master[:, 0, :].reshape(D)
    bias_value = split_master[:, 1, :].reshape(D)
    bias_hidden = split_master[:, 2:, :].reshape(FF)
    normed = low(layer_norm(patch_input, rep_master[0], rep_master[1]))
    queries = rounded_both(project(normed, joined[:, 0]) + bias_query)
    key_rows = rounded_both(project(normed, joined[:, 1]))
    value_rows = rounded_both(project(normed, joined[:, 2]) + bias_value)
    pair_shape = (PAIRS, 2 * CAP, D)
    attended = lax.map(jax.checkpoint(pair_attention), (queries.reshape(pair_shape), key_rows.reshape(pair_shape), value_rows.reshape(pair_shape), valid_rows.reshape(PAIRS, 2 * CAP)))
    attended = rounded_both(attended.reshape(STRIPS * CAP, D))
    branch = low_back(project(attended, w_output) + rep_master[4])
    middle = patch_input + branch
    normed_two = low(layer_norm(middle, rep_master[2], rep_master[3]))
    hidden = low_back(project(normed_two, fc_one) + bias_hidden)
    active = low(exact_gelu(hidden))
    second = low_back(project(active, fc_two) + rep_master[5])
    result = low(middle + second).reshape(STRIPS, CAP, D)
    picked = result[inverse[:, None], jnp.maximum(rank, 0)]
    filled = jnp.where(visible[:, :, None], picked, mask_vector[None, None, :])
    tail = jnp.zeros((STRIPS, POS_DEV * N_DP - PATCHES, D), jnp.float32)
    return jnp.concatenate([filled, tail], axis=1).reshape(STRIPS, POS_DEV, N_DP, D)

def adam_step(weight, moment_one, moment_two, gradient, step_rate, decay_rate):
    one_new = BETA_ONE * moment_one + (1.0 - BETA_ONE) * gradient
    two_new = BETA_TWO * moment_two + (1.0 - BETA_TWO) * gradient * gradient
    one_hat = one_new / (1.0 - BETA_ONE ** STEP)
    two_hat = two_new / (1.0 - BETA_TWO ** STEP)
    weight_new = weight - step_rate * (one_hat / (jnp.sqrt(two_hat) + ADAM_EPS) + decay_rate * weight)
    return (weight_new, one_new, two_new)

def reference(patch_rows, cotangent, mask_token, lengths, masked, dealing, qkv_master, qkv_first, qkv_second, out_master, out_first, out_second, fc1_master, fc1_first, fc1_second, fc2_master, fc2_first, fc2_second, rep_master, rep_first, rep_second, split_master, split_first, split_second):
    patch_index = jnp.arange(PATCHES, dtype=jnp.int32)
    visible = (patch_index[None, :] < lengths[:, None]) & (masked == 0)
    rank = jnp.cumsum(visible.astype(jnp.int32), axis=1) - 1
    counts = lax.optimization_barrier(jnp.sum(visible.astype(jnp.int32), axis=1))
    valid_rows = jnp.arange(CAP, dtype=jnp.int32)[None, :] < counts[dealing][:, None]
    inverse = jnp.argsort(dealing).astype(jnp.int32)

    def restored(patch_input, qkv_param, out_param, fc1_param, fc2_param, rep_param, split_param, mask_vector):
        return restore_forward(patch_input, qkv_param, out_param, fc1_param, fc2_param, rep_param, split_param, mask_vector, valid_rows, visible, rank, inverse)
    full_out, pullback = jax.vjp(restored, patch_rows.astype(jnp.float32).reshape(STRIPS * CAP, D), qkv_master, out_master, fc1_master, fc2_master, rep_master, split_master, mask_token.astype(jnp.float32))
    gradients = pullback(cotangent.astype(jnp.float32))
    input_grad = gradients[0].reshape(STRIPS, CAP, D)
    qkv_new = adam_step(qkv_master, qkv_first, qkv_second, gradients[1], MATRIX_RATE, MATRIX_DECAY)
    out_new = adam_step(out_master, out_first, out_second, gradients[2], MATRIX_RATE, MATRIX_DECAY)
    fc1_new = adam_step(fc1_master, fc1_first, fc1_second, gradients[3], MATRIX_RATE, MATRIX_DECAY)
    fc2_new = adam_step(fc2_master, fc2_first, fc2_second, gradients[4], MATRIX_RATE, MATRIX_DECAY)
    rep_new = adam_step(rep_master, rep_first, rep_second, gradients[5], VECTOR_RATE, 0.0)
    split_new = adam_step(split_master, split_first, split_second, gradients[6], VECTOR_RATE, 0.0)
    return (full_out.astype(jnp.bfloat16), input_grad, gradients[7], qkv_new[0], qkv_new[1], qkv_new[2], out_new[0], out_new[1], out_new[2], fc1_new[0], fc1_new[1], fc1_new[2], fc2_new[0], fc2_new[1], fc2_new[2], rep_new[0], rep_new[1], rep_new[2], split_new[0], split_new[1], split_new[2])
```

```python
import jax
import jax.numpy as jnp
from jax import lax
from jax.experimental import pallas as pl
from jax.experimental.pallas import tpu as pltpu
from jax.sharding import PartitionSpec as P

HEAD = 64
PATCHES = 529
STEP = 10


NORM_EPS = 1e-06
BETA_ONE = 0.9
BETA_TWO = 0.999
ADAM_EPS = 1e-08
MATRIX_RATE = 0.15
MATRIX_DECAY = 0.05
VECTOR_RATE = 0.6


def layer_norm(signal, norm_gain, norm_shift):
    average = jnp.mean(signal, axis=-1, keepdims=True)
    centered = signal - average
    spread = jnp.mean(centered * centered, axis=-1, keepdims=True)
    return centered * lax.rsqrt(spread + NORM_EPS) * norm_gain + norm_shift


def exact_gelu(signal):
    return jax.nn.gelu(signal, approximate=False)


def product(left, right):
    return jnp.dot(left, right, preferred_element_type=jnp.float32)


def contract_last(left, right):
    return lax.dot_general(
        left, right, (((1,), (1,)), ((), ())), preferred_element_type=jnp.float32
    )


def contract_rows(left, right):
    return lax.dot_general(
        left, right, (((0,), (0,)), ((), ())), preferred_element_type=jnp.float32
    )


def adam_step(weight, moment_one, moment_two, gradient, step_rate, decay_rate):
    one_new = BETA_ONE * moment_one + (1.0 - BETA_ONE) * gradient
    two_new = BETA_TWO * moment_two + (1.0 - BETA_TWO) * gradient * gradient
    one_hat = one_new / (1.0 - BETA_ONE**STEP)
    two_hat = two_new / (1.0 - BETA_TWO**STEP)
    weight_new = weight - step_rate * (
        one_hat / (jnp.sqrt(two_hat) + ADAM_EPS) + decay_rate * weight
    )
    return (weight_new, one_new, two_new)


def total_over_cores(partial):
    return partial.astype(jnp.float32) + swap_cores(partial).astype(jnp.float32)


def pair_scores(queries, key_rows, valid_rows):
    scores = jnp.einsum(
        "qhd,khd->hqk", queries, key_rows, preferred_element_type=jnp.float32
    ) * HEAD ** (-0.5)
    return jnp.where(valid_rows[None, None, :], scores, -1e30)


def attend_pair(pair_block):
    queries, key_rows, value_rows, valid_rows = pair_block
    scores = pair_scores(queries, key_rows, valid_rows)
    row_max = jnp.max(scores, axis=2, keepdims=True)
    lifted = jnp.exp(scores - row_max)
    row_total = jnp.sum(lifted, axis=2, keepdims=True)
    probability = (lifted / row_total).astype(jnp.bfloat16)
    attended = jnp.einsum(
        "hqk,khd->qhd", probability, value_rows, preferred_element_type=jnp.float32
    )
    return (attended.astype(jnp.bfloat16), row_max[:, :, 0] + jnp.log(row_total[:, :, 0]))


def attend_pair_back(pair_block):
    queries, key_rows, value_rows, valid_rows, log_total, grad_attended = pair_block
    scores = pair_scores(queries, key_rows, valid_rows)
    probability = jnp.exp(scores - log_total[:, :, None])
    grad_prob = jnp.einsum(
        "qhd,khd->hqk", grad_attended, value_rows, preferred_element_type=jnp.float32
    )
    inner_sum = jnp.sum(probability * grad_prob, axis=2, keepdims=True)
    grad_scores = (probability * (grad_prob - inner_sum)).astype(jnp.bfloat16)
    score_scale = HEAD ** (-0.5)
    grad_queries = (
        jnp.einsum("hqk,khd->qhd", grad_scores, key_rows, preferred_element_type=jnp.float32)
        * score_scale
    )
    grad_keys = (
        jnp.einsum("hqk,qhd->khd", grad_scores, queries, preferred_element_type=jnp.float32)
        * score_scale
    )
    grad_values = jnp.einsum(
        "hqk,qhd->khd",
        probability.astype(jnp.bfloat16),
        grad_attended,
        preferred_element_type=jnp.float32,
    )
    return (
        grad_queries.astype(jnp.bfloat16),
        grad_keys.astype(jnp.bfloat16),
        grad_values.astype(jnp.bfloat16),
    )


def hop(array, distance, axis_count):
    return lax.ppermute(array, "dp", [(i, i ^ distance) for i in range(axis_count)])


def swap_cores(array):
    return lax.ppermute(array, "mp", [(0, 1), (1, 0)])


def place_chunks(pieces, chunk_ids, member, count):
    rows, width = pieces[0].shape[1:]

    def body(member_ref, *refs):
        sources, target, semaphores = refs[:-2], refs[-2], refs[-1]
        copies = []
        for source, ids in zip(sources, chunk_ids):
            for place, distance in enumerate(ids):
                copies.append(
                    pltpu.make_async_copy(
                        source.at[place],
                        target.at[member_ref[0] ^ distance],
                        semaphores.at[len(copies)],
                    )
                )
        for copy in copies:
            copy.start()
        for copy in copies:
            copy.wait()

    return pl.pallas_call(
        body,
        in_specs=[pl.BlockSpec(memory_space=pltpu.SMEM)]
        + [pl.BlockSpec(memory_space=pl.ANY)] * len(pieces),
        out_specs=pl.BlockSpec(memory_space=pltpu.VMEM),
        out_shape=jax.ShapeDtypeStruct((count, rows, width), pieces[0].dtype),
        scratch_shapes=[pltpu.SemaphoreType.DMA((count,))],
        cost_estimate=pl.CostEstimate(
            flops=0, transcendentals=0, bytes_accessed=4 * count * rows * width
        ),
        name="place_chunks",
    )(member, *pieces)


def pick_chunks(whole, chunk_ids, member):
    count, rows, width = whole.shape

    def body(member_ref, source, *refs):
        targets, semaphores = refs[:-1], refs[-1]
        copies = []
        for target, ids in zip(targets, chunk_ids):
            for place, distance in enumerate(ids):
                copies.append(
                    pltpu.make_async_copy(
                        source.at[member_ref[0] ^ distance],
                        target.at[place],
                        semaphores.at[len(copies)],
                    )
                )
        for copy in copies:
            copy.start()
        for copy in copies:
            copy.wait()

    return pl.pallas_call(
        body,
        in_specs=[pl.BlockSpec(memory_space=pltpu.SMEM), pl.BlockSpec(memory_space=pltpu.VMEM)],
        out_specs=[pl.BlockSpec(memory_space=pl.ANY)] * len(chunk_ids),
        out_shape=[
            jax.ShapeDtypeStruct((len(ids), rows, width), whole.dtype) for ids in chunk_ids
        ],
        scratch_shapes=[pltpu.SemaphoreType.DMA((count,))],
        cost_estimate=pl.CostEstimate(
            flops=0, transcendentals=0, bytes_accessed=4 * count * rows * width
        ),
        name="pick_chunks",
    )(member, whole)


def gather_chunks(chunk, member, count):
    own = chunk[None]
    if count == 16:
        near, far, last = (hop(own, k, count) for k in (4, 8, 12))
        first, second = jnp.concatenate([own, near]), jnp.concatenate([far, last])
        x_first, x_second = hop(first, 1, count), hop(second, 1, count)
        y_first, y_second = hop(first, 2, count), hop(second, 2, count)
        d_first, d_second = hop(y_first, 1, count), hop(x_second, 2, count)
        pieces = [first, second, x_first, x_second, y_first, y_second, d_first, d_second]
        ids = [(0, 4), (8, 12), (1, 5), (9, 13), (2, 6), (10, 14), (3, 7), (11, 15)]
    else:
        held, step = own, 1
        while step < count:
            held = jnp.concatenate([held, hop(held, step, count)])
            step *= 2
        pieces, ids = [held], [tuple(range(count))]
    return place_chunks(pieces, ids, member, count)


def scatter_chunks(whole, member, count):
    def wide(array):
        return array.astype(jnp.float32)

    if count == 16:
        ids = [(3, 7), (11, 15), (2, 6), (9, 13), (10, 14), (1, 5), (0, 4), (8, 12)]
        d_first, d_second, y_first, x_second, y_second, x_first, first, second = pick_chunks(
            whole, ids, member
        )
        d_first, d_second = hop(d_first, 1, count), hop(d_second, 2, count)
        y_second, x_first = hop(y_second, 2, count), hop(x_first, 1, count)
        y_first = hop((wide(y_first) + wide(d_first)).astype(jnp.bfloat16), 2, count)
        x_second = hop((wide(x_second) + wide(d_second)).astype(jnp.bfloat16), 1, count)
        first = wide(first) + wide(y_first) + wide(x_first)
        second = wide(second) + wide(y_second) + wide(x_second)
        near = hop(first[1].astype(jnp.bfloat16), 4, count)
        far = hop(second[0].astype(jnp.bfloat16), 8, count)
        last = hop(second[1].astype(jnp.bfloat16), 12, count)
        return first[0] + wide(near) + wide(far) + wide(last)
    (held,) = pick_chunks(whole, [tuple(range(count))], member)
    held = wide(held)
    step = count // 2
    while step:
        held = held[:step] + wide(hop(held[step:].astype(jnp.bfloat16), step, count))
        step //= 2
    return held[0]


def sum_over_dp(vector, count):
    if count == 16:
        for low, high in ((1, 2), (4, 8)):
            other, third, fourth = (hop(vector, k, count) for k in (low, high, low + high))
            vector = (vector + other) + (third + fourth)
        return vector
    step = 1
    while step < count:
        vector = vector + hop(vector, step, count)
        step *= 2
    return vector


def on_device(
    patch_rows,
    cotangent,
    mask_token,
    lengths,
    masked,
    dealing,
    qkv_master,
    qkv_first,
    qkv_second,
    out_master,
    out_first,
    out_second,
    fc1_master,
    fc1_first,
    fc1_second,
    fc2_master,
    fc2_first,
    fc2_second,
    rep_master,
    rep_first,
    rep_second,
    split_master,
    split_first,
    split_second,
):
    slot_count, capacity, feature_width = patch_rows.shape
    half_width = mask_token.shape[0]
    dp_count = lax.axis_size("dp")
    member = lax.axis_index("dp")
    core_index = lax.axis_index("mp")
    positions_here = cotangent.shape[1]
    position_span = positions_here * dp_count
    heads_here = half_width // HEAD
    hidden_width = (split_master.shape[1] - 2) * half_width
    row_count = slot_count * capacity
    pair_count = slot_count // 2
    pair_length = 2 * capacity
    patch_index = jnp.arange(PATCHES, dtype=jnp.int32)
    visible_all = (patch_index[None, :] < lengths[:, None]) & (masked == 0)
    strips_here = lax.dynamic_slice_in_dim(dealing, member * slot_count, slot_count)
    visible_here = visible_all[strips_here]
    rank_here = jnp.cumsum(visible_here.astype(jnp.int32), axis=1) - 1
    counts_here = jnp.sum(visible_here.astype(jnp.int32), axis=1)
    valid_rows = jnp.arange(capacity, dtype=jnp.int32)[None, :] < counts_here[:, None]
    padding = position_span - PATCHES
    visible_padded = jnp.pad(visible_here, ((0, 0), (0, padding)))
    rank_padded = jnp.pad(jnp.maximum(rank_here, 0), ((0, 0), (0, padding)))
    own_positions = jnp.arange(positions_here, dtype=jnp.int32) * dp_count + member
    inside = own_positions < PATCHES
    visible_own = visible_all[:, jnp.minimum(own_positions, PATCHES - 1)] & inside[None, :]
    strip_count = lengths.shape[0]
    held_count = strip_count * positions_here
    strip_row = (
        jnp.arange(positions_here, dtype=jnp.int32)[None, :] * strip_count + dealing[:, None]
    ).reshape(held_count)
    deal = (
        strip_row[:, None] == jnp.arange(held_count, dtype=jnp.int32)[None, :]
    ).astype(jnp.bfloat16)
    encoder_row = jnp.where(
        visible_padded,
        rank_padded + jnp.arange(slot_count, dtype=jnp.int32)[:, None] * capacity,
        -1,
    )
    encoder_row = jnp.transpose(
        encoder_row.reshape(slot_count, positions_here, dp_count), (2, 0, 1)
    ).reshape(held_count)
    pick = (
        jnp.arange(row_count, dtype=jnp.int32)[:, None] == encoder_row[None, :]
    ).astype(jnp.bfloat16)
    unseen = jnp.transpose(jnp.logical_not(visible_own) & inside[None, :]).reshape(held_count)
    member_word = member.astype(jnp.int32).reshape(1)

    cotangent_rows = jnp.transpose(cotangent.reshape(strip_count, positions_here, half_width), (1, 0, 2))
    cotangent_rows = cotangent_rows.reshape(held_count, half_width)
    dealt = product(deal, cotangent_rows).astype(jnp.bfloat16)
    returned = lax.all_to_all(
        dealt.reshape(dp_count, slot_count * positions_here, half_width),
        "dp",
        split_axis=0,
        concat_axis=0,
        tiled=True,
    ).reshape(held_count, half_width)
    gathered = product(pick, returned).astype(jnp.bfloat16)
    gathered_other = swap_cores(gathered)
    grad_out = jnp.where(
        core_index == 0,
        jnp.concatenate([gathered, gathered_other], axis=1),
        jnp.concatenate([gathered_other, gathered], axis=1),
    )
    mask_grad = product(unseen.astype(jnp.bfloat16)[None, :], cotangent_rows)[0]

    def gathered_matrix(master, rows, width):
        chunk = master.astype(jnp.bfloat16).reshape(rows // dp_count, width)
        return gather_chunks(chunk, member_word, dp_count).reshape(rows, width)

    w_attention = gathered_matrix(qkv_master, feature_width, 3 * half_width)
    w_output = gathered_matrix(out_master, half_width, feature_width)
    w_first = gathered_matrix(fc1_master, feature_width, hidden_width)
    w_second = gathered_matrix(fc2_master, hidden_width, feature_width)
    inputs = patch_rows.reshape(row_count, feature_width).astype(jnp.float32)
    normed_full, norm_back_one = jax.vjp(layer_norm, inputs, rep_master[0], rep_master[1])
    normed = normed_full.astype(jnp.bfloat16)
    projected = product(normed, w_attention).reshape(row_count, 3, half_width)
    queries = (projected[:, 0] + split_master[0, 0]).astype(jnp.bfloat16)
    key_rows = projected[:, 1].astype(jnp.bfloat16)
    value_rows = (projected[:, 2] + split_master[0, 1]).astype(jnp.bfloat16)

    def by_pair(array):
        return array.reshape(pair_count, pair_length, heads_here, HEAD)

    pair_valid = valid_rows.reshape(pair_count, pair_length)
    attended, log_total = lax.map(
        attend_pair, (by_pair(queries), by_pair(key_rows), by_pair(value_rows), pair_valid)
    )
    attended = attended.reshape(row_count, half_width)
    branch = total_over_cores(product(attended, w_output)) + rep_master[4]
    middle = inputs + branch
    normed_two_full, norm_back_two = jax.vjp(layer_norm, middle, rep_master[2], rep_master[3])
    normed_two = normed_two_full.astype(jnp.bfloat16)
    hidden = product(normed_two, w_first) + split_master[0, 2:].reshape(hidden_width)
    active_full, gelu_back = jax.vjp(exact_gelu, hidden)
    active = active_full.astype(jnp.bfloat16)
    second = total_over_cores(product(active, w_second).astype(jnp.bfloat16)) + rep_master[5]
    result = (middle + second).astype(jnp.bfloat16)
    result_half = lax.dynamic_slice_in_dim(result, core_index * half_width, half_width, 1)
    outgoing = contract_rows(pick, result_half).astype(jnp.bfloat16)
    arrived = lax.all_to_all(
        outgoing.reshape(dp_count, slot_count * positions_here, half_width),
        "dp",
        split_axis=0,
        concat_axis=0,
        tiled=True,
    ).reshape(held_count, half_width)
    full_out = contract_rows(deal, arrived)
    full_out = jnp.where(unseen[:, None], mask_token.astype(jnp.float32)[None, :], full_out)
    full_out = full_out.astype(jnp.bfloat16).reshape(positions_here, strip_count, half_width)
    full_out = jnp.transpose(full_out, (1, 0, 2))[:, :, None, :]
    grad_rows = grad_out.astype(jnp.float32)
    bias_two_grad = jnp.sum(grad_rows, axis=0)
    grad_active = contract_last(grad_out, w_second)
    grad_hidden = gelu_back(grad_active)[0].astype(jnp.bfloat16)
    fc2_grad = contract_rows(active, grad_out)
    fc1_grad = contract_rows(normed_two, grad_hidden)
    hidden_bias_grad = jnp.sum(grad_hidden.astype(jnp.float32), axis=0)
    grad_normed_two = total_over_cores(contract_last(grad_hidden, w_first))
    grad_middle_part, gain_two_grad, shift_two_grad = norm_back_two(grad_normed_two)
    grad_middle = grad_rows + grad_middle_part
    grad_branch = grad_middle.astype(jnp.bfloat16)
    out_bias_grad = jnp.sum(grad_branch.astype(jnp.float32), axis=0)
    out_grad = contract_rows(attended, grad_branch)
    grad_attended = contract_last(grad_branch, w_output).astype(jnp.bfloat16)
    grad_queries, grad_keys, grad_values = lax.map(
        attend_pair_back,
        (
            by_pair(queries),
            by_pair(key_rows),
            by_pair(value_rows),
            pair_valid,
            log_total,
            by_pair(grad_attended),
        ),
    )
    grad_queries = grad_queries.reshape(row_count, half_width)
    grad_keys = grad_keys.reshape(row_count, half_width)
    grad_values = grad_values.reshape(row_count, half_width)
    grad_projected = jnp.stack([grad_queries, grad_keys, grad_values], axis=1).reshape(
        row_count, 3 * half_width
    )
    qkv_grad = contract_rows(normed, grad_projected)
    query_bias_grad = jnp.sum(grad_queries.astype(jnp.float32), axis=0)
    value_bias_grad = jnp.sum(grad_values.astype(jnp.float32), axis=0)
    grad_normed = total_over_cores(contract_last(grad_projected, w_attention))
    grad_inputs_part, gain_one_grad, shift_one_grad = norm_back_one(grad_normed)
    input_grad = (grad_middle + grad_inputs_part).reshape(slot_count, capacity, feature_width)
    def scattered(gradient):
        rows, width = gradient.shape
        chunks = gradient.astype(jnp.bfloat16).reshape(dp_count, rows // dp_count, width)
        return scatter_chunks(chunks, member_word, dp_count).reshape(1, -1)

    fc2_total = scattered(fc2_grad)
    fc1_total = scattered(fc1_grad)
    out_total = scattered(out_grad)
    qkv_total = scattered(qkv_grad)
    rep_grad = jnp.stack(
        [gain_one_grad, shift_one_grad, gain_two_grad, shift_two_grad, out_bias_grad, bias_two_grad]
    )
    split_grad = jnp.concatenate(
        [query_bias_grad[None], value_bias_grad[None], hidden_bias_grad.reshape(-1, half_width)],
        axis=0,
    )[None]
    packed = jnp.concatenate([mask_grad, rep_grad.reshape(-1), split_grad.reshape(-1)])
    packed = sum_over_dp(packed.reshape(-1, 128), dp_count).reshape(-1)
    mask_total = packed[:half_width]
    rep_total = packed[half_width : half_width + rep_grad.size].reshape(rep_grad.shape)
    split_total = packed[half_width + rep_grad.size :].reshape(split_grad.shape)
    qkv_new = adam_step(qkv_master, qkv_first, qkv_second, qkv_total, MATRIX_RATE, MATRIX_DECAY)
    out_new = adam_step(out_master, out_first, out_second, out_total, MATRIX_RATE, MATRIX_DECAY)
    fc1_new = adam_step(fc1_master, fc1_first, fc1_second, fc1_total, MATRIX_RATE, MATRIX_DECAY)
    fc2_new = adam_step(fc2_master, fc2_first, fc2_second, fc2_total, MATRIX_RATE, MATRIX_DECAY)
    rep_new = adam_step(rep_master, rep_first, rep_second, rep_total, VECTOR_RATE, 0.0)
    split_new = adam_step(split_master, split_first, split_second, split_total, VECTOR_RATE, 0.0)
    return (
        full_out,
        input_grad,
        mask_total,
        qkv_new[0],
        qkv_new[1],
        qkv_new[2],
        out_new[0],
        out_new[1],
        out_new[2],
        fc1_new[0],
        fc1_new[1],
        fc1_new[2],
        fc2_new[0],
        fc2_new[1],
        fc2_new[2],
        rep_new[0],
        rep_new[1],
        rep_new[2],
        split_new[0],
        split_new[1],
        split_new[2],
    )


def solution(mesh):
    placed = (
        P("dp", None, None),
        P(None, None, "dp", "mp"),
        P("mp"),
        P(),
        P(),
        P(),
        P("mp", "dp"),
        P("mp", "dp"),
        P("mp", "dp"),
        P("mp", "dp"),
        P("mp", "dp"),
        P("mp", "dp"),
        P("mp", "dp"),
        P("mp", "dp"),
        P("mp", "dp"),
        P("mp", "dp"),
        P("mp", "dp"),
        P("mp", "dp"),
        P(),
        P(),
        P(),
        P("mp", None, None),
        P("mp", None, None),
        P("mp", None, None),
    )
    return jax.shard_map(
        on_device,
        mesh=mesh,
        in_specs=placed,
        out_specs=(
            P(None, None, "dp", "mp"),
            P("dp", None, None),
            P("mp"),
            P("mp", "dp"),
            P("mp", "dp"),
            P("mp", "dp"),
            P("mp", "dp"),
            P("mp", "dp"),
            P("mp", "dp"),
            P("mp", "dp"),
            P("mp", "dp"),
            P("mp", "dp"),
            P("mp", "dp"),
            P("mp", "dp"),
            P("mp", "dp"),
            P(),
            P(),
            P(),
            P("mp", None, None),
            P("mp", None, None),
            P("mp", None, None),
        ),
        check_vma=False,
    )
```

```python
import jax
import jax.numpy as jnp
from jax import lax
from jax.experimental import pallas as pl
from jax.experimental.pallas import tpu as pltpu
from jax.sharding import PartitionSpec as P

HEAD = 64
PATCHES = 529
STEP = 10


NORM_EPS = 1e-06
BETA_ONE = 0.9
BETA_TWO = 0.999
ADAM_EPS = 1e-08
MATRIX_RATE = 0.15
MATRIX_DECAY = 0.05
VECTOR_RATE = 0.6


def layer_norm(signal, norm_gain, norm_shift):
    average = jnp.mean(signal, axis=-1, keepdims=True)
    centered = signal - average
    spread = jnp.mean(centered * centered, axis=-1, keepdims=True)
    return centered * lax.rsqrt(spread + NORM_EPS) * norm_gain + norm_shift


def exact_gelu(signal):
    return jax.nn.gelu(signal, approximate=False)


def product(left, right):
    return jnp.dot(left, right, preferred_element_type=jnp.float32)


def contract_last(left, right):
    return lax.dot_general(
        left, right, (((1,), (1,)), ((), ())), preferred_element_type=jnp.float32
    )


def contract_rows(left, right):
    return lax.dot_general(
        left, right, (((0,), (0,)), ((), ())), preferred_element_type=jnp.float32
    )


def adam_step(weight, moment_one, moment_two, gradient, step_rate, decay_rate):
    one_new = BETA_ONE * moment_one + (1.0 - BETA_ONE) * gradient
    two_new = BETA_TWO * moment_two + (1.0 - BETA_TWO) * gradient * gradient
    one_hat = one_new / (1.0 - BETA_ONE**STEP)
    two_hat = two_new / (1.0 - BETA_TWO**STEP)
    weight_new = weight - step_rate * (
        one_hat / (jnp.sqrt(two_hat) + ADAM_EPS) + decay_rate * weight
    )
    return (weight_new, one_new, two_new)


def total_over_cores(partial):
    return partial.astype(jnp.float32) + swap_cores(partial).astype(jnp.float32)


def pair_scores(queries, key_rows, valid_rows):
    scores = jnp.einsum(
        "qhd,khd->hqk", queries, key_rows, preferred_element_type=jnp.float32
    ) * HEAD ** (-0.5)
    return jnp.where(valid_rows[None, None, :], scores, -1e30)


def attend_pair(pair_block):
    queries, key_rows, value_rows, valid_rows = pair_block
    scores = pair_scores(queries, key_rows, valid_rows)
    row_max = jnp.max(scores, axis=2, keepdims=True)
    lifted = jnp.exp(scores - row_max)
    row_total = jnp.sum(lifted, axis=2, keepdims=True)
    probability = (lifted / row_total).astype(jnp.bfloat16)
    attended = jnp.einsum(
        "hqk,khd->qhd", probability, value_rows, preferred_element_type=jnp.float32
    )
    return (attended.astype(jnp.bfloat16), row_max[:, :, 0] + jnp.log(row_total[:, :, 0]))


def attend_pair_back(pair_block):
    queries, key_rows, value_rows, valid_rows, log_total, grad_attended = pair_block
    scores = pair_scores(queries, key_rows, valid_rows)
    probability = jnp.exp(scores - log_total[:, :, None])
    grad_prob = jnp.einsum(
        "qhd,khd->hqk", grad_attended, value_rows, preferred_element_type=jnp.float32
    )
    inner_sum = jnp.sum(probability * grad_prob, axis=2, keepdims=True)
    grad_scores = (probability * (grad_prob - inner_sum)).astype(jnp.bfloat16)
    score_scale = HEAD ** (-0.5)
    grad_queries = (
        jnp.einsum("hqk,khd->qhd", grad_scores, key_rows, preferred_element_type=jnp.float32)
        * score_scale
    )
    grad_keys = (
        jnp.einsum("hqk,qhd->khd", grad_scores, queries, preferred_element_type=jnp.float32)
        * score_scale
    )
    grad_values = jnp.einsum(
        "hqk,qhd->khd",
        probability.astype(jnp.bfloat16),
        grad_attended,
        preferred_element_type=jnp.float32,
    )
    return (
        grad_queries.astype(jnp.bfloat16),
        grad_keys.astype(jnp.bfloat16),
        grad_values.astype(jnp.bfloat16),
    )


def hop(array, distance, axis_count):
    return lax.ppermute(array, "dp", [(i, i ^ distance) for i in range(axis_count)])


def swap_cores(array):
    return lax.ppermute(array, "mp", [(0, 1), (1, 0)])


def place_chunks(pieces, chunk_ids, member, count):
    rows, width = pieces[0].shape[1:]

    def body(member_ref, *refs):
        sources, target, semaphores = refs[:-2], refs[-2], refs[-1]
        copies = []
        for source, ids in zip(sources, chunk_ids):
            for place, distance in enumerate(ids):
                copies.append(
                    pltpu.make_async_copy(
                        source.at[place],
                        target.at[member_ref[0] ^ distance],
                        semaphores.at[len(copies)],
                    )
                )
        for copy in copies:
            copy.start()
        for copy in copies:
            copy.wait()

    return pl.pallas_call(
        body,
        in_specs=[pl.BlockSpec(memory_space=pltpu.SMEM)]
        + [pl.BlockSpec(memory_space=pl.ANY)] * len(pieces),
        out_specs=pl.BlockSpec(memory_space=pltpu.VMEM),
        out_shape=jax.ShapeDtypeStruct((count, rows, width), pieces[0].dtype),
        scratch_shapes=[pltpu.SemaphoreType.DMA((count,))],
        cost_estimate=pl.CostEstimate(
            flops=0, transcendentals=0, bytes_accessed=4 * count * rows * width
        ),
        name="place_chunks",
    )(member, *pieces)


def pick_chunks(whole, chunk_ids, member):
    count, rows, width = whole.shape

    def body(member_ref, source, *refs):
        targets, semaphores = refs[:-1], refs[-1]
        copies = []
        for target, ids in zip(targets, chunk_ids):
            for place, distance in enumerate(ids):
                copies.append(
                    pltpu.make_async_copy(
                        source.at[member_ref[0] ^ distance],
                        target.at[place],
                        semaphores.at[len(copies)],
                    )
                )
        for copy in copies:
            copy.start()
        for copy in copies:
            copy.wait()

    return pl.pallas_call(
        body,
        in_specs=[pl.BlockSpec(memory_space=pltpu.SMEM), pl.BlockSpec(memory_space=pltpu.VMEM)],
        out_specs=[pl.BlockSpec(memory_space=pl.ANY)] * len(chunk_ids),
        out_shape=[
            jax.ShapeDtypeStruct((len(ids), rows, width), whole.dtype) for ids in chunk_ids
        ],
        scratch_shapes=[pltpu.SemaphoreType.DMA((count,))],
        cost_estimate=pl.CostEstimate(
            flops=0, transcendentals=0, bytes_accessed=4 * count * rows * width
        ),
        name="pick_chunks",
    )(member, whole)


def gather_chunks(chunk, member, count):
    own = chunk[None]
    if count == 16:
        near, far, last = (hop(own, k, count) for k in (4, 8, 12))
        first, second = jnp.concatenate([own, near]), jnp.concatenate([far, last])
        x_first, x_second = hop(first, 1, count), hop(second, 1, count)
        y_first, y_second = hop(first, 2, count), hop(second, 2, count)
        d_first, d_second = hop(y_first, 1, count), hop(x_second, 2, count)
        pieces = [first, second, x_first, x_second, y_first, y_second, d_first, d_second]
        ids = [(0, 4), (8, 12), (1, 5), (9, 13), (2, 6), (10, 14), (3, 7), (11, 15)]
    else:
        held, step = own, 1
        while step < count:
            held = jnp.concatenate([held, hop(held, step, count)])
            step *= 2
        pieces, ids = [held], [tuple(range(count))]
    return place_chunks(pieces, ids, member, count)


def scatter_chunks(whole, member, count):
    def wide(array):
        return array.astype(jnp.float32)

    if count == 16:
        ids = [(3, 7), (11, 15), (2, 6), (9, 13), (10, 14), (1, 5), (0, 4), (8, 12)]
        d_first, d_second, y_first, x_second, y_second, x_first, first, second = pick_chunks(
            whole, ids, member
        )
        d_first, d_second = hop(d_first, 1, count), hop(d_second, 2, count)
        y_second, x_first = hop(y_second, 2, count), hop(x_first, 1, count)
        y_first = hop((wide(y_first) + wide(d_first)).astype(jnp.bfloat16), 2, count)
        x_second = hop((wide(x_second) + wide(d_second)).astype(jnp.bfloat16), 1, count)
        first = wide(first) + wide(y_first) + wide(x_first)
        second = wide(second) + wide(y_second) + wide(x_second)
        near = hop(first[1].astype(jnp.bfloat16), 4, count)
        far = hop(second[0].astype(jnp.bfloat16), 8, count)
        last = hop(second[1].astype(jnp.bfloat16), 12, count)
        return first[0] + wide(near) + wide(far) + wide(last)
    (held,) = pick_chunks(whole, [tuple(range(count))], member)
    held = wide(held)
    step = count // 2
    while step:
        held = held[:step] + wide(hop(held[step:].astype(jnp.bfloat16), step, count))
        step //= 2
    return held[0]


def sum_over_dp(vector, count):
    if count == 16:
        for low, high in ((1, 2), (4, 8)):
            other, third, fourth = (hop(vector, k, count) for k in (low, high, low + high))
            vector = (vector + other) + (third + fourth)
        return vector
    step = 1
    while step < count:
        vector = vector + hop(vector, step, count)
        step *= 2
    return vector


def on_device_general(
    patch_rows,
    cotangent,
    mask_token,
    lengths,
    masked,
    dealing,
    qkv_master,
    qkv_first,
    qkv_second,
    out_master,
    out_first,
    out_second,
    fc1_master,
    fc1_first,
    fc1_second,
    fc2_master,
    fc2_first,
    fc2_second,
    rep_master,
    rep_first,
    rep_second,
    split_master,
    split_first,
    split_second,
):
    slot_count, capacity, feature_width = patch_rows.shape
    half_width = mask_token.shape[0]
    dp_count = lax.axis_size("dp")
    member = lax.axis_index("dp")
    core_index = lax.axis_index("mp")
    positions_here = cotangent.shape[1]
    position_span = positions_here * dp_count
    heads_here = half_width // HEAD
    hidden_width = (split_master.shape[1] - 2) * half_width
    row_count = slot_count * capacity
    pair_count = slot_count // 2
    pair_length = 2 * capacity
    patch_index = jnp.arange(PATCHES, dtype=jnp.int32)
    visible_all = (patch_index[None, :] < lengths[:, None]) & (masked == 0)
    strips_here = lax.dynamic_slice_in_dim(dealing, member * slot_count, slot_count)
    visible_here = visible_all[strips_here]
    rank_here = jnp.cumsum(visible_here.astype(jnp.int32), axis=1) - 1
    counts_here = jnp.sum(visible_here.astype(jnp.int32), axis=1)
    valid_rows = jnp.arange(capacity, dtype=jnp.int32)[None, :] < counts_here[:, None]
    padding = position_span - PATCHES
    visible_padded = jnp.pad(visible_here, ((0, 0), (0, padding)))
    rank_padded = jnp.pad(jnp.maximum(rank_here, 0), ((0, 0), (0, padding)))
    own_positions = jnp.arange(positions_here, dtype=jnp.int32) * dp_count + member
    inside = own_positions < PATCHES
    visible_own = visible_all[:, jnp.minimum(own_positions, PATCHES - 1)] & inside[None, :]
    strip_count = lengths.shape[0]
    held_count = strip_count * positions_here
    strip_row = (
        jnp.arange(positions_here, dtype=jnp.int32)[None, :] * strip_count + dealing[:, None]
    ).reshape(held_count)
    deal = (
        strip_row[:, None] == jnp.arange(held_count, dtype=jnp.int32)[None, :]
    ).astype(jnp.bfloat16)
    encoder_row = jnp.where(
        visible_padded,
        rank_padded + jnp.arange(slot_count, dtype=jnp.int32)[:, None] * capacity,
        -1,
    )
    encoder_row = jnp.transpose(
        encoder_row.reshape(slot_count, positions_here, dp_count), (2, 0, 1)
    ).reshape(held_count)
    pick = (
        jnp.arange(row_count, dtype=jnp.int32)[:, None] == encoder_row[None, :]
    ).astype(jnp.bfloat16)
    unseen = jnp.transpose(jnp.logical_not(visible_own) & inside[None, :]).reshape(held_count)
    member_word = member.astype(jnp.int32).reshape(1)

    cotangent_rows = jnp.transpose(cotangent.reshape(strip_count, positions_here, half_width), (1, 0, 2))
    cotangent_rows = cotangent_rows.reshape(held_count, half_width)
    dealt = product(deal, cotangent_rows).astype(jnp.bfloat16)
    returned = lax.all_to_all(
        dealt.reshape(dp_count, slot_count * positions_here, half_width),
        "dp",
        split_axis=0,
        concat_axis=0,
        tiled=True,
    ).reshape(held_count, half_width)
    gathered = product(pick, returned).astype(jnp.bfloat16)
    gathered_other = swap_cores(gathered)
    grad_out = jnp.where(
        core_index == 0,
        jnp.concatenate([gathered, gathered_other], axis=1),
        jnp.concatenate([gathered_other, gathered], axis=1),
    )
    mask_grad = product(unseen.astype(jnp.bfloat16)[None, :], cotangent_rows)[0]

    def gathered_matrix(master, rows, width):
        chunk = master.astype(jnp.bfloat16).reshape(rows // dp_count, width)
        return gather_chunks(chunk, member_word, dp_count).reshape(rows, width)

    w_attention = gathered_matrix(qkv_master, feature_width, 3 * half_width)
    w_output = gathered_matrix(out_master, half_width, feature_width)
    w_first = gathered_matrix(fc1_master, feature_width, hidden_width)
    w_second = gathered_matrix(fc2_master, hidden_width, feature_width)
    inputs = patch_rows.reshape(row_count, feature_width).astype(jnp.float32)
    normed_full, norm_back_one = jax.vjp(layer_norm, inputs, rep_master[0], rep_master[1])
    normed = normed_full.astype(jnp.bfloat16)
    projected = product(normed, w_attention).reshape(row_count, 3, half_width)
    queries = (projected[:, 0] + split_master[0, 0]).astype(jnp.bfloat16)
    key_rows = projected[:, 1].astype(jnp.bfloat16)
    value_rows = (projected[:, 2] + split_master[0, 1]).astype(jnp.bfloat16)

    def by_pair(array):
        return array.reshape(pair_count, pair_length, heads_here, HEAD)

    pair_valid = valid_rows.reshape(pair_count, pair_length)
    attended, log_total = lax.map(
        attend_pair, (by_pair(queries), by_pair(key_rows), by_pair(value_rows), pair_valid)
    )
    attended = attended.reshape(row_count, half_width)
    branch = total_over_cores(product(attended, w_output)) + rep_master[4]
    middle = inputs + branch
    normed_two_full, norm_back_two = jax.vjp(layer_norm, middle, rep_master[2], rep_master[3])
    normed_two = normed_two_full.astype(jnp.bfloat16)
    hidden = product(normed_two, w_first) + split_master[0, 2:].reshape(hidden_width)
    active_full, gelu_back = jax.vjp(exact_gelu, hidden)
    active = active_full.astype(jnp.bfloat16)
    second = total_over_cores(product(active, w_second).astype(jnp.bfloat16)) + rep_master[5]
    result = (middle + second).astype(jnp.bfloat16)
    result_half = lax.dynamic_slice_in_dim(result, core_index * half_width, half_width, 1)
    outgoing = contract_rows(pick, result_half).astype(jnp.bfloat16)
    arrived = lax.all_to_all(
        outgoing.reshape(dp_count, slot_count * positions_here, half_width),
        "dp",
        split_axis=0,
        concat_axis=0,
        tiled=True,
    ).reshape(held_count, half_width)
    full_out = contract_rows(deal, arrived)
    full_out = jnp.where(unseen[:, None], mask_token.astype(jnp.float32)[None, :], full_out)
    full_out = full_out.astype(jnp.bfloat16).reshape(positions_here, strip_count, half_width)
    full_out = jnp.transpose(full_out, (1, 0, 2))[:, :, None, :]
    grad_rows = grad_out.astype(jnp.float32)
    bias_two_grad = jnp.sum(grad_rows, axis=0)
    grad_active = contract_last(grad_out, w_second)
    grad_hidden = gelu_back(grad_active)[0].astype(jnp.bfloat16)
    fc2_grad = contract_rows(active, grad_out)
    fc1_grad = contract_rows(normed_two, grad_hidden)
    hidden_bias_grad = jnp.sum(grad_hidden.astype(jnp.float32), axis=0)
    grad_normed_two = total_over_cores(contract_last(grad_hidden, w_first))
    grad_middle_part, gain_two_grad, shift_two_grad = norm_back_two(grad_normed_two)
    grad_middle = grad_rows + grad_middle_part
    grad_branch = grad_middle.astype(jnp.bfloat16)
    out_bias_grad = jnp.sum(grad_branch.astype(jnp.float32), axis=0)
    out_grad = contract_rows(attended, grad_branch)
    grad_attended = contract_last(grad_branch, w_output).astype(jnp.bfloat16)
    grad_queries, grad_keys, grad_values = lax.map(
        attend_pair_back,
        (
            by_pair(queries),
            by_pair(key_rows),
            by_pair(value_rows),
            pair_valid,
            log_total,
            by_pair(grad_attended),
        ),
    )
    grad_queries = grad_queries.reshape(row_count, half_width)
    grad_keys = grad_keys.reshape(row_count, half_width)
    grad_values = grad_values.reshape(row_count, half_width)
    grad_projected = jnp.stack([grad_queries, grad_keys, grad_values], axis=1).reshape(
        row_count, 3 * half_width
    )
    qkv_grad = contract_rows(normed, grad_projected)
    query_bias_grad = jnp.sum(grad_queries.astype(jnp.float32), axis=0)
    value_bias_grad = jnp.sum(grad_values.astype(jnp.float32), axis=0)
    grad_normed = total_over_cores(contract_last(grad_projected, w_attention))
    grad_inputs_part, gain_one_grad, shift_one_grad = norm_back_one(grad_normed)
    input_grad = (grad_middle + grad_inputs_part).reshape(slot_count, capacity, feature_width)
    def scattered(gradient):
        rows, width = gradient.shape
        chunks = gradient.astype(jnp.bfloat16).reshape(dp_count, rows // dp_count, width)
        return scatter_chunks(chunks, member_word, dp_count).reshape(1, -1)

    fc2_total = scattered(fc2_grad)
    fc1_total = scattered(fc1_grad)
    out_total = scattered(out_grad)
    qkv_total = scattered(qkv_grad)
    rep_grad = jnp.stack(
        [gain_one_grad, shift_one_grad, gain_two_grad, shift_two_grad, out_bias_grad, bias_two_grad]
    )
    split_grad = jnp.concatenate(
        [query_bias_grad[None], value_bias_grad[None], hidden_bias_grad.reshape(-1, half_width)],
        axis=0,
    )[None]
    packed = jnp.concatenate([mask_grad, rep_grad.reshape(-1), split_grad.reshape(-1)])
    packed = sum_over_dp(packed.reshape(-1, 128), dp_count).reshape(-1)
    mask_total = packed[:half_width]
    rep_total = packed[half_width : half_width + rep_grad.size].reshape(rep_grad.shape)
    split_total = packed[half_width + rep_grad.size :].reshape(split_grad.shape)
    qkv_new = adam_step(qkv_master, qkv_first, qkv_second, qkv_total, MATRIX_RATE, MATRIX_DECAY)
    out_new = adam_step(out_master, out_first, out_second, out_total, MATRIX_RATE, MATRIX_DECAY)
    fc1_new = adam_step(fc1_master, fc1_first, fc1_second, fc1_total, MATRIX_RATE, MATRIX_DECAY)
    fc2_new = adam_step(fc2_master, fc2_first, fc2_second, fc2_total, MATRIX_RATE, MATRIX_DECAY)
    rep_new = adam_step(rep_master, rep_first, rep_second, rep_total, VECTOR_RATE, 0.0)
    split_new = adam_step(split_master, split_first, split_second, split_total, VECTOR_RATE, 0.0)
    return (
        full_out,
        input_grad,
        mask_total,
        qkv_new[0],
        qkv_new[1],
        qkv_new[2],
        out_new[0],
        out_new[1],
        out_new[2],
        fc1_new[0],
        fc1_new[1],
        fc1_new[2],
        fc2_new[0],
        fc2_new[1],
        fc2_new[2],
        rep_new[0],
        rep_new[1],
        rep_new[2],
        split_new[0],
        split_new[1],
        split_new[2],
    )


BLOCK = 256
UNIT_ROWS = 48
UNIT_WIDTH = 1536
Z_ORDER = (0, 12, 4, 8)
VMEM_BYTES = 60 * 1024 * 1024
ANY = pl.BlockSpec(memory_space=pl.ANY)
IN_VMEM = pl.BlockSpec(memory_space=pltpu.VMEM)
IN_SMEM = pl.BlockSpec(memory_space=pltpu.SMEM)


def shaped(shape, dtype):
    return jax.ShapeDtypeStruct(shape, dtype)


def params(grid_axes=0):
    semantics = ("arbitrary",) * grid_axes if grid_axes else None
    return pltpu.CompilerParams(dimension_semantics=semantics, vmem_limit_bytes=VMEM_BYTES)


def cost(microseconds):
    return pl.CostEstimate(
        flops=int(microseconds * 1.15e9), transcendentals=0, bytes_accessed=1000000
    )


def together(*values):
    return lax.optimization_barrier(values)


def hop_by_core(array, first_core, second_core, count):
    pairs = []
    for i in range(count):
        pairs.append((2 * i, 2 * (i ^ first_core)))
        pairs.append((2 * i + 1, 2 * (i ^ second_core) + 1))
    return lax.ppermute(array, ("dp", "mp"), pairs)


def pack_units(qkv, out, fc1, fc2):
    def body(qkv_ref, out_ref, fc1_ref, fc2_ref, unit_a, unit_b, unit_c):
        def put(unit, column, rows):
            unit[0, :, column * 128 : (column + 1) * 128] = rows.astype(jnp.bfloat16)

        for j in range(9):
            put(unit_a, j, qkv_ref[pl.ds(j, UNIT_ROWS, stride=9), :])
        for j in range(3):
            put(unit_a, 9 + j, out_ref[pl.ds(j, UNIT_ROWS, stride=3), :])
        for j in range(12):
            put(unit_b, j, fc1_ref[pl.ds(j, UNIT_ROWS, stride=12), :])
        for half in range(2):
            for j in range(6):
                start = half * UNIT_ROWS * 6 + j
                put(unit_c, half * 6 + j, fc2_ref[pl.ds(start, UNIT_ROWS, stride=6), :])

    unit = shaped((1, UNIT_ROWS, UNIT_WIDTH), jnp.bfloat16)
    return pl.pallas_call(
        body,
        out_shape=[unit, unit, unit],
        compiler_params=params(),
        cost_estimate=cost(2),
        name="pack_units",
    )(
        *(array.reshape(-1, 128) for array in (qkv, out, fc1, fc2))
    )


def gather_columns(unit, count):
    far = hop(unit, 12, count)
    pair = jnp.concatenate([unit, far])
    return far, jnp.concatenate([pair, hop(pair, 4, count)])


def gather_sides(column, count):
    return hop_by_core(column, 1, 2, count), hop_by_core(column, 2, 1, count)


def owner_of(words, piece, entry):
    extra = (0, words[1], words[2], 3)[piece]
    return words[0] ^ Z_ORDER[entry] ^ extra


def added(start, stop, *arrays):
    total = arrays[0][start:stop].astype(jnp.float32)
    for array in arrays[1:]:
        total = total + array[start:stop].astype(jnp.float32)
    return total.astype(jnp.bfloat16)


def unit_shapes():
    size = (8, UNIT_ROWS, UNIT_WIDTH)
    return [shaped(size, jnp.bfloat16), shaped(size, jnp.bfloat16)]


def unit_targets(words, sent, kept):
    places = []
    for entry, distance in enumerate(Z_ORDER):
        own = words[0] ^ distance
        places.append((sent.at[4 + entry], own ^ 3))
        places.append((sent.at[entry], own ^ words[2]))
        places.append((kept.at[entry], own))
        places.append((kept.at[4 + entry], own ^ words[1]))
    return places


def norm_parts(signal):
    average = jnp.mean(signal, axis=1, keepdims=True)
    centered = signal - average
    scale = lax.rsqrt(jnp.mean(centered * centered, axis=1, keepdims=True) + NORM_EPS)
    return centered * scale, scale


def norm_back(grad, unit_signal, scale, gain):
    scaled = grad * gain
    mean_one = jnp.mean(scaled, axis=1, keepdims=True)
    mean_two = jnp.mean(scaled * unit_signal, axis=1, keepdims=True)
    return scale * (scaled - mean_one - unit_signal * mean_two)


def first_norm(rows, rep):
    count, width = rows.shape

    def body(rows_ref, rep_ref, normed_ref):
        unit_signal, _ = norm_parts(rows_ref[...].astype(jnp.float32))
        normed = unit_signal * rep_ref[0:1, :] + rep_ref[1:2, :]
        normed_ref[...] = normed.astype(jnp.bfloat16)

    return pl.pallas_call(
        body,
        grid=(count // BLOCK,),
        in_specs=[
            pl.BlockSpec((BLOCK, width), lambda i: (i, 0)),
            pl.BlockSpec(rep.shape, lambda i: (0, 0)),
        ],
        out_specs=pl.BlockSpec((BLOCK, width), lambda i: (i, 0)),
        out_shape=shaped((count, width), jnp.bfloat16),
        compiler_params=params(1),
        cost_estimate=cost(3.5),
        name="first_norm",
    )(rows, rep)


def fixed(*shape):
    return pl.BlockSpec(shape, lambda i: (0,) * len(shape))


def run_copies(pairs, semaphores):
    copies = [
        pltpu.make_async_copy(source, target, semaphores.at[i])
        for i, (source, target) in enumerate(pairs)
    ]
    for copy in copies:
        copy.start()
    for copy in copies:
        copy.wait()


def head_lanes(head):
    lane = pl.multiple_of((head // 2) * (2 * HEAD), 2 * HEAD)
    chosen = (lax.broadcasted_iota(jnp.int32, (1, 2 * HEAD), 1) // HEAD) == head % 2
    return lane, chosen


def attend_head(head, first_head, qkv_ref, bias_ref, prob_ref, attended_ref):
    count = qkv_ref.shape[0]
    half = qkv_ref.shape[1] // 3
    lane, chosen = head_lanes(head)
    keys = qkv_ref[:, pl.ds(half + lane, 2 * HEAD)]
    values = qkv_ref[:, pl.ds(2 * half + lane, 2 * HEAD)]
    target = pl.ds(pl.multiple_of(lane - first_head * HEAD, 2 * HEAD), 2 * HEAD)

    @pl.loop(0, count // BLOCK)
    def _(block):
        rows = pl.ds(block * BLOCK, BLOCK)
        queries = qkv_ref[rows, pl.ds(lane, 2 * HEAD)]
        queries = jnp.where(chosen, queries, jnp.zeros_like(queries))
        scores = contract_last(queries, keys) * HEAD ** (-0.5) + bias_ref[...]
        lifted = jnp.exp(scores - jnp.max(scores, axis=1, keepdims=True))
        total = jnp.sum(lifted, axis=1, keepdims=True)
        probability = (lifted * (1.0 / total)).astype(jnp.bfloat16)
        prob_ref[0, rows, :] = probability
        attended = product(probability, values).astype(jnp.bfloat16)
        held = attended_ref[rows, target]
        attended_ref[rows, target] = jnp.where(chosen, attended, held)


def attention_first(words, normed, split, column_bias, pieces, heads):
    count, width = normed.shape
    half = split.shape[1]

    def body(
        words_ref, normed_ref, split_ref, bias_ref, p0, p1, p2, p3,
        qkv_ref, prob_ref, attended_ref, weights_ref, w_out_ref, spread, semaphores,
    ):
        head = pl.program_id(0)

        @pl.when(head == 0)
        def _():
            pairs = []
            for piece, source in enumerate((p0, p1, p2, p3)):
                for entry in range(4):
                    row = pl.multiple_of(owner_of(words_ref, piece, entry) * UNIT_ROWS, 16)
                    pairs.append((source.at[entry], weights_ref.at[pl.ds(row, UNIT_ROWS), :]))
            run_copies(pairs, semaphores)

            @pl.loop(0, count // BLOCK)
            def _(block):
                rows = pl.ds(block * BLOCK, BLOCK)
                projected = product(normed_ref[rows, :], weights_ref[:, : 3 * half])
                queries = projected[:, :half] + split_ref[0:1, :]
                values = projected[:, 2 * half :] + split_ref[1:2, :]
                qkv_ref[rows, 0:half] = queries.astype(jnp.bfloat16)
                qkv_ref[rows, half : 2 * half] = projected[:, half : 2 * half].astype(jnp.bfloat16)
                qkv_ref[rows, 2 * half :] = values.astype(jnp.bfloat16)

            for strip in range(half // 128):
                start = 3 * half + strip * 128
                spread[strip] = weights_ref[:, start : start + 128].astype(jnp.float32)
                for side in range(2):
                    start = side * half + strip * 128
                    w_out_ref[:, start : start + 128] = spread[
                        strip, pl.ds(side, half, stride=2), :
                    ].astype(jnp.bfloat16)

        attend_head(head, 0, qkv_ref, bias_ref, prob_ref, attended_ref)

    return pl.pallas_call(
        body,
        grid=(heads,),
        in_specs=[IN_SMEM, fixed(count, width), fixed(6, half), fixed(1, count)] + [ANY] * 4,
        out_specs=[
            fixed(count, 3 * half),
            pl.BlockSpec((1, count, count), lambda h: (h, 0, 0)),
            fixed(count, heads * HEAD),
            fixed(width, UNIT_WIDTH),
            fixed(half, width),
        ],
        out_shape=[
            shaped((count, 3 * half), jnp.bfloat16),
            shaped((heads, count, count), jnp.bfloat16),
            shaped((count, heads * HEAD), jnp.bfloat16),
            shaped((width, UNIT_WIDTH), jnp.bfloat16),
            shaped((half, width), jnp.bfloat16),
        ],
        scratch_shapes=[
            pltpu.VMEM((half // 128, width, 128), jnp.float32),
            pltpu.SemaphoreType.DMA((16,)),
        ],
        compiler_params=params(1),
        cost_estimate=cost(11),
        name="attention_first",
    )(words, normed, split, column_bias, *pieces)


def attention_rest(qkv, column_bias, attended, w_out, first_head):
    count, span = qkv.shape
    half = span // 3
    width = w_out.shape[1]
    heads = half // HEAD - first_head

    def body(qkv_ref, bias_ref, before_ref, w_out_ref, prob_ref, attended_ref, partial_ref):
        attend_head(
            pl.program_id(0) + first_head, first_head, qkv_ref, bias_ref, prob_ref, attended_ref
        )

        @pl.when(pl.program_id(0) == heads - 1)
        def _():
            @pl.loop(0, count // BLOCK)
            def _(block):
                rows = pl.ds(block * BLOCK, BLOCK)
                both = jnp.concatenate([before_ref[rows, :], attended_ref[rows, :]], axis=1)
                partial_ref[rows, :] = product(both, w_out_ref[...]).astype(jnp.bfloat16)

    return pl.pallas_call(
        body,
        grid=(heads,),
        in_specs=[
            fixed(count, span), fixed(1, count), fixed(count, first_head * HEAD),
            fixed(half, width),
        ],
        out_specs=[
            pl.BlockSpec((1, count, count), lambda h: (h, 0, 0)),
            fixed(count, heads * HEAD),
            fixed(count, width),
        ],
        out_shape=[
            shaped((heads, count, count), jnp.bfloat16),
            shaped((count, heads * HEAD), jnp.bfloat16),
            shaped((count, width), jnp.bfloat16),
        ],
        compiler_params=params(1),
        cost_estimate=cost(14),
        name="attention_rest",
    )(qkv, column_bias, attended, w_out)


def row_block(size):
    return pl.BlockSpec((BLOCK, size), lambda i: (i, 0))


def mlp_forward(words, rows_in, own, other, rep, split, pieces):
    count, width = rows_in.shape
    half = split.shape[1]

    def body(
        words_ref, in_ref, own_ref, other_ref, rep_ref, split_ref, b0, b1, b2, b3,
        middle_ref, normed_ref, active_ref, slope_ref, w_first, semaphores,
    ):
        @pl.when(pl.program_id(0) == 0)
        def _():
            pairs = []
            for piece, source in enumerate((b0, b1, b2, b3)):
                for entry in range(4):
                    row = pl.multiple_of(owner_of(words_ref, piece, entry) * UNIT_ROWS, 16)
                    pairs.append((source.at[entry], w_first.at[pl.ds(row, UNIT_ROWS), :]))
            run_copies(pairs, semaphores)

        branch = own_ref[...].astype(jnp.float32) + other_ref[...].astype(jnp.float32)
        middle = in_ref[...].astype(jnp.float32) + branch + rep_ref[4:5, :]
        middle_ref[...] = middle
        unit_signal, _ = norm_parts(middle)
        normed = (unit_signal * rep_ref[2:3, :] + rep_ref[3:4, :]).astype(jnp.bfloat16)
        normed_ref[...] = normed
        for part in range(UNIT_WIDTH // half):
            columns = slice(part * half, (part + 1) * half)
            hidden = product(normed, w_first[:, columns]) + split_ref[2 + part : 3 + part, :]
            spread = 0.5 + 0.5 * lax.erf(hidden * 0.7071067811865476)
            active_ref[:, columns] = (hidden * spread).astype(jnp.bfloat16)
            slope = spread + hidden * jnp.exp(-0.5 * hidden * hidden) * 0.3989422804014327
            slope_ref[:, columns] = slope.astype(jnp.bfloat16)

    return pl.pallas_call(
        body,
        grid=(count // BLOCK,),
        in_specs=[IN_SMEM, row_block(width), row_block(width), row_block(width)]
        + [fixed(6, width), fixed(6, half)]
        + [ANY] * 4,
        out_specs=[
            row_block(width), row_block(width), row_block(UNIT_WIDTH), row_block(UNIT_WIDTH),
            fixed(width, UNIT_WIDTH),
        ],
        out_shape=[
            shaped((count, width), jnp.float32),
            shaped((count, width), jnp.bfloat16),
            shaped((count, UNIT_WIDTH), jnp.bfloat16),
            shaped((count, UNIT_WIDTH), jnp.bfloat16),
            shaped((width, UNIT_WIDTH), jnp.bfloat16),
        ],
        scratch_shapes=[pltpu.SemaphoreType.DMA((16,))],
        compiler_params=params(1),
        cost_estimate=cost(9),
        name="mlp_forward",
    )(words, rows_in, own, other, rep, split, *pieces)


def mlp_back(words, active, slope, grad_out, w_first, pieces):
    count, width = grad_out.shape
    hidden_width = UNIT_WIDTH

    def body(
        words_ref, active_ref, slope_ref, grad_ref, w_first_ref, c0, c1, c2, c3,
        grad_hidden_ref, back_ref, second_ref, hidden_sum_ref, grad_sum_ref, w_second, semaphores,
    ):
        @pl.when(pl.program_id(0) == 0)
        def _():
            pairs = []
            for piece, source in enumerate((c0, c1, c2, c3)):
                for entry in range(4):
                    owner = owner_of(words_ref, piece, entry)
                    for side in range(2):
                        row = pl.multiple_of((owner * 2 + side) * UNIT_ROWS, 16)
                        pairs.append(
                            (
                                source.at[entry, :, pl.ds(side * width, width)],
                                w_second.at[pl.ds(row, UNIT_ROWS), :],
                            )
                        )
            run_copies(pairs, semaphores)
            hidden_sum_ref[...] = jnp.zeros_like(hidden_sum_ref)
            grad_sum_ref[...] = jnp.zeros_like(grad_sum_ref)

        grad = grad_ref[...]
        grad_sum_ref[...] += jnp.sum(grad.astype(jnp.float32), axis=0, keepdims=True)
        for part in range(hidden_width // BLOCK):
            columns = slice(part * BLOCK, (part + 1) * BLOCK)
            grad_active = contract_last(grad, w_second[columns, :])
            grad_hidden = (grad_active * slope_ref[:, columns].astype(jnp.float32)).astype(
                jnp.bfloat16
            )
            grad_hidden_ref[:, columns] = grad_hidden
            hidden_sum_ref[:, columns] += jnp.sum(
                grad_hidden.astype(jnp.float32), axis=0, keepdims=True
            )
        back_ref[...] = contract_last(grad_hidden_ref[...], w_first_ref[...]).astype(jnp.bfloat16)
        second_ref[...] = product(active_ref[...], w_second[...]).astype(jnp.bfloat16)

    return pl.pallas_call(
        body,
        grid=(count // BLOCK,),
        in_specs=[IN_SMEM, row_block(hidden_width), row_block(hidden_width), row_block(width)]
        + [fixed(width, hidden_width)]
        + [ANY] * 4,
        out_specs=[
            row_block(hidden_width), row_block(width), row_block(width),
            fixed(1, hidden_width), fixed(1, width),
        ],
        out_shape=[
            shaped((count, hidden_width), jnp.bfloat16),
            shaped((count, width), jnp.bfloat16),
            shaped((count, width), jnp.bfloat16),
            shaped((1, hidden_width), jnp.float32),
            shaped((1, width), jnp.float32),
        ],
        scratch_shapes=[
            pltpu.VMEM((hidden_width, width), jnp.bfloat16),
            pltpu.SemaphoreType.DMA((32,)),
        ],
        compiler_params=params(1),
        cost_estimate=cost(9),
        name="mlp_back",
    )(words, active, slope, grad_out, w_first, *pieces)


def second_gradient(words, active, grad_out):
    count, hidden_width = active.shape
    width = grad_out.shape[1]

    def body(words_ref, active_ref, grad_ref, sent, kept, whole, semaphores):
        @pl.loop(0, hidden_width // BLOCK)
        def _(block):
            columns = pl.ds(pl.multiple_of(block * BLOCK, BLOCK), BLOCK)
            whole[columns, :] = contract_rows(active_ref[:, columns], grad_ref[...]).astype(
                jnp.bfloat16
            )

        copies = []
        for target, owner in unit_targets(words_ref, sent, kept):
            for part in range(2):
                row = pl.multiple_of(owner * 2 * UNIT_ROWS + part * UNIT_ROWS, 16)
                copies.append(
                    pltpu.make_async_copy(
                        whole.at[pl.ds(row, UNIT_ROWS), :],
                        target.at[:, pl.ds(part * width, width)],
                        semaphores.at[len(copies)],
                    )
                )
        for copy in copies:
            copy.start()
        for copy in copies:
            copy.wait()

    return pl.pallas_call(
        body,
        in_specs=[IN_SMEM, IN_VMEM, IN_VMEM],
        out_specs=[ANY] * 2,
        out_shape=unit_shapes(),
        scratch_shapes=[
            pltpu.VMEM((hidden_width, width), jnp.bfloat16),
            pltpu.SemaphoreType.DMA((32,)),
        ],
        compiler_params=params(),
        cost_estimate=cost(6.8),
        name="second_gradient",
    )(words, active, grad_out)


def send_rows(words_ref, whole, sent, kept, semaphores):
    copies = []
    for target, owner in unit_targets(words_ref, sent, kept):
        row = pl.multiple_of(owner * UNIT_ROWS, 16)
        copies.append(
            pltpu.make_async_copy(
                whole.at[pl.ds(row, UNIT_ROWS), :], target, semaphores.at[len(copies)]
            )
        )
    for copy in copies:
        copy.start()
    for copy in copies:
        copy.wait()


def first_gradient(words, normed, grad_hidden):
    count, width = normed.shape
    hidden_width = grad_hidden.shape[1]

    def body(words_ref, normed_ref, grad_ref, sent, kept, whole, semaphores):
        @pl.loop(0, width // BLOCK)
        def _(block):
            columns = pl.ds(pl.multiple_of(block * BLOCK, BLOCK), BLOCK)
            whole[columns, :] = contract_rows(normed_ref[:, columns], grad_ref[...]).astype(
                jnp.bfloat16
            )

        send_rows(words_ref, whole, sent, kept, semaphores)

    return pl.pallas_call(
        body,
        in_specs=[IN_SMEM, IN_VMEM, IN_VMEM],
        out_specs=[ANY] * 2,
        out_shape=unit_shapes(),
        scratch_shapes=[
            pltpu.VMEM((width, hidden_width), jnp.bfloat16),
            pltpu.SemaphoreType.DMA((16,)),
        ],
        compiler_params=params(),
        cost_estimate=cost(6.3),
        name="first_gradient",
    )(words, normed, grad_hidden)


def attend_head_back(
    head, first_head, qkv_ref, prob_ref, grad_attended, grad_qkv_ref, key_total, value_total
):
    count = qkv_ref.shape[0]
    half = qkv_ref.shape[1] // 3
    own_half = grad_qkv_ref.shape[1] // 3
    lane, chosen = head_lanes(head)
    keys = qkv_ref[:, pl.ds(half + lane, 2 * HEAD)]
    values = qkv_ref[:, pl.ds(2 * half + lane, 2 * HEAD)]
    key_total[...] = jnp.zeros_like(key_total)
    value_total[...] = jnp.zeros_like(value_total)

    def merge(part, rows, total):
        start = pl.multiple_of(part * own_half + lane - first_head * HEAD, 2 * HEAD)
        columns = pl.ds(start, 2 * HEAD)
        held = grad_qkv_ref[rows, columns]
        grad_qkv_ref[rows, columns] = jnp.where(chosen, total.astype(jnp.bfloat16), held)

    @pl.loop(0, count // BLOCK)
    def _(block):
        rows = pl.ds(block * BLOCK, BLOCK)
        grad = grad_attended[rows, pl.ds(lane, 2 * HEAD)]
        grad = jnp.where(chosen, grad, jnp.zeros_like(grad))
        low_probability = prob_ref[0, rows, :]
        probability = low_probability.astype(jnp.float32)
        weighted = probability * contract_last(grad, values)
        inner = jnp.sum(weighted, axis=1, keepdims=True)
        grad_scores = (weighted - probability * inner).astype(jnp.bfloat16)
        merge(0, rows, product(grad_scores, keys) * HEAD ** (-0.5))
        key_total[...] += contract_rows(grad_scores, qkv_ref[rows, pl.ds(lane, 2 * HEAD)])
        value_total[...] += contract_rows(low_probability, grad)

    everything = pl.ds(0, count)
    merge(1, everything, key_total[...] * HEAD ** (-0.5))
    merge(2, everything, value_total[...])


def attention_back_first(
    middle, own, other, grad_out, rep, w_out, qkv, prob, attended, attended_rest
):
    count, width = middle.shape
    half = qkv.shape[1] // 3
    heads = prob.shape[0]

    def body(
        middle_ref, own_ref, other_ref, grad_ref, rep_ref, w_out_ref, qkv_ref, prob_ref,
        attended_ref, rest_ref,
        grad_middle_ref, grad_attended, grad_qkv_ref, out_rows, width_sums,
        branch, spread, key_total, value_total,
    ):
        head = pl.program_id(0)

        @pl.when(head == 0)
        def _():
            width_sums[...] = jnp.zeros_like(width_sums)

            @pl.loop(0, count // BLOCK)
            def _(block):
                rows = pl.ds(block * BLOCK, BLOCK)
                unit_signal, scale = norm_parts(middle_ref[rows, :])
                mine = own_ref[rows, :].astype(jnp.float32)
                grad_normed = mine + other_ref[rows, :].astype(jnp.float32)
                grad_middle = grad_ref[rows, :].astype(jnp.float32) + norm_back(
                    grad_normed, unit_signal, scale, rep_ref[2:3, :]
                )
                grad_middle_ref[rows, :] = grad_middle
                grad_branch = grad_middle.astype(jnp.bfloat16)
                branch[rows, :] = grad_branch
                width_sums[0:1, :] += jnp.sum(mine * unit_signal, axis=0, keepdims=True)
                width_sums[1:2, :] += jnp.sum(mine, axis=0, keepdims=True)
                width_sums[2:3, :] += 0.5 * jnp.sum(
                    grad_branch.astype(jnp.float32), axis=0, keepdims=True
                )
                grad_attended[rows, :] = contract_last(grad_branch, w_out_ref[...]).astype(
                    jnp.bfloat16
                )

            both = jnp.concatenate([attended_ref[...], rest_ref[...]], axis=1)
            out_gradient = contract_rows(both, branch[...])
            for strip in range(half // 128):
                for side in range(2):
                    start = side * half + strip * 128
                    spread[strip, pl.ds(side, half, stride=2), :] = out_gradient[
                        :, start : start + 128
                    ]
                start = strip * 128
                out_rows[:, start : start + 128] = spread[strip].astype(jnp.bfloat16)

        attend_head_back(
            head, 0, qkv_ref, prob_ref, grad_attended, grad_qkv_ref, key_total, value_total
        )

    return pl.pallas_call(
        body,
        grid=(heads,),
        in_specs=[
            fixed(count, width), fixed(count, width), fixed(count, width), fixed(count, width),
            fixed(6, width), fixed(half, width), fixed(count, 3 * half),
            pl.BlockSpec((1, count, count), lambda h: (h, 0, 0)),
            fixed(count, attended.shape[1]), fixed(count, attended_rest.shape[1]),
        ],
        out_specs=[
            fixed(count, width), fixed(count, half), fixed(count, 3 * heads * HEAD),
            fixed(width, half), fixed(3, width),
        ],
        out_shape=[
            shaped((count, width), jnp.float32),
            shaped((count, half), jnp.bfloat16),
            shaped((count, 3 * heads * HEAD), jnp.bfloat16),
            shaped((width, half), jnp.bfloat16),
            shaped((3, width), jnp.float32),
        ],
        scratch_shapes=[
            pltpu.VMEM((count, width), jnp.bfloat16),
            pltpu.VMEM((half // 128, width, 128), jnp.float32),
            pltpu.VMEM((count, 2 * HEAD), jnp.float32),
            pltpu.VMEM((count, 2 * HEAD), jnp.float32),
        ],
        compiler_params=params(1),
        cost_estimate=cost(14),
        name="attention_back_first",
    )(middle, own, other, grad_out, rep, w_out, qkv, prob, attended, attended_rest)


def attention_back_rest(words, grad_attended, qkv, prob, normed, grad_first, out_rows):
    count, width = normed.shape
    half = qkv.shape[1] // 3
    heads = prob.shape[0]
    first = half - heads * HEAD

    def body(
        words_ref, grad_attended_ref, qkv_ref, prob_ref, normed_ref, first_ref, out_ref,
        grad_qkv_ref, half_sums, sent, kept, grad_rest, whole, key_total, value_total, semaphores,
    ):
        head = pl.program_id(0)
        attend_head_back(
            head + first // HEAD, first // HEAD, qkv_ref, prob_ref, grad_attended_ref, grad_rest,
            key_total, value_total,
        )

        @pl.when(head == heads - 1)
        def _():
            for part in range(3):
                start = part * half
                grad_qkv_ref[:, start : start + first] = first_ref[
                    :, part * first : (part + 1) * first
                ]
                grad_qkv_ref[:, start + first : start + half] = grad_rest[
                    :, part * heads * HEAD : (part + 1) * heads * HEAD
                ]
            whole[:, 3 * half :] = out_ref[...]

            @pl.loop(0, width // BLOCK)
            def _(block):
                columns = pl.ds(pl.multiple_of(block * BLOCK, BLOCK), BLOCK)
                whole[columns, : 3 * half] = contract_rows(
                    normed_ref[:, columns], grad_qkv_ref[...]
                ).astype(jnp.bfloat16)

            send_rows(words_ref, whole, sent, kept, semaphores)
            half_sums[0:1, :] = jnp.sum(
                grad_qkv_ref[:, :half].astype(jnp.float32), axis=0, keepdims=True
            )
            half_sums[1:2, :] = jnp.sum(
                grad_qkv_ref[:, 2 * half :].astype(jnp.float32), axis=0, keepdims=True
            )

    return pl.pallas_call(
        body,
        grid=(heads,),
        in_specs=[
            IN_SMEM, fixed(count, half), fixed(count, 3 * half),
            pl.BlockSpec((1, count, count), lambda h: (h, 0, 0)),
            fixed(count, width), fixed(count, 3 * first), fixed(width, half),
        ],
        out_specs=[fixed(count, 3 * half), fixed(2, half), ANY, ANY],
        out_shape=[
            shaped((count, 3 * half), jnp.bfloat16),
            shaped((2, half), jnp.float32),
        ]
        + unit_shapes(),
        scratch_shapes=[
            pltpu.VMEM((count, 3 * heads * HEAD), jnp.bfloat16),
            pltpu.VMEM((width, UNIT_WIDTH), jnp.bfloat16),
            pltpu.VMEM((count, 2 * HEAD), jnp.float32),
            pltpu.VMEM((count, 2 * HEAD), jnp.float32),
            pltpu.SemaphoreType.DMA((16,)),
        ],
        compiler_params=params(1),
        cost_estimate=cost(18),
        name="attention_back_rest",
    )(words, grad_attended, qkv, prob, normed, grad_first, out_rows)


def normed_gradient(grad_qkv, weights, rows_in):
    count, width = rows_in.shape
    span = grad_qkv.shape[1]

    def body(grad_ref, weights_ref, in_ref, back_ref, sums):
        @pl.when(pl.program_id(0) == 0)
        def _():
            sums[...] = jnp.zeros_like(sums)

        back = contract_last(grad_ref[...], weights_ref[:, :span])
        back_ref[...] = back.astype(jnp.bfloat16)
        unit_signal, _ = norm_parts(in_ref[...].astype(jnp.float32))
        sums[0:1, :] += jnp.sum(back * unit_signal, axis=0, keepdims=True)
        sums[1:2, :] += jnp.sum(back, axis=0, keepdims=True)

    return pl.pallas_call(
        body,
        grid=(count // BLOCK,),
        in_specs=[
            pl.BlockSpec((BLOCK, span), lambda i: (i, 0)),
            pl.BlockSpec(weights.shape, lambda i: (0, 0)),
            pl.BlockSpec((BLOCK, width), lambda i: (i, 0)),
        ],
        out_specs=[
            pl.BlockSpec((BLOCK, width), lambda i: (i, 0)),
            pl.BlockSpec((2, width), lambda i: (0, 0)),
        ],
        out_shape=[shaped((count, width), jnp.bfloat16), shaped((2, width), jnp.float32)],
        compiler_params=params(1),
        cost_estimate=cost(5.6),
        name="normed_gradient",
    )(grad_qkv, weights, rows_in)


def input_gradient(rows_in, own, other, grad_middle, rep):
    count, width = rows_in.shape

    def body(in_ref, own_ref, other_ref, middle_ref, rep_ref, out_ref):
        unit_signal, scale = norm_parts(in_ref[...].astype(jnp.float32))
        grad = own_ref[...].astype(jnp.float32) + other_ref[...].astype(jnp.float32)
        out_ref[...] = middle_ref[...] + norm_back(grad, unit_signal, scale, rep_ref[0:1, :])

    block = pl.BlockSpec((BLOCK, width), lambda i: (i, 0))
    return pl.pallas_call(
        body,
        grid=(count // BLOCK,),
        in_specs=[block, block, block, block, pl.BlockSpec(rep.shape, lambda i: (0, 0))],
        out_specs=block,
        out_shape=shaped((count, width), jnp.float32),
        compiler_params=params(1),
        cost_estimate=cost(5.7),
        name="input_gradient",
    )(rows_in, own, other, grad_middle, rep)


def adam_unit(terms, states, strides):
    flat = [array.reshape(-1, 128) for state in states for array in state]

    def body(*refs):
        terms_here, refs = refs[: len(terms)], refs[len(terms) :]
        inputs, outputs = refs[: len(flat)], refs[len(flat) :]
        for state, start, step, column in strides:
            columns = slice(column * 128, (column + 1) * 128)
            gradient = terms_here[0][0, :, columns].astype(jnp.float32)
            for term in terms_here[1:]:
                gradient = gradient + term[0, :, columns].astype(jnp.float32)
            rows = pl.ds(start, UNIT_ROWS, stride=step)
            weight, one, two = (inputs[3 * state + i][rows, :] for i in range(3))
            updated = adam_step(weight, one, two, gradient, MATRIX_RATE, MATRIX_DECAY)
            for i in range(3):
                outputs[3 * state + i][rows, :] = updated[i]

    whole = [pl.BlockSpec(array.shape, lambda i: (0, 0)) for array in flat]
    results = pl.pallas_call(
        body,
        grid=(1,),
        in_specs=[pl.BlockSpec((1, UNIT_ROWS, UNIT_WIDTH), lambda i: (0, 0, 0))] * len(terms)
        + whole,
        out_specs=whole,
        out_shape=[shaped(array.shape, jnp.float32) for array in flat],
        compiler_params=params(1),
        cost_estimate=cost(2.5),
        name="adam_unit",
    )(*terms, *flat)
    return [array.reshape(1, -1) for array in results]


def on_device(
    patch_rows,
    cotangent,
    mask_token,
    lengths,
    masked,
    dealing,
    qkv_master,
    qkv_first,
    qkv_second,
    out_master,
    out_first,
    out_second,
    fc1_master,
    fc1_first,
    fc1_second,
    fc2_master,
    fc2_first,
    fc2_second,
    rep_master,
    rep_first,
    rep_second,
    split_master,
    split_first,
    split_second,
):
    slot_count, capacity, feature_width = patch_rows.shape
    half_width = mask_token.shape[0]
    dp_count = lax.axis_size("dp")
    member = lax.axis_index("dp")
    core_index = lax.axis_index("mp")
    positions_here = cotangent.shape[1]
    position_span = positions_here * dp_count
    heads_here = half_width // HEAD
    row_count = slot_count * capacity
    strip_count = lengths.shape[0]
    held_count = strip_count * positions_here
    words = jnp.stack([member, 1 + core_index, 2 - core_index, core_index]).astype(jnp.int32)

    inputs = patch_rows.reshape(row_count, feature_width)
    split_rows = split_master[0]
    unit_a, unit_b, unit_c = pack_units(qkv_master, out_master, fc1_master, fc2_master)

    patch_index = jnp.arange(PATCHES, dtype=jnp.int32)
    visible_all = (patch_index[None, :] < lengths[:, None]) & (masked == 0)
    strips_here = lax.dynamic_slice_in_dim(dealing, member * slot_count, slot_count)
    visible_here = visible_all[strips_here]
    rank_here = jnp.cumsum(visible_here.astype(jnp.int32), axis=1) - 1
    counts_here = jnp.sum(visible_here.astype(jnp.int32), axis=1)
    valid_rows = jnp.arange(capacity, dtype=jnp.int32)[None, :] < counts_here[:, None]
    column_bias = jnp.where(valid_rows, 0.0, -1e30).astype(jnp.float32).reshape(1, row_count)
    padding = position_span - PATCHES
    visible_padded = jnp.pad(visible_here, ((0, 0), (0, padding)))
    rank_padded = jnp.pad(jnp.maximum(rank_here, 0), ((0, 0), (0, padding)))
    own_positions = jnp.arange(positions_here, dtype=jnp.int32) * dp_count + member
    inside = own_positions < PATCHES
    visible_own = visible_all[:, jnp.minimum(own_positions, PATCHES - 1)] & inside[None, :]
    strip_row = (
        jnp.arange(positions_here, dtype=jnp.int32)[None, :] * strip_count + dealing[:, None]
    ).reshape(held_count)
    deal = (
        strip_row[:, None] == jnp.arange(held_count, dtype=jnp.int32)[None, :]
    ).astype(jnp.bfloat16)
    encoder_row = jnp.where(
        visible_padded,
        rank_padded + jnp.arange(slot_count, dtype=jnp.int32)[:, None] * capacity,
        -1,
    )
    encoder_row = jnp.transpose(
        encoder_row.reshape(slot_count, positions_here, dp_count), (2, 0, 1)
    ).reshape(held_count)
    pick = (
        jnp.arange(row_count, dtype=jnp.int32)[:, None] == encoder_row[None, :]
    ).astype(jnp.bfloat16)
    unseen = jnp.transpose(jnp.logical_not(visible_own) & inside[None, :]).reshape(held_count)

    cotangent_rows = jnp.transpose(
        cotangent.reshape(strip_count, positions_here, half_width), (1, 0, 2)
    ).reshape(held_count, half_width)

    def spread_out(array):
        return hop_by_core(array, 1, 2, dp_count), hop_by_core(array, 2, 1, dp_count)

    def exchanged(array):
        array = array.reshape(dp_count, slot_count * positions_here, half_width)
        array = lax.all_to_all(array, "dp", split_axis=0, concat_axis=0, tiled=True)
        return array.reshape(held_count, half_width)

    far_a = hop(unit_a, 12, dp_count)
    normed = first_norm(inputs, rep_master)
    dealt = product(deal, cotangent_rows).astype(jnp.bfloat16)
    far_a, normed, dealt, unit_b, unit_c = together(far_a, normed, dealt, unit_b, unit_c)

    pair_a = jnp.concatenate([unit_a, far_a])
    near_a = hop(pair_a, 4, dp_count)
    far_b = hop(unit_b, 12, dp_count)
    near_a, far_b, dealt, column_bias, pick = together(near_a, far_b, dealt, column_bias, pick)

    column_a = jnp.concatenate([pair_a, near_a])
    first_a, second_a = spread_out(column_a)
    returned = exchanged(dealt)
    pair_b = jnp.concatenate([unit_b, far_b])
    near_b = hop(pair_b, 4, dp_count)
    far_c = hop(unit_c, 12, dp_count)
    first_a, second_a, near_b, far_c = together(first_a, second_a, near_b, far_c)

    third_a = hop_by_core(first_a, 2, 1, dp_count)
    column_b = jnp.concatenate([pair_b, near_b])
    pair_c = jnp.concatenate([unit_c, far_c])
    near_c = hop(pair_c, 4, dp_count)
    third_a, near_c, normed, column_b = together(third_a, near_c, normed, column_b)

    first_heads = 2
    first_b, second_b = spread_out(column_b)
    column_c = jnp.concatenate([pair_c, near_c])
    qkv, prob, attended, weights_a, w_output = attention_first(
        words, normed, split_rows, column_bias, (column_a, first_a, second_a, third_a), first_heads
    )
    first_b, second_b, column_c, qkv, attended = together(
        first_b, second_b, column_c, qkv, attended
    )

    third_b = hop_by_core(first_b, 2, 1, dp_count)
    first_c, second_c = spread_out(column_c)
    prob_rest, attended_rest, branch = attention_rest(
        qkv, column_bias, attended, w_output, first_heads
    )
    third_b, first_c, second_c, branch, returned, pick = together(
        third_b, first_c, second_c, branch, returned, pick
    )

    branch_other = swap_cores(branch)
    gathered = product(pick, returned).astype(jnp.bfloat16)
    branch_other, gathered, first_c = together(branch_other, gathered, first_c)

    gathered_other = swap_cores(gathered)
    third_c = hop_by_core(first_c, 2, 1, dp_count)
    middle, normed_two, active, slope, w_first = mlp_forward(
        words, inputs, branch, branch_other, rep_master, split_rows,
        (column_b, first_b, second_b, third_b),
    )
    gathered_other, third_c, active = together(gathered_other, third_c, active)

    grad_out = jnp.where(
        core_index == 0,
        jnp.concatenate([gathered, gathered_other], axis=1),
        jnp.concatenate([gathered_other, gathered], axis=1),
    )
    sent_c, kept_c = second_gradient(words, active, grad_out)
    sent_c, kept_c, active, grad_out = together(sent_c, kept_c, active, grad_out)

    one_c = hop_by_core(sent_c, 2, 1, dp_count)
    grad_hidden, back_two, second, hidden_sum, grad_sum = mlp_back(
        words, active, slope, grad_out, w_first, (column_c, first_c, second_c, third_c)
    )
    one_c, grad_hidden, back_two, second = together(one_c, grad_hidden, back_two, second)

    two_c_sent = added(4, 8, kept_c, one_c)
    two_c = hop_by_core(two_c_sent, 1, 2, dp_count)
    back_two_other = swap_cores(back_two)
    second_other = swap_cores(second)
    sent_b, kept_b = first_gradient(words, normed_two, grad_hidden)
    two_c, back_two_other, second_other, sent_b, kept_b = together(
        two_c, back_two_other, second_other, sent_b, kept_b
    )

    one_b = hop_by_core(sent_b, 2, 1, dp_count)
    three_c = hop(added(2, 4, kept_c, one_c, two_c), 4, dp_count)
    grad_middle, grad_attended, grad_first, out_rows, width_sums = attention_back_first(
        middle, back_two, back_two_other, grad_out, rep_master, w_output, qkv, prob, attended,
        attended_rest,
    )
    total = second.astype(jnp.float32) + second_other.astype(jnp.float32) + rep_master[5]
    result = (middle + total).astype(jnp.bfloat16)
    result_half = lax.dynamic_slice_in_dim(result, core_index * half_width, half_width, 1)
    outgoing = contract_rows(pick, result_half).astype(jnp.bfloat16)
    one_b, three_c, grad_attended, grad_first, out_rows, outgoing = together(
        one_b, three_c, grad_attended, grad_first, out_rows, outgoing
    )

    arrived = exchanged(outgoing)
    two_b = hop_by_core(added(4, 8, kept_b, one_b), 1, 2, dp_count)
    four_c = hop(added(1, 2, kept_c, one_c, two_c, three_c), 12, dp_count)
    grad_qkv, half_sums, sent_a, kept_a = attention_back_rest(
        words, grad_attended, qkv, prob_rest, normed, grad_first, out_rows
    )
    two_b, four_c, grad_qkv, sent_a, kept_a = together(two_b, four_c, grad_qkv, sent_a, kept_a)

    one_a = hop_by_core(sent_a, 2, 1, dp_count)
    three_b = hop(added(2, 4, kept_b, one_b, two_b), 4, dp_count)
    back_one, norm_sums = normed_gradient(grad_qkv, weights_a, inputs)
    terms_c = (kept_c, one_c, two_c, three_c, four_c)
    fc2_state = (fc2_master, fc2_first, fc2_second)
    fc2_new = adam_unit(
        terms_c,
        [fc2_state],
        [(0, part * UNIT_ROWS * 6 + j, 6, part * 6 + j) for part in range(2) for j in range(6)],
    )
    mask_grad = product(unseen.astype(jnp.bfloat16)[None, :], cotangent_rows)
    rep_part = jnp.concatenate([norm_sums, width_sums, 0.5 * grad_sum]).reshape(-1, half_width)
    rep_rows = rep_part.shape[0]
    one_a, three_b, back_one, rep_part, mask_grad, *fc2_new = together(
        one_a, three_b, back_one, rep_part, mask_grad, *fc2_new
    )

    back_one_other = swap_cores(back_one)
    rep_part = rep_part + swap_cores(rep_part)
    two_a = hop_by_core(added(4, 8, kept_a, one_a), 1, 2, dp_count)
    four_b = hop(added(1, 2, kept_b, one_b, two_b, three_b), 12, dp_count)
    vectors = jnp.concatenate(
        [rep_part, half_sums, hidden_sum.reshape(-1, half_width), mask_grad]
    )
    two_a, four_b, vectors, back_one_other = together(two_a, four_b, vectors, back_one_other)

    three_a = hop(added(2, 4, kept_a, one_a, two_a), 4, dp_count)
    parts = [hop(vectors, distance, dp_count) for distance in (1, 2, 3)]
    input_grad = input_gradient(inputs, back_one, back_one_other, grad_middle, rep_master)
    fc1_state = (fc1_master, fc1_first, fc1_second)
    fc1_new = adam_unit(
        (kept_b, one_b, two_b, three_b, four_b),
        [fc1_state],
        [(0, j, 12, j) for j in range(12)],
    )
    three_a, vectors, parts, input_grad, arrived, *fc1_new = together(
        three_a, vectors, parts, input_grad, arrived, *fc1_new
    )

    four_a = hop(added(1, 2, kept_a, one_a, two_a, three_a), 12, dp_count)
    vectors = (vectors + parts[0]) + (parts[1] + parts[2])
    parts = [hop(vectors, distance, dp_count) for distance in (4, 8, 12)]
    full_out = contract_rows(deal, arrived)
    full_out = jnp.where(unseen[:, None], mask_token.astype(jnp.float32)[None, :], full_out)
    full_out = full_out.astype(jnp.bfloat16)
    four_a, vectors, parts, full_out = together(four_a, vectors, parts, full_out)

    vectors = (vectors + parts[0]) + (parts[1] + parts[2])
    full_out = full_out.reshape(positions_here, strip_count, half_width)
    full_out = jnp.transpose(full_out, (1, 0, 2))[:, :, None, :]
    input_grad = input_grad.reshape(slot_count, capacity, feature_width)
    rep_total = vectors[:rep_rows].reshape(rep_master.shape)
    split_total = vectors[rep_rows:-1].reshape(split_master.shape)
    mask_total = vectors[-1]
    terms_a = (kept_a, one_a, two_a, three_a, four_a)
    qkv_state = (qkv_master, qkv_first, qkv_second)
    out_state = (out_master, out_first, out_second)
    qkv_out_new = adam_unit(
        terms_a,
        [qkv_state, out_state],
        [(0, j, 9, j) for j in range(9)] + [(1, j, 3, 9 + j) for j in range(3)],
    )
    rep_new = adam_step(rep_master, rep_first, rep_second, rep_total, VECTOR_RATE, 0.0)
    split_new = adam_step(split_master, split_first, split_second, split_total, VECTOR_RATE, 0.0)
    return (
        full_out,
        input_grad,
        mask_total,
        *qkv_out_new,
        *fc1_new,
        *fc2_new,
        *rep_new,
        *split_new,
    )


def solution(mesh):
    placed = (
        P("dp", None, None),
        P(None, None, "dp", "mp"),
        P("mp"),
        P(),
        P(),
        P(),
        P("mp", "dp"),
        P("mp", "dp"),
        P("mp", "dp"),
        P("mp", "dp"),
        P("mp", "dp"),
        P("mp", "dp"),
        P("mp", "dp"),
        P("mp", "dp"),
        P("mp", "dp"),
        P("mp", "dp"),
        P("mp", "dp"),
        P("mp", "dp"),
        P(),
        P(),
        P(),
        P("mp", None, None),
        P("mp", None, None),
        P("mp", None, None),
    )
    tuned = mesh.shape["dp"] == 16 and mesh.shape["mp"] == 2
    return jax.shard_map(
        on_device if tuned else on_device_general,
        mesh=mesh,
        in_specs=placed,
        out_specs=(
            P(None, None, "dp", "mp"),
            P("dp", None, None),
            P("mp"),
            P("mp", "dp"),
            P("mp", "dp"),
            P("mp", "dp"),
            P("mp", "dp"),
            P("mp", "dp"),
            P("mp", "dp"),
            P("mp", "dp"),
            P("mp", "dp"),
            P("mp", "dp"),
            P("mp", "dp"),
            P("mp", "dp"),
            P("mp", "dp"),
            P(),
            P(),
            P(),
            P("mp", None, None),
            P("mp", None, None),
            P("mp", None, None),
        ),
        check_vma=False,
    )
```

```python
import jax
import jax.numpy as jnp
from jax import lax
from jax.experimental import pallas as pl
from jax.experimental.pallas import tpu as pltpu
from jax.sharding import PartitionSpec as P

HEAD = 64
PATCHES = 529
STEP = 10


NORM_EPS = 1e-06
BETA_ONE = 0.9
BETA_TWO = 0.999
ADAM_EPS = 1e-08
MATRIX_RATE = 0.15
MATRIX_DECAY = 0.05
VECTOR_RATE = 0.6


def layer_norm(signal, norm_gain, norm_shift):
    average = jnp.mean(signal, axis=-1, keepdims=True)
    centered = signal - average
    spread = jnp.mean(centered * centered, axis=-1, keepdims=True)
    return centered * lax.rsqrt(spread + NORM_EPS) * norm_gain + norm_shift


def exact_gelu(signal):
    return jax.nn.gelu(signal, approximate=False)


def product(left, right):
    return jnp.dot(left, right, preferred_element_type=jnp.float32)


def contract_last(left, right):
    return lax.dot_general(
        left, right, (((1,), (1,)), ((), ())), preferred_element_type=jnp.float32
    )


def contract_rows(left, right):
    return lax.dot_general(
        left, right, (((0,), (0,)), ((), ())), preferred_element_type=jnp.float32
    )


def adam_step(weight, moment_one, moment_two, gradient, step_rate, decay_rate):
    one_new = BETA_ONE * moment_one + (1.0 - BETA_ONE) * gradient
    two_new = BETA_TWO * moment_two + (1.0 - BETA_TWO) * gradient * gradient
    one_hat = one_new / (1.0 - BETA_ONE**STEP)
    two_hat = two_new / (1.0 - BETA_TWO**STEP)
    weight_new = weight - step_rate * (
        one_hat / (jnp.sqrt(two_hat) + ADAM_EPS) + decay_rate * weight
    )
    return (weight_new, one_new, two_new)


def total_over_cores(partial):
    return partial.astype(jnp.float32) + swap_cores(partial).astype(jnp.float32)


def pair_scores(queries, key_rows, valid_rows):
    scores = jnp.einsum(
        "qhd,khd->hqk", queries, key_rows, preferred_element_type=jnp.float32
    ) * HEAD ** (-0.5)
    return jnp.where(valid_rows[None, None, :], scores, -1e30)


def attend_pair(pair_block):
    queries, key_rows, value_rows, valid_rows = pair_block
    scores = pair_scores(queries, key_rows, valid_rows)
    row_max = jnp.max(scores, axis=2, keepdims=True)
    lifted = jnp.exp(scores - row_max)
    row_total = jnp.sum(lifted, axis=2, keepdims=True)
    probability = (lifted / row_total).astype(jnp.bfloat16)
    attended = jnp.einsum(
        "hqk,khd->qhd", probability, value_rows, preferred_element_type=jnp.float32
    )
    return (attended.astype(jnp.bfloat16), row_max[:, :, 0] + jnp.log(row_total[:, :, 0]))


def attend_pair_back(pair_block):
    queries, key_rows, value_rows, valid_rows, log_total, grad_attended = pair_block
    scores = pair_scores(queries, key_rows, valid_rows)
    probability = jnp.exp(scores - log_total[:, :, None])
    grad_prob = jnp.einsum(
        "qhd,khd->hqk", grad_attended, value_rows, preferred_element_type=jnp.float32
    )
    inner_sum = jnp.sum(probability * grad_prob, axis=2, keepdims=True)
    grad_scores = (probability * (grad_prob - inner_sum)).astype(jnp.bfloat16)
    score_scale = HEAD ** (-0.5)
    grad_queries = (
        jnp.einsum("hqk,khd->qhd", grad_scores, key_rows, preferred_element_type=jnp.float32)
        * score_scale
    )
    grad_keys = (
        jnp.einsum("hqk,qhd->khd", grad_scores, queries, preferred_element_type=jnp.float32)
        * score_scale
    )
    grad_values = jnp.einsum(
        "hqk,qhd->khd",
        probability.astype(jnp.bfloat16),
        grad_attended,
        preferred_element_type=jnp.float32,
    )
    return (
        grad_queries.astype(jnp.bfloat16),
        grad_keys.astype(jnp.bfloat16),
        grad_values.astype(jnp.bfloat16),
    )


def hop(array, distance, axis_count):
    return lax.ppermute(array, "dp", [(i, i ^ distance) for i in range(axis_count)])


def swap_cores(array):
    return lax.ppermute(array, "mp", [(0, 1), (1, 0)])


def place_chunks(pieces, chunk_ids, member, count):
    rows, width = pieces[0].shape[1:]

    def body(member_ref, *refs):
        sources, target, semaphores = refs[:-2], refs[-2], refs[-1]
        copies = []
        for source, ids in zip(sources, chunk_ids):
            for place, distance in enumerate(ids):
                copies.append(
                    pltpu.make_async_copy(
                        source.at[place],
                        target.at[member_ref[0] ^ distance],
                        semaphores.at[len(copies)],
                    )
                )
        for copy in copies:
            copy.start()
        for copy in copies:
            copy.wait()

    return pl.pallas_call(
        body,
        in_specs=[pl.BlockSpec(memory_space=pltpu.SMEM)]
        + [pl.BlockSpec(memory_space=pl.ANY)] * len(pieces),
        out_specs=pl.BlockSpec(memory_space=pltpu.VMEM),
        out_shape=jax.ShapeDtypeStruct((count, rows, width), pieces[0].dtype),
        scratch_shapes=[pltpu.SemaphoreType.DMA((count,))],
        cost_estimate=pl.CostEstimate(
            flops=0, transcendentals=0, bytes_accessed=4 * count * rows * width
        ),
        name="place_chunks",
    )(member, *pieces)


def pick_chunks(whole, chunk_ids, member):
    count, rows, width = whole.shape

    def body(member_ref, source, *refs):
        targets, semaphores = refs[:-1], refs[-1]
        copies = []
        for target, ids in zip(targets, chunk_ids):
            for place, distance in enumerate(ids):
                copies.append(
                    pltpu.make_async_copy(
                        source.at[member_ref[0] ^ distance],
                        target.at[place],
                        semaphores.at[len(copies)],
                    )
                )
        for copy in copies:
            copy.start()
        for copy in copies:
            copy.wait()

    return pl.pallas_call(
        body,
        in_specs=[pl.BlockSpec(memory_space=pltpu.SMEM), pl.BlockSpec(memory_space=pltpu.VMEM)],
        out_specs=[pl.BlockSpec(memory_space=pl.ANY)] * len(chunk_ids),
        out_shape=[
            jax.ShapeDtypeStruct((len(ids), rows, width), whole.dtype) for ids in chunk_ids
        ],
        scratch_shapes=[pltpu.SemaphoreType.DMA((count,))],
        cost_estimate=pl.CostEstimate(
            flops=0, transcendentals=0, bytes_accessed=4 * count * rows * width
        ),
        name="pick_chunks",
    )(member, whole)


def gather_chunks(chunk, member, count):
    own = chunk[None]
    if count == 16:
        near, far, last = (hop(own, k, count) for k in (4, 8, 12))
        first, second = jnp.concatenate([own, near]), jnp.concatenate([far, last])
        x_first, x_second = hop(first, 1, count), hop(second, 1, count)
        y_first, y_second = hop(first, 2, count), hop(second, 2, count)
        d_first, d_second = hop(y_first, 1, count), hop(x_second, 2, count)
        pieces = [first, second, x_first, x_second, y_first, y_second, d_first, d_second]
        ids = [(0, 4), (8, 12), (1, 5), (9, 13), (2, 6), (10, 14), (3, 7), (11, 15)]
    else:
        held, step = own, 1
        while step < count:
            held = jnp.concatenate([held, hop(held, step, count)])
            step *= 2
        pieces, ids = [held], [tuple(range(count))]
    return place_chunks(pieces, ids, member, count)


def scatter_chunks(whole, member, count):
    def wide(array):
        return array.astype(jnp.float32)

    if count == 16:
        ids = [(3, 7), (11, 15), (2, 6), (9, 13), (10, 14), (1, 5), (0, 4), (8, 12)]
        d_first, d_second, y_first, x_second, y_second, x_first, first, second = pick_chunks(
            whole, ids, member
        )
        d_first, d_second = hop(d_first, 1, count), hop(d_second, 2, count)
        y_second, x_first = hop(y_second, 2, count), hop(x_first, 1, count)
        y_first = hop((wide(y_first) + wide(d_first)).astype(jnp.bfloat16), 2, count)
        x_second = hop((wide(x_second) + wide(d_second)).astype(jnp.bfloat16), 1, count)
        first = wide(first) + wide(y_first) + wide(x_first)
        second = wide(second) + wide(y_second) + wide(x_second)
        near = hop(first[1].astype(jnp.bfloat16), 4, count)
        far = hop(second[0].astype(jnp.bfloat16), 8, count)
        last = hop(second[1].astype(jnp.bfloat16), 12, count)
        return first[0] + wide(near) + wide(far) + wide(last)
    (held,) = pick_chunks(whole, [tuple(range(count))], member)
    held = wide(held)
    step = count // 2
    while step:
        held = held[:step] + wide(hop(held[step:].astype(jnp.bfloat16), step, count))
        step //= 2
    return held[0]


def sum_over_dp(vector, count):
    if count == 16:
        for low, high in ((1, 2), (4, 8)):
            other, third, fourth = (hop(vector, k, count) for k in (low, high, low + high))
            vector = (vector + other) + (third + fourth)
        return vector
    step = 1
    while step < count:
        vector = vector + hop(vector, step, count)
        step *= 2
    return vector


def on_device_general(
    patch_rows,
    cotangent,
    mask_token,
    lengths,
    masked,
    dealing,
    qkv_master,
    qkv_first,
    qkv_second,
    out_master,
    out_first,
    out_second,
    fc1_master,
    fc1_first,
    fc1_second,
    fc2_master,
    fc2_first,
    fc2_second,
    rep_master,
    rep_first,
    rep_second,
    split_master,
    split_first,
    split_second,
):
    slot_count, capacity, feature_width = patch_rows.shape
    half_width = mask_token.shape[0]
    dp_count = lax.axis_size("dp")
    member = lax.axis_index("dp")
    core_index = lax.axis_index("mp")
    positions_here = cotangent.shape[1]
    position_span = positions_here * dp_count
    heads_here = half_width // HEAD
    hidden_width = (split_master.shape[1] - 2) * half_width
    row_count = slot_count * capacity
    pair_count = slot_count // 2
    pair_length = 2 * capacity
    patch_index = jnp.arange(PATCHES, dtype=jnp.int32)
    visible_all = (patch_index[None, :] < lengths[:, None]) & (masked == 0)
    strips_here = lax.dynamic_slice_in_dim(dealing, member * slot_count, slot_count)
    visible_here = visible_all[strips_here]
    rank_here = jnp.cumsum(visible_here.astype(jnp.int32), axis=1) - 1
    counts_here = jnp.sum(visible_here.astype(jnp.int32), axis=1)
    valid_rows = jnp.arange(capacity, dtype=jnp.int32)[None, :] < counts_here[:, None]
    padding = position_span - PATCHES
    visible_padded = jnp.pad(visible_here, ((0, 0), (0, padding)))
    rank_padded = jnp.pad(jnp.maximum(rank_here, 0), ((0, 0), (0, padding)))
    own_positions = jnp.arange(positions_here, dtype=jnp.int32) * dp_count + member
    inside = own_positions < PATCHES
    visible_own = visible_all[:, jnp.minimum(own_positions, PATCHES - 1)] & inside[None, :]
    strip_count = lengths.shape[0]
    held_count = strip_count * positions_here
    strip_row = (
        jnp.arange(positions_here, dtype=jnp.int32)[None, :] * strip_count + dealing[:, None]
    ).reshape(held_count)
    deal = (
        strip_row[:, None] == jnp.arange(held_count, dtype=jnp.int32)[None, :]
    ).astype(jnp.bfloat16)
    encoder_row = jnp.where(
        visible_padded,
        rank_padded + jnp.arange(slot_count, dtype=jnp.int32)[:, None] * capacity,
        -1,
    )
    encoder_row = jnp.transpose(
        encoder_row.reshape(slot_count, positions_here, dp_count), (2, 0, 1)
    ).reshape(held_count)
    pick = (
        jnp.arange(row_count, dtype=jnp.int32)[:, None] == encoder_row[None, :]
    ).astype(jnp.bfloat16)
    unseen = jnp.transpose(jnp.logical_not(visible_own) & inside[None, :]).reshape(held_count)
    member_word = member.astype(jnp.int32).reshape(1)

    cotangent_rows = jnp.transpose(cotangent.reshape(strip_count, positions_here, half_width), (1, 0, 2))
    cotangent_rows = cotangent_rows.reshape(held_count, half_width)
    dealt = product(deal, cotangent_rows).astype(jnp.bfloat16)
    returned = lax.all_to_all(
        dealt.reshape(dp_count, slot_count * positions_here, half_width),
        "dp",
        split_axis=0,
        concat_axis=0,
        tiled=True,
    ).reshape(held_count, half_width)
    gathered = product(pick, returned).astype(jnp.bfloat16)
    gathered_other = swap_cores(gathered)
    grad_out = jnp.where(
        core_index == 0,
        jnp.concatenate([gathered, gathered_other], axis=1),
        jnp.concatenate([gathered_other, gathered], axis=1),
    )
    mask_grad = product(unseen.astype(jnp.bfloat16)[None, :], cotangent_rows)[0]

    def gathered_matrix(master, rows, width):
        chunk = master.astype(jnp.bfloat16).reshape(rows // dp_count, width)
        return gather_chunks(chunk, member_word, dp_count).reshape(rows, width)

    w_attention = gathered_matrix(qkv_master, feature_width, 3 * half_width)
    w_output = gathered_matrix(out_master, half_width, feature_width)
    w_first = gathered_matrix(fc1_master, feature_width, hidden_width)
    w_second = gathered_matrix(fc2_master, hidden_width, feature_width)
    inputs = patch_rows.reshape(row_count, feature_width).astype(jnp.float32)
    normed_full, norm_back_one = jax.vjp(layer_norm, inputs, rep_master[0], rep_master[1])
    normed = normed_full.astype(jnp.bfloat16)
    projected = product(normed, w_attention).reshape(row_count, 3, half_width)
    queries = (projected[:, 0] + split_master[0, 0]).astype(jnp.bfloat16)
    key_rows = projected[:, 1].astype(jnp.bfloat16)
    value_rows = (projected[:, 2] + split_master[0, 1]).astype(jnp.bfloat16)

    def by_pair(array):
        return array.reshape(pair_count, pair_length, heads_here, HEAD)

    pair_valid = valid_rows.reshape(pair_count, pair_length)
    attended, log_total = lax.map(
        attend_pair, (by_pair(queries), by_pair(key_rows), by_pair(value_rows), pair_valid)
    )
    attended = attended.reshape(row_count, half_width)
    branch = total_over_cores(product(attended, w_output)) + rep_master[4]
    middle = inputs + branch
    normed_two_full, norm_back_two = jax.vjp(layer_norm, middle, rep_master[2], rep_master[3])
    normed_two = normed_two_full.astype(jnp.bfloat16)
    hidden = product(normed_two, w_first) + split_master[0, 2:].reshape(hidden_width)
    active_full, gelu_back = jax.vjp(exact_gelu, hidden)
    active = active_full.astype(jnp.bfloat16)
    second = total_over_cores(product(active, w_second).astype(jnp.bfloat16)) + rep_master[5]
    result = (middle + second).astype(jnp.bfloat16)
    result_half = lax.dynamic_slice_in_dim(result, core_index * half_width, half_width, 1)
    outgoing = contract_rows(pick, result_half).astype(jnp.bfloat16)
    arrived = lax.all_to_all(
        outgoing.reshape(dp_count, slot_count * positions_here, half_width),
        "dp",
        split_axis=0,
        concat_axis=0,
        tiled=True,
    ).reshape(held_count, half_width)
    full_out = contract_rows(deal, arrived)
    full_out = jnp.where(unseen[:, None], mask_token.astype(jnp.float32)[None, :], full_out)
    full_out = full_out.astype(jnp.bfloat16).reshape(positions_here, strip_count, half_width)
    full_out = jnp.transpose(full_out, (1, 0, 2))[:, :, None, :]
    grad_rows = grad_out.astype(jnp.float32)
    bias_two_grad = jnp.sum(grad_rows, axis=0)
    grad_active = contract_last(grad_out, w_second)
    grad_hidden = gelu_back(grad_active)[0].astype(jnp.bfloat16)
    fc2_grad = contract_rows(active, grad_out)
    fc1_grad = contract_rows(normed_two, grad_hidden)
    hidden_bias_grad = jnp.sum(grad_hidden.astype(jnp.float32), axis=0)
    grad_normed_two = total_over_cores(contract_last(grad_hidden, w_first))
    grad_middle_part, gain_two_grad, shift_two_grad = norm_back_two(grad_normed_two)
    grad_middle = grad_rows + grad_middle_part
    grad_branch = grad_middle.astype(jnp.bfloat16)
    out_bias_grad = jnp.sum(grad_branch.astype(jnp.float32), axis=0)
    out_grad = contract_rows(attended, grad_branch)
    grad_attended = contract_last(grad_branch, w_output).astype(jnp.bfloat16)
    grad_queries, grad_keys, grad_values = lax.map(
        attend_pair_back,
        (
            by_pair(queries),
            by_pair(key_rows),
            by_pair(value_rows),
            pair_valid,
            log_total,
            by_pair(grad_attended),
        ),
    )
    grad_queries = grad_queries.reshape(row_count, half_width)
    grad_keys = grad_keys.reshape(row_count, half_width)
    grad_values = grad_values.reshape(row_count, half_width)
    grad_projected = jnp.stack([grad_queries, grad_keys, grad_values], axis=1).reshape(
        row_count, 3 * half_width
    )
    qkv_grad = contract_rows(normed, grad_projected)
    query_bias_grad = jnp.sum(grad_queries.astype(jnp.float32), axis=0)
    value_bias_grad = jnp.sum(grad_values.astype(jnp.float32), axis=0)
    grad_normed = total_over_cores(contract_last(grad_projected, w_attention))
    grad_inputs_part, gain_one_grad, shift_one_grad = norm_back_one(grad_normed)
    input_grad = (grad_middle + grad_inputs_part).reshape(slot_count, capacity, feature_width)
    def scattered(gradient):
        rows, width = gradient.shape
        chunks = gradient.astype(jnp.bfloat16).reshape(dp_count, rows // dp_count, width)
        return scatter_chunks(chunks, member_word, dp_count).reshape(1, -1)

    fc2_total = scattered(fc2_grad)
    fc1_total = scattered(fc1_grad)
    out_total = scattered(out_grad)
    qkv_total = scattered(qkv_grad)
    rep_grad = jnp.stack(
        [gain_one_grad, shift_one_grad, gain_two_grad, shift_two_grad, out_bias_grad, bias_two_grad]
    )
    split_grad = jnp.concatenate(
        [query_bias_grad[None], value_bias_grad[None], hidden_bias_grad.reshape(-1, half_width)],
        axis=0,
    )[None]
    packed = jnp.concatenate([mask_grad, rep_grad.reshape(-1), split_grad.reshape(-1)])
    packed = sum_over_dp(packed.reshape(-1, 128), dp_count).reshape(-1)
    mask_total = packed[:half_width]
    rep_total = packed[half_width : half_width + rep_grad.size].reshape(rep_grad.shape)
    split_total = packed[half_width + rep_grad.size :].reshape(split_grad.shape)
    qkv_new = adam_step(qkv_master, qkv_first, qkv_second, qkv_total, MATRIX_RATE, MATRIX_DECAY)
    out_new = adam_step(out_master, out_first, out_second, out_total, MATRIX_RATE, MATRIX_DECAY)
    fc1_new = adam_step(fc1_master, fc1_first, fc1_second, fc1_total, MATRIX_RATE, MATRIX_DECAY)
    fc2_new = adam_step(fc2_master, fc2_first, fc2_second, fc2_total, MATRIX_RATE, MATRIX_DECAY)
    rep_new = adam_step(rep_master, rep_first, rep_second, rep_total, VECTOR_RATE, 0.0)
    split_new = adam_step(split_master, split_first, split_second, split_total, VECTOR_RATE, 0.0)
    return (
        full_out,
        input_grad,
        mask_total,
        qkv_new[0],
        qkv_new[1],
        qkv_new[2],
        out_new[0],
        out_new[1],
        out_new[2],
        fc1_new[0],
        fc1_new[1],
        fc1_new[2],
        fc2_new[0],
        fc2_new[1],
        fc2_new[2],
        rep_new[0],
        rep_new[1],
        rep_new[2],
        split_new[0],
        split_new[1],
        split_new[2],
    )


BLOCK = 384
UNIT_ROWS = 48
UNIT_WIDTH = 1536
Z_ORDER = (0, 12, 4, 8)
VMEM_BYTES = 60 * 1024 * 1024
ANY = pl.BlockSpec(memory_space=pl.ANY)
IN_VMEM = pl.BlockSpec(memory_space=pltpu.VMEM)
IN_SMEM = pl.BlockSpec(memory_space=pltpu.SMEM)


def shaped(shape, dtype):
    return jax.ShapeDtypeStruct(shape, dtype)


def params(grid_axes=0):
    semantics = ("arbitrary",) * grid_axes if grid_axes else None
    return pltpu.CompilerParams(dimension_semantics=semantics, vmem_limit_bytes=VMEM_BYTES)


def cost(microseconds):
    return pl.CostEstimate(
        flops=int(microseconds * 1.15e9), transcendentals=0, bytes_accessed=1000000
    )


def together(*values):
    return lax.optimization_barrier(values)


def hop_by_core(array, first_core, second_core, count):
    pairs = []
    for i in range(count):
        pairs.append((2 * i, 2 * (i ^ first_core)))
        pairs.append((2 * i + 1, 2 * (i ^ second_core) + 1))
    return lax.ppermute(array, ("dp", "mp"), pairs)


def pack_units(qkv, out, fc1, fc2):
    def body(qkv_ref, out_ref, fc1_ref, fc2_ref, unit_a, unit_b, unit_c):
        def put(unit, column, rows):
            unit[0, :, column * 128 : (column + 1) * 128] = rows.astype(jnp.bfloat16)

        for j in range(9):
            put(unit_a, j, qkv_ref[pl.ds(j, UNIT_ROWS, stride=9), :])
        for j in range(3):
            put(unit_a, 9 + j, out_ref[pl.ds(j, UNIT_ROWS, stride=3), :])
        for j in range(12):
            put(unit_b, j, fc1_ref[pl.ds(j, UNIT_ROWS, stride=12), :])
        for half in range(2):
            for j in range(6):
                start = half * UNIT_ROWS * 6 + j
                put(unit_c, half * 6 + j, fc2_ref[pl.ds(start, UNIT_ROWS, stride=6), :])

    unit = shaped((1, UNIT_ROWS, UNIT_WIDTH), jnp.bfloat16)
    return pl.pallas_call(
        body,
        out_shape=[unit, unit, unit],
        compiler_params=params(),
        cost_estimate=cost(2),
        name="pack_units",
    )(
        *(array.reshape(-1, 128) for array in (qkv, out, fc1, fc2))
    )


def owner_of(words, piece, entry):
    extra = (0, words[1], words[2], 3)[piece]
    return words[0] ^ Z_ORDER[entry] ^ extra


def join_chunks(chunks):
    def body(*refs):
        for entry, ref in enumerate(refs[:-1]):
            refs[-1][entry] = ref[0]

    return pl.pallas_call(
        body,
        out_shape=shaped((len(chunks),) + chunks[0].shape[1:], chunks[0].dtype),
        compiler_params=params(),
        cost_estimate=cost(1.3),
        name="join_chunks",
    )(*chunks)


def last_messages(kept, one, two, carried):
    def body(kept_ref, one_ref, two_ref, carried_ref, *targets):
        vectors = carried_ref[...].astype(jnp.float32)
        vectors = (vectors + two_ref[4 * UNIT_ROWS :, :].astype(jnp.float32)).astype(jnp.bfloat16)
        for entry, target in enumerate(targets):
            rows = slice((entry + 1) * UNIT_ROWS, (entry + 2) * UNIT_ROWS)
            total = kept_ref[rows, :].astype(jnp.float32) + one_ref[rows, :].astype(jnp.float32)
            total = total + two_ref[rows, :].astype(jnp.float32)
            target[:UNIT_ROWS, :] = total.astype(jnp.bfloat16)
            target[UNIT_ROWS:, :] = vectors

    def rows(count, start=0):
        return pl.BlockSpec((count, UNIT_WIDTH), lambda i: (start, 0))

    message = shaped((UNIT_ROWS + 16, UNIT_WIDTH), jnp.bfloat16)
    return pl.pallas_call(
        body,
        grid=(1,),
        in_specs=[
            rows(4 * UNIT_ROWS), rows(4 * UNIT_ROWS), rows(4 * UNIT_ROWS + 16),
            rows(16, 4 * UNIT_ROWS // 16),
        ],
        out_specs=[rows(UNIT_ROWS + 16)] * 3,
        out_shape=[message] * 3,
        compiler_params=params(1),
        cost_estimate=cost(1.5),
        name="last_messages",
    )(kept, one, two, carried)


def added(start, stop, *arrays):
    total = 0.0
    for array, offset in arrays:
        total = total + array[start - offset : stop - offset].astype(jnp.float32)
    return total.astype(jnp.bfloat16)


def unit_shapes(extra=0):
    return [shaped((8 * UNIT_ROWS + extra, UNIT_WIDTH), jnp.bfloat16)] * 2


def unit_targets(words, sent, kept):
    def rows(array, entry):
        return array.at[pl.ds(entry * UNIT_ROWS, UNIT_ROWS), :]

    places = []
    for entry, distance in enumerate(Z_ORDER):
        own = words[0] ^ distance
        places.append((rows(sent, 4 + entry), own ^ 3))
        places.append((rows(sent, entry), own ^ words[2]))
        places.append((rows(kept, entry), own))
        places.append((rows(kept, 4 + entry), own ^ words[1]))
    return places


def unit_rows(owner, rows=UNIT_ROWS):
    return pl.ds(pl.multiple_of(owner * rows, 16), rows)


def norm_parts(signal):
    average = jnp.mean(signal, axis=1, keepdims=True)
    centered = signal - average
    scale = lax.rsqrt(jnp.mean(centered * centered, axis=1, keepdims=True) + NORM_EPS)
    return centered * scale, scale


def norm_back(grad, unit_signal, scale, gain):
    scaled = grad * gain
    mean_one = jnp.mean(scaled, axis=1, keepdims=True)
    mean_two = jnp.mean(scaled * unit_signal, axis=1, keepdims=True)
    return scale * (scaled - mean_one - unit_signal * mean_two)


def first_norm(rows, rep):
    count, width = rows.shape

    def body(rows_ref, rep_ref, normed_ref):
        unit_signal, _ = norm_parts(rows_ref[...].astype(jnp.float32))
        normed = unit_signal * rep_ref[0:1, :] + rep_ref[1:2, :]
        normed_ref[...] = normed.astype(jnp.bfloat16)

    return pl.pallas_call(
        body,
        grid=(count // BLOCK,),
        in_specs=[
            pl.BlockSpec((BLOCK, width), lambda i: (i, 0)),
            pl.BlockSpec(rep.shape, lambda i: (0, 0)),
        ],
        out_specs=pl.BlockSpec((BLOCK, width), lambda i: (i, 0)),
        out_shape=shaped((count, width), jnp.bfloat16),
        compiler_params=params(1),
        cost_estimate=cost(3.5),
        name="first_norm",
    )(rows, rep)


def fixed(*shape):
    return pl.BlockSpec(shape, lambda i: (0,) * len(shape))


def run_copies(pairs, semaphores):
    copies = [
        pltpu.make_async_copy(source, target, semaphores.at[i])
        for i, (source, target) in enumerate(pairs)
    ]
    for copy in copies:
        copy.start()
    for copy in copies:
        copy.wait()


class Copies:
    def __init__(self, semaphores):
        self.semaphores, self.used = semaphores, 0

    def start(self, pairs):
        started = []
        for source, target in pairs:
            copy = pltpu.make_async_copy(source, target, self.semaphores.at[self.used])
            self.used += 1
            copy.start()
            started.append(copy)
        return started


def finish(copies):
    for copy in copies:
        copy.wait()


def chunk_pairs(words_ref, pieces, target):
    pairs = []
    for piece, source in enumerate(pieces):
        for entry in range(4):
            owner = owner_of(words_ref, piece, entry)
            pairs.append((source.at[entry], target.at[unit_rows(owner), :]))
    return pairs


def attention_forward(words, normed, split, column_bias, pieces):
    count, width = normed.shape
    half = split.shape[1]
    pairs_of_heads = half // (2 * HEAD)

    def body(
        words_ref, normed_ref, split_ref, bias_ref, p0, p1, p2, p3,
        qkv_ref, prob_ref, attended_ref, partial_ref, weights_ref, w_out_ref, spread, semaphores,
    ):
        pair = pl.program_id(0)

        @pl.when(pair == 0)
        def _():
            copies = Copies(semaphores)
            finish(copies.start(chunk_pairs(words_ref, (p0, p1, p2, p3), weights_ref)))
            for block in range(count // BLOCK):
                rows = pl.ds(block * BLOCK, BLOCK)
                for part in range(3):
                    columns = slice(part * half, (part + 1) * half)
                    projected = product(normed_ref[rows, :], weights_ref[:, columns])
                    if part != 1:
                        projected = projected + split_ref[part // 2 : part // 2 + 1, :]
                    qkv_ref[rows, columns] = projected.astype(jnp.bfloat16)

        lane = pl.multiple_of(pair * (2 * HEAD), 2 * HEAD)
        upper = lax.broadcasted_iota(jnp.int32, (1, 2 * HEAD), 1) >= HEAD
        keys = qkv_ref[:, pl.ds(half + lane, 2 * HEAD)]
        values = qkv_ref[:, pl.ds(2 * half + lane, 2 * HEAD)]
        for block in range(count // BLOCK):
            rows = pl.ds(block * BLOCK, BLOCK)
            queries = qkv_ref[rows, pl.ds(lane, 2 * HEAD)]
            found = []
            for side in range(2):
                chosen = upper if side else jnp.logical_not(upper)
                own = jnp.where(chosen, queries, jnp.zeros_like(queries))
                scores = contract_last(own, keys) * HEAD ** (-0.5) + bias_ref[...]
                lifted = jnp.exp(scores - jnp.max(scores, axis=1, keepdims=True))
                total = jnp.sum(lifted, axis=1, keepdims=True)
                probability = (lifted * (1.0 / total)).astype(jnp.bfloat16)
                prob_ref[side, rows, :] = probability
                found.append(product(probability, values))
            attended = jnp.where(upper, found[1], found[0])
            attended_ref[rows, pl.ds(lane, 2 * HEAD)] = attended.astype(jnp.bfloat16)

        @pl.when(pair == pairs_of_heads - 1)
        def _():
            for strip in range(half // 128):
                start = 3 * half + strip * 128
                spread[strip] = weights_ref[:, start : start + 128].astype(jnp.float32)
                for side in range(2):
                    start = side * half + strip * 128
                    w_out_ref[:, start : start + 128] = spread[
                        strip, pl.ds(side, half, stride=2), :
                    ].astype(jnp.bfloat16)
            partial_ref[...] = product(attended_ref[...], w_out_ref[...]).astype(jnp.bfloat16)

    return pl.pallas_call(
        body,
        grid=(pairs_of_heads,),
        in_specs=[IN_SMEM, fixed(count, width), fixed(6, half), fixed(1, count)] + [ANY] * 4,
        out_specs=[
            fixed(count, 3 * half),
            pl.BlockSpec((2, count, count), lambda h: (h, 0, 0)),
            fixed(count, half),
            fixed(count, width),
            fixed(width, UNIT_WIDTH),
            fixed(half, width),
        ],
        out_shape=[
            shaped((count, 3 * half), jnp.bfloat16),
            shaped((2 * pairs_of_heads, count, count), jnp.bfloat16),
            shaped((count, half), jnp.bfloat16),
            shaped((count, width), jnp.bfloat16),
            shaped((width, UNIT_WIDTH), jnp.bfloat16),
            shaped((half, width), jnp.bfloat16),
        ],
        scratch_shapes=[
            pltpu.VMEM((half // 128, width, 128), jnp.float32),
            pltpu.SemaphoreType.DMA((16,)),
        ],
        compiler_params=params(1),
        cost_estimate=cost(18),
        name="attention_forward",
    )(words, normed, split, column_bias, *pieces)


def mlp_all(words, rows_in, own, other, rep, split, grad_out, pieces_b, pieces_c):
    count, width = rows_in.shape
    half = split.shape[1]
    hidden_width = UNIT_WIDTH
    parts = hidden_width // half

    def body(
        words_ref, rep_ref, split_ref, in_any, own_any, other_any, grad_any,
        b0, b1, b2, b3, c0, c1, c2, c3,
        hidden_sum_ref, grad_sum_ref, middle_any, back_any, second_any,
        sent_b, kept_b, sent_c, kept_c,
        w_first, w_second, rows_ref, own_ref, other_ref, grad_ref, middle_ref, normed_ref,
        active_ref, slope_ref, grad_hidden_ref, back_ref, second_ref, whole_b, whole_c, semaphores,
    ):
        copies = Copies(semaphores)
        first_loads = copies.start(
            [(in_any, rows_ref), (own_any, own_ref), (other_any, other_ref)]
        )
        loads_b = copies.start(chunk_pairs(words_ref, (b0, b1, b2, b3), w_first))
        pairs = [(grad_any, grad_ref)]
        for piece, source in enumerate((c0, c1, c2, c3)):
            for entry in range(4):
                owner = owner_of(words_ref, piece, entry)
                for side in range(2):
                    pairs.append(
                        (
                            source.at[entry, :, pl.ds(side * width, width)],
                            w_second.at[unit_rows(owner * 2 + side), :],
                        )
                    )
        loads_c = copies.start(pairs)
        finish(first_loads)
        for block in range(count // BLOCK):
            rows = pl.ds(block * BLOCK, BLOCK)
            branch = own_ref[rows, :].astype(jnp.float32) + other_ref[rows, :].astype(jnp.float32)
            middle = rows_ref[rows, :].astype(jnp.float32) + branch + rep_ref[4:5, :]
            middle_ref[rows, :] = middle
            unit_signal, _ = norm_parts(middle)
            normed = unit_signal * rep_ref[2:3, :] + rep_ref[3:4, :]
            normed_ref[rows, :] = normed.astype(jnp.bfloat16)
        stores = copies.start([(middle_ref, middle_any)])
        finish(loads_b)
        for part in range(parts):
            columns = slice(part * half, (part + 1) * half)
            hidden = product(normed_ref[...], w_first[:, columns])
            hidden = hidden + split_ref[2 + part : 3 + part, :]
            spread = 0.5 + 0.5 * lax.erf(hidden * 0.7071067811865476)
            active_ref[:, columns] = (hidden * spread).astype(jnp.bfloat16)
            slope = spread + hidden * jnp.exp(-0.5 * hidden * hidden) * 0.3989422804014327
            slope_ref[:, columns] = slope.astype(jnp.bfloat16)
        finish(loads_c)
        second_ref[...] = product(active_ref[...], w_second[...]).astype(jnp.bfloat16)
        stores += copies.start([(second_ref, second_any)])
        grad_sum_ref[...] = jnp.sum(grad_ref[...].astype(jnp.float32), axis=0, keepdims=True)
        for part in range(parts):
            columns = slice(part * half, (part + 1) * half)
            grad_active = contract_last(grad_ref[...], w_second[columns, :])
            grad_hidden = grad_active * slope_ref[:, columns].astype(jnp.float32)
            grad_hidden = grad_hidden.astype(jnp.bfloat16)
            grad_hidden_ref[:, columns] = grad_hidden
            hidden_sum_ref[:, columns] = jnp.sum(
                grad_hidden.astype(jnp.float32), axis=0, keepdims=True
            )
        back_ref[...] = contract_last(grad_hidden_ref[...], w_first[...]).astype(jnp.bfloat16)
        stores += copies.start([(back_ref, back_any)])
        for part in range(parts):
            columns = slice(part * half, (part + 1) * half)
            whole_c[columns, :] = contract_rows(active_ref[:, columns], grad_ref[...]).astype(
                jnp.bfloat16
            )
        for target, owner in unit_targets(words_ref, sent_c, kept_c):
            stores += copies.start(
                [
                    (
                        whole_c.at[unit_rows(owner * 2 + side), :],
                        target.at[:, pl.ds(side * width, width)],
                    )
                    for side in range(2)
                ]
            )
        for part in range(width // half):
            columns = slice(part * half, (part + 1) * half)
            whole_b[columns, :] = contract_rows(normed_ref[:, columns], grad_hidden_ref[...]).astype(
                jnp.bfloat16
            )
        for target, owner in unit_targets(words_ref, sent_b, kept_b):
            stores += copies.start([(whole_b.at[unit_rows(owner), :], target)])
        finish(stores)

    low, full = jnp.bfloat16, jnp.float32
    return pl.pallas_call(
        body,
        in_specs=[IN_SMEM, IN_VMEM, IN_VMEM] + [ANY] * 12,
        out_specs=[IN_VMEM, IN_VMEM] + [ANY] * 7,
        out_shape=[
            shaped((1, hidden_width), full),
            shaped((1, width), full),
            shaped((count, width), full),
            shaped((count, width), low),
            shaped((count, width), low),
        ]
        + unit_shapes()
        + unit_shapes(),
        scratch_shapes=[
            pltpu.VMEM((width, hidden_width), low),
            pltpu.VMEM((hidden_width, width), low),
            pltpu.VMEM((count, width), low),
            pltpu.VMEM((count, width), low),
            pltpu.VMEM((count, width), low),
            pltpu.VMEM((count, width), low),
            pltpu.VMEM((count, width), full),
            pltpu.VMEM((count, width), low),
            pltpu.VMEM((count, hidden_width), low),
            pltpu.VMEM((count, hidden_width), low),
            pltpu.VMEM((count, hidden_width), low),
            pltpu.VMEM((count, width), low),
            pltpu.VMEM((count, width), low),
            pltpu.VMEM((width, hidden_width), low),
            pltpu.VMEM((hidden_width, width), low),
            pltpu.SemaphoreType.DMA((104,)),
        ],
        compiler_params=params(),
        cost_estimate=cost(18),
        name="mlp_all",
    )(words, rep, split, rows_in, own, other, grad_out, *pieces_b, *pieces_c)


def attention_back(
    words, rep, hidden_sum, grad_sum, mask_sum, middle, own, other, grad_out, w_out, attended, qkv,
    prob, normed, weights, rows_in,
):
    count, width = middle.shape
    half = qkv.shape[1] // 3
    span = 3 * half
    pairs_of_heads = half // (2 * HEAD)
    low, full = jnp.bfloat16, jnp.float32

    def body(
        words_ref, rep_ref, hidden_sum_ref, grad_sum_ref, mask_sum_ref,
        middle_any, own_any, other_any, grad_any, w_out_any, attended_any, qkv_any, prob_any,
        normed_any, weights_any, in_any,
        grad_middle_any, back_any, sent, kept,
        middle_ref, own_ref, other_ref, grad_ref, w_out_ref, attended_ref, qkv_ref, prob_ref,
        normed_ref, weights_ref, in_ref, grad_middle_ref, back_ref, branch, grad_attended,
        grad_qkv, spread, whole, vectors, low_vectors, semaphores,
    ):
        copies = Copies(semaphores)
        early = copies.start(
            [
                (middle_any, middle_ref), (own_any, own_ref), (other_any, other_ref),
                (grad_any, grad_ref),
            ]
        )
        outer = copies.start([(w_out_any, w_out_ref), (attended_any, attended_ref)])
        inner = copies.start([(qkv_any, qkv_ref)])
        probs = copies.start(
            [(prob_any.at[pl.ds(2 * pair, 2)], prob_ref.at[pair]) for pair in range(2)]
        )
        late = copies.start(
            [(normed_any, normed_ref), (weights_any, weights_ref), (in_any, in_ref)]
        )
        vectors[...] = jnp.zeros_like(vectors)
        finish(early)
        for block in range(count // BLOCK):
            rows = pl.ds(block * BLOCK, BLOCK)
            unit_signal, scale = norm_parts(middle_ref[rows, :])
            mine = own_ref[rows, :].astype(full)
            grad_normed = mine + other_ref[rows, :].astype(full)
            grad_middle = grad_ref[rows, :].astype(full) + norm_back(
                grad_normed, unit_signal, scale, rep_ref[2:3, :]
            )
            grad_middle_ref[rows, :] = grad_middle
            grad_branch = grad_middle.astype(low)
            branch[rows, :] = grad_branch
            vectors[1:2, :width] += jnp.sum(mine * unit_signal, axis=0, keepdims=True)
            vectors[1:2, width:] += jnp.sum(mine, axis=0, keepdims=True)
            vectors[2:3, :width] += 0.5 * jnp.sum(grad_branch.astype(full), axis=0, keepdims=True)
        stores = copies.start([(grad_middle_ref, grad_middle_any)])
        finish(outer)
        grad_attended[...] = contract_last(branch[...], w_out_ref[...]).astype(low)
        out_gradient = contract_rows(attended_ref[...], branch[...])
        for strip in range(half // 128):
            for side in range(2):
                start = side * half + strip * 128
                spread[strip, pl.ds(side, half, stride=2), :] = out_gradient[
                    :, start : start + 128
                ]
            start = span + strip * 128
            whole[:, start : start + 128] = spread[strip].astype(low)
        finish(inner)
        upper = lax.broadcasted_iota(jnp.int32, (1, 2 * HEAD), 1) >= HEAD
        for pair in range(pairs_of_heads):
            finish(probs[:1])
            probs = probs[1:]
            lanes = [slice(part * half + pair * 128, part * half + pair * 128 + 128) for part in range(3)]
            queries, keys, values = (qkv_ref[:, lane] for lane in lanes)
            grad = grad_attended[:, lanes[0]]
            found = []
            for side in range(2):
                chosen = upper if side else jnp.logical_not(upper)
                own_grad = jnp.where(chosen, grad, jnp.zeros_like(grad))
                low_probability = prob_ref[pair % 2, side]
                probability = low_probability.astype(full)
                weighted = probability * contract_last(own_grad, values)
                inner_sum = jnp.sum(weighted, axis=1, keepdims=True)
                grad_scores = (weighted - probability * inner_sum).astype(low)
                found.append(
                    (
                        product(grad_scores, keys),
                        contract_rows(queries, grad_scores)[side * HEAD : (side + 1) * HEAD],
                        contract_rows(grad, low_probability)[side * HEAD : (side + 1) * HEAD],
                    )
                )
            if pair + 2 < pairs_of_heads:
                probs += copies.start(
                    [(prob_any.at[pl.ds(2 * pair + 4, 2)], prob_ref.at[pair % 2])]
                )
            backs = (
                jnp.where(upper, found[1][0], found[0][0]) * HEAD ** (-0.5),
                jnp.transpose(jnp.concatenate([found[0][1], found[1][1]])) * HEAD ** (-0.5),
                jnp.transpose(jnp.concatenate([found[0][2], found[1][2]])),
            )
            for lane, value in zip(lanes, backs):
                grad_qkv[:, lane] = value.astype(low)
        finish(late)
        for part in range(width // half):
            columns = slice(part * half, (part + 1) * half)
            whole[columns, :span] = contract_rows(normed_ref[:, columns], grad_qkv[...]).astype(low)
        for target, owner in unit_targets(words_ref, sent, kept):
            stores += copies.start([(whole.at[unit_rows(owner), :], target)])
        for block in range(count // BLOCK):
            rows = pl.ds(block * BLOCK, BLOCK)
            back = contract_last(grad_qkv[rows, :], weights_ref[:, :span])
            back_ref[rows, :] = back.astype(low)
            unit_signal, _ = norm_parts(in_ref[rows, :].astype(full))
            vectors[0:1, :width] += jnp.sum(back * unit_signal, axis=0, keepdims=True)
            vectors[0:1, width:] += jnp.sum(back, axis=0, keepdims=True)
            for place, part in enumerate((0, 2)):
                sums = jnp.sum(
                    grad_qkv[rows, part * half : (part + 1) * half].astype(full),
                    axis=0,
                    keepdims=True,
                )
                vectors[3:4, place * half : (place + 1) * half] += sums
        stores += copies.start([(back_ref, back_any)])
        vectors[2:3, width:] = 0.5 * grad_sum_ref[...]
        vectors[3:4, 2 * half : span] = mask_sum_ref[...]
        vectors[4:5, :] = hidden_sum_ref[...]
        low_vectors[...] = vectors[...].astype(low)
        last = pl.ds(8 * UNIT_ROWS, 16)
        stores += copies.start([(low_vectors, sent.at[last, :]), (low_vectors, kept.at[last, :])])
        finish(stores)

    return pl.pallas_call(
        body,
        in_specs=[IN_SMEM] + [IN_VMEM] * 4 + [ANY] * 11,
        out_specs=[ANY] * 4,
        out_shape=[shaped((count, width), full), shaped((count, width), low)] + unit_shapes(16),
        scratch_shapes=[
            pltpu.VMEM((count, width), full),
            pltpu.VMEM((count, width), low),
            pltpu.VMEM((count, width), low),
            pltpu.VMEM((count, width), low),
            pltpu.VMEM((half, width), low),
            pltpu.VMEM((count, half), low),
            pltpu.VMEM((count, span), low),
            pltpu.VMEM((2, 2, count, count), low),
            pltpu.VMEM((count, width), low),
            pltpu.VMEM((width, UNIT_WIDTH), low),
            pltpu.VMEM((count, width), low),
            pltpu.VMEM((count, width), full),
            pltpu.VMEM((count, width), low),
            pltpu.VMEM((count, width), low),
            pltpu.VMEM((count, half), low),
            pltpu.VMEM((count, span), low),
            pltpu.VMEM((half // 128, width, 128), full),
            pltpu.VMEM((width, UNIT_WIDTH), low),
            pltpu.VMEM((16, UNIT_WIDTH), full),
            pltpu.VMEM((16, UNIT_WIDTH), low),
            pltpu.SemaphoreType.DMA((40,)),
        ],
        compiler_params=params(),
        cost_estimate=cost(22),
        name="attention_back",
    )(
        words, rep, hidden_sum, grad_sum, mask_sum, middle, own, other, grad_out, w_out, attended,
        qkv, prob, normed, weights, rows_in,
    )


def input_gradient(rows_in, own, other, grad_middle, rep):
    count, width = rows_in.shape

    def body(in_ref, own_ref, other_ref, middle_ref, rep_ref, out_ref):
        unit_signal, scale = norm_parts(in_ref[...].astype(jnp.float32))
        grad = own_ref[...].astype(jnp.float32) + other_ref[...].astype(jnp.float32)
        out_ref[...] = middle_ref[...] + norm_back(grad, unit_signal, scale, rep_ref[0:1, :])

    block = pl.BlockSpec((BLOCK, width), lambda i: (i, 0))
    return pl.pallas_call(
        body,
        grid=(count // BLOCK,),
        in_specs=[block, block, block, block, pl.BlockSpec(rep.shape, lambda i: (0, 0))],
        out_specs=block,
        out_shape=shaped((count, width), jnp.float32),
        compiler_params=params(1),
        cost_estimate=cost(5.7),
        name="input_gradient",
    )(rows_in, own, other, grad_middle, rep)


def adam_unit(units, states, strides):
    flat = [array.reshape(-1, 128) for state in states for array in state]
    terms = [array for unit in units for array in unit]
    counts = [len(unit) for unit in units]

    def body(*refs):
        terms_here, refs = refs[: len(terms)], refs[len(terms) :]
        inputs, outputs = refs[: len(flat)], refs[len(flat) :]
        for unit, column, state, start, step in strides:
            columns = slice(column * 128, (column + 1) * 128)
            skip = sum(counts[:unit])
            gradient = terms_here[skip][:, columns].astype(jnp.float32)
            for term in terms_here[skip + 1 : skip + counts[unit]]:
                gradient = gradient + term[:, columns].astype(jnp.float32)
            rows = pl.ds(start, UNIT_ROWS, stride=step)
            weight, one, two = (inputs[3 * state + i][rows, :] for i in range(3))
            updated = adam_step(weight, one, two, gradient, MATRIX_RATE, MATRIX_DECAY)
            for i in range(3):
                outputs[3 * state + i][rows, :] = updated[i]

    whole = [pl.BlockSpec(array.shape, lambda i: (0, 0)) for array in flat]
    results = pl.pallas_call(
        body,
        grid=(1,),
        in_specs=[
            pl.BlockSpec((UNIT_ROWS, term.shape[1]), lambda i: (0, 0)) for term in terms
        ]
        + whole,
        out_specs=whole,
        out_shape=[shaped(array.shape, jnp.float32) for array in flat],
        compiler_params=params(1),
        cost_estimate=cost(2.5),
        name="adam_unit",
    )(*terms, *flat)
    return [array.reshape(1, -1) for array in results]


def on_device(
    patch_rows,
    cotangent,
    mask_token,
    lengths,
    masked,
    dealing,
    qkv_master,
    qkv_first,
    qkv_second,
    out_master,
    out_first,
    out_second,
    fc1_master,
    fc1_first,
    fc1_second,
    fc2_master,
    fc2_first,
    fc2_second,
    rep_master,
    rep_first,
    rep_second,
    split_master,
    split_first,
    split_second,
):
    slot_count, capacity, feature_width = patch_rows.shape
    half_width = mask_token.shape[0]
    dp_count = lax.axis_size("dp")
    member = lax.axis_index("dp")
    core_index = lax.axis_index("mp")
    positions_here = cotangent.shape[1]
    position_span = positions_here * dp_count
    heads_here = half_width // HEAD
    row_count = slot_count * capacity
    strip_count = lengths.shape[0]
    position_rows = -(-positions_here // 4) * 4
    held_count = strip_count * positions_here
    dealt_count = strip_count * position_rows
    words = jnp.stack([member, 1 + core_index, 2 - core_index, core_index]).astype(jnp.int32)

    inputs = patch_rows.reshape(row_count, feature_width)
    split_rows = split_master[0]
    unit_a, unit_b, unit_c = pack_units(qkv_master, out_master, fc1_master, fc2_master)

    patch_index = jnp.arange(PATCHES, dtype=jnp.int32)
    visible_all = (patch_index[None, :] < lengths[:, None]) & (masked == 0)
    strips_here = lax.dynamic_slice_in_dim(dealing, member * slot_count, slot_count)
    visible_here = visible_all[strips_here]
    rank_here = jnp.cumsum(visible_here.astype(jnp.int32), axis=1) - 1
    counts_here = jnp.sum(visible_here.astype(jnp.int32), axis=1)
    valid_rows = jnp.arange(capacity, dtype=jnp.int32)[None, :] < counts_here[:, None]
    column_bias = jnp.where(valid_rows, 0.0, -1e30).astype(jnp.float32).reshape(1, row_count)
    padding = position_span - PATCHES
    visible_padded = jnp.pad(visible_here, ((0, 0), (0, padding)))
    rank_padded = jnp.pad(jnp.maximum(rank_here, 0), ((0, 0), (0, padding)))
    own_positions = jnp.arange(positions_here, dtype=jnp.int32) * dp_count + member
    inside = own_positions < PATCHES
    visible_own = visible_all[:, jnp.minimum(own_positions, PATCHES - 1)] & inside[None, :]
    row_time = jnp.arange(position_rows, dtype=jnp.int32)[None, :]
    strip_row = jnp.where(
        row_time < positions_here, row_time * strip_count + dealing[:, None], -1
    ).reshape(dealt_count)
    deal = (
        strip_row[:, None] == jnp.arange(held_count, dtype=jnp.int32)[None, :]
    ).astype(jnp.bfloat16)
    encoder_row = jnp.where(
        visible_padded,
        rank_padded + jnp.arange(slot_count, dtype=jnp.int32)[:, None] * capacity,
        -1,
    )
    encoder_row = jnp.transpose(
        encoder_row.reshape(slot_count, positions_here, dp_count), (2, 0, 1)
    )
    encoder_row = jnp.pad(
        encoder_row, ((0, 0), (0, 0), (0, position_rows - positions_here)), constant_values=-1
    ).reshape(dealt_count)
    pick = (
        jnp.arange(row_count, dtype=jnp.int32)[:, None] == encoder_row[None, :]
    ).astype(jnp.bfloat16)
    unseen = jnp.transpose(jnp.logical_not(visible_own) & inside[None, :]).reshape(held_count)

    cotangent_rows = jnp.transpose(
        cotangent.reshape(strip_count, positions_here, half_width), (1, 0, 2)
    ).reshape(held_count, half_width)

    def spread_out(array):
        return hop_by_core(array, 1, 2, dp_count), hop_by_core(array, 2, 1, dp_count)

    def exchanged(array):
        array = array.reshape(dp_count, slot_count * position_rows, half_width)
        array = lax.all_to_all(array, "dp", split_axis=0, concat_axis=0, tiled=True)
        return array.reshape(dealt_count, half_width)

    def columns_of(unit):
        return [hop(unit, distance, dp_count) for distance in Z_ORDER[1:]]

    column_a = columns_of(unit_a)
    normed = first_norm(inputs, rep_master)
    column_a, normed, unit_b, unit_c, cotangent_rows, deal, unseen = together(
        column_a, normed, unit_b, unit_c, cotangent_rows, deal, unseen
    )

    column_a = join_chunks([unit_a, *column_a])
    first_a, second_a = spread_out(column_a)
    column_b = columns_of(unit_b)
    dealt = product(deal, cotangent_rows).astype(jnp.bfloat16)
    mask_sum = product(unseen.astype(jnp.bfloat16)[None, :], cotangent_rows)
    first_a, second_a, column_b, dealt, mask_sum, column_bias, pick = together(
        first_a, second_a, column_b, dealt, mask_sum, column_bias, pick
    )

    third_a = hop_by_core(first_a, 2, 1, dp_count)
    column_c = columns_of(unit_c)
    returned = exchanged(dealt)
    column_b = join_chunks([unit_b, *column_b])
    third_a, column_c, normed, column_b = together(third_a, column_c, normed, column_b)

    first_b, second_b = spread_out(column_b)
    column_c = join_chunks([unit_c, *column_c])
    first_c, second_c = spread_out(column_c)
    qkv, prob, attended, branch, weights_a, w_output = attention_forward(
        words, normed, split_rows, column_bias, (column_a, first_a, second_a, third_a)
    )
    first_b, second_b, first_c, second_c = together(first_b, second_b, first_c, second_c)

    third_b = hop_by_core(first_b, 2, 1, dp_count)
    third_c = hop_by_core(first_c, 2, 1, dp_count)
    branch_other = swap_cores(branch)
    gathered = product(pick, returned).astype(jnp.bfloat16)
    gathered_other = swap_cores(gathered)
    grad_out = jnp.where(
        core_index == 0,
        jnp.concatenate([gathered, gathered_other], axis=1),
        jnp.concatenate([gathered_other, gathered], axis=1),
    )
    third_b, third_c, branch_other, grad_out = together(third_b, third_c, branch_other, grad_out)

    hidden_sum, grad_sum, middle, back_two, second, sent_b, kept_b, sent_c, kept_c = mlp_all(
        words, inputs, branch, branch_other, rep_master, split_rows, grad_out,
        (column_b, first_b, second_b, third_b), (column_c, first_c, second_c, third_c),
    )
    middle, back_two, second, sent_b, kept_b, sent_c, kept_c = together(
        middle, back_two, second, sent_b, kept_b, sent_c, kept_c
    )

    one_c = hop_by_core(sent_c, 2, 1, dp_count)
    back_two_other = swap_cores(back_two)
    second_other = swap_cores(second)
    total = second.astype(jnp.float32) + second_other.astype(jnp.float32) + rep_master[5]
    result = (middle + total).astype(jnp.bfloat16)
    result_half = lax.dynamic_slice_in_dim(result, core_index * half_width, half_width, 1)
    outgoing = contract_rows(pick, result_half).astype(jnp.bfloat16)
    one_c, back_two_other, outgoing = together(one_c, back_two_other, outgoing)

    half_unit, quarter, eighth = 4 * UNIT_ROWS, 2 * UNIT_ROWS, UNIT_ROWS
    one_b = hop_by_core(sent_b, 2, 1, dp_count)
    two_c = hop_by_core(
        added(half_unit, 2 * half_unit, (kept_c, 0), (one_c, 0)), 1, 2, dp_count
    )
    arrived = exchanged(outgoing)
    grad_middle, back_one, sent_a, kept_a = attention_back(
        words, rep_master, hidden_sum, grad_sum, mask_sum, middle, back_two, back_two_other,
        grad_out, w_output, attended, qkv, prob, normed, weights_a, inputs,
    )
    two_c, one_b, back_one, sent_a, kept_a, arrived = together(
        two_c, one_b, back_one, sent_a, kept_a, arrived
    )

    one_a = hop_by_core(sent_a, 2, 1, dp_count)
    back_one_other = swap_cores(back_one)
    two_b = hop_by_core(
        added(half_unit, 2 * half_unit, (kept_b, 0), (one_b, 0)), 1, 2, dp_count
    )
    three_c = hop(
        added(quarter, half_unit, (kept_c, 0), (one_c, 0), (two_c, 0)), 4, dp_count
    )
    full_out = contract_rows(deal, arrived)
    full_out = jnp.where(unseen[:, None], mask_token.astype(jnp.float32)[None, :], full_out)
    full_out = full_out.astype(jnp.bfloat16)
    one_a, three_c, two_b, back_one_other, full_out = together(
        one_a, three_c, two_b, back_one_other, full_out
    )

    two_a_sent = added(half_unit, 2 * half_unit + 16, (kept_a, 0), (one_a, 0))
    two_a = hop_by_core(two_a_sent, 1, 2, dp_count)
    three_b = hop(
        added(quarter, half_unit, (kept_b, 0), (one_b, 0), (two_b, 0)), 4, dp_count
    )
    four_c = hop(
        added(eighth, quarter, (kept_c, 0), (one_c, 0), (two_c, 0), (three_c, 0)), 12, dp_count
    )
    input_grad = input_gradient(inputs, back_one, back_one_other, grad_middle, rep_master)
    two_a_sent, two_a, four_c, three_b, input_grad = together(
        two_a_sent, two_a, four_c, three_b, input_grad
    )

    messages = last_messages(kept_a, one_a, two_a, two_a_sent)
    arrivals = [hop(message, k, dp_count) for message, k in zip(messages, Z_ORDER[1:])]
    four_b = hop(
        added(eighth, quarter, (kept_b, 0), (one_b, 0), (two_b, 0), (three_b, 0)), 12, dp_count
    )
    fc2_new = adam_unit(
        [(kept_c, one_c, two_c, three_c, four_c)],
        [(fc2_master, fc2_first, fc2_second)],
        [(0, side * 6 + j, 0, side * UNIT_ROWS * 6 + j, 6) for side in range(2) for j in range(6)],
    )
    arrivals, four_b, message, *fc2_new = together(arrivals, four_b, messages[0], *fc2_new)

    fc1_new = adam_unit(
        [(kept_b, one_b, two_b, three_b, four_b)],
        [(fc1_master, fc1_first, fc1_second)],
        [(0, j, 0, j, 12) for j in range(12)],
    )
    vectors = [array[eighth:].astype(jnp.float32) for array in (message, *arrivals)]
    vectors = (vectors[0] + vectors[1]) + (vectors[2] + vectors[3])
    rep_total = (vectors[:3] + swap_cores(vectors[:3])).reshape(rep_master.shape)
    split_total = jnp.concatenate(
        [vectors[3, : 2 * half_width], vectors[4]]
    ).reshape(split_master.shape)
    mask_total = vectors[3, 2 * half_width : 3 * half_width]
    qkv_out_new = adam_unit(
        [(kept_a, one_a, two_a, *arrivals)],
        [(qkv_master, qkv_first, qkv_second), (out_master, out_first, out_second)],
        [(0, j, 0, j, 9) for j in range(9)] + [(0, 9 + j, 1, j, 3) for j in range(3)],
    )
    full_out = full_out.reshape(positions_here, strip_count, half_width)
    full_out = jnp.transpose(full_out, (1, 0, 2))[:, :, None, :]
    input_grad = input_grad.reshape(slot_count, capacity, feature_width)
    rep_new = adam_step(rep_master, rep_first, rep_second, rep_total, VECTOR_RATE, 0.0)
    split_new = adam_step(split_master, split_first, split_second, split_total, VECTOR_RATE, 0.0)
    return (
        full_out,
        input_grad,
        mask_total,
        *qkv_out_new,
        *fc1_new,
        *fc2_new,
        *rep_new,
        *split_new,
    )


def solution(mesh):
    placed = (
        P("dp", None, None),
        P(None, None, "dp", "mp"),
        P("mp"),
        P(),
        P(),
        P(),
        P("mp", "dp"),
        P("mp", "dp"),
        P("mp", "dp"),
        P("mp", "dp"),
        P("mp", "dp"),
        P("mp", "dp"),
        P("mp", "dp"),
        P("mp", "dp"),
        P("mp", "dp"),
        P("mp", "dp"),
        P("mp", "dp"),
        P("mp", "dp"),
        P(),
        P(),
        P(),
        P("mp", None, None),
        P("mp", None, None),
        P("mp", None, None),
    )
    tuned = mesh.shape["dp"] == 16 and mesh.shape["mp"] == 2
    return jax.shard_map(
        on_device if tuned else on_device_general,
        mesh=mesh,
        in_specs=placed,
        out_specs=(
            P(None, None, "dp", "mp"),
            P("dp", None, None),
            P("mp"),
            P("mp", "dp"),
            P("mp", "dp"),
            P("mp", "dp"),
            P("mp", "dp"),
            P("mp", "dp"),
            P("mp", "dp"),
            P("mp", "dp"),
            P("mp", "dp"),
            P("mp", "dp"),
            P("mp", "dp"),
            P("mp", "dp"),
            P("mp", "dp"),
            P(),
            P(),
            P(),
            P("mp", None, None),
            P("mp", None, None),
            P("mp", None, None),
        ),
        check_vma=False,
    )
```

```python
import jax
import jax.numpy as jnp
from jax import lax
from jax.experimental import pallas as pl
from jax.experimental.pallas import tpu as pltpu
from jax.sharding import PartitionSpec as P

HEAD = 64
PATCHES = 529
STEP = 10


NORM_EPS = 1e-06
BETA_ONE = 0.9
BETA_TWO = 0.999
ADAM_EPS = 1e-08
MATRIX_RATE = 0.15
MATRIX_DECAY = 0.05
VECTOR_RATE = 0.6


def layer_norm(signal, norm_gain, norm_shift):
    average = jnp.mean(signal, axis=-1, keepdims=True)
    centered = signal - average
    spread = jnp.mean(centered * centered, axis=-1, keepdims=True)
    return centered * lax.rsqrt(spread + NORM_EPS) * norm_gain + norm_shift


def exact_gelu(signal):
    return jax.nn.gelu(signal, approximate=False)


def product(left, right):
    return jnp.dot(left, right, preferred_element_type=jnp.float32)


def contract_last(left, right):
    return lax.dot_general(
        left, right, (((1,), (1,)), ((), ())), preferred_element_type=jnp.float32
    )


def contract_rows(left, right):
    return lax.dot_general(
        left, right, (((0,), (0,)), ((), ())), preferred_element_type=jnp.float32
    )


def adam_step(weight, moment_one, moment_two, gradient, step_rate, decay_rate):
    one_new = BETA_ONE * moment_one + (1.0 - BETA_ONE) * gradient
    two_new = BETA_TWO * moment_two + (1.0 - BETA_TWO) * gradient * gradient
    one_hat = one_new / (1.0 - BETA_ONE**STEP)
    two_hat = two_new / (1.0 - BETA_TWO**STEP)
    weight_new = weight - step_rate * (
        one_hat / (jnp.sqrt(two_hat) + ADAM_EPS) + decay_rate * weight
    )
    return (weight_new, one_new, two_new)


def total_over_cores(partial):
    return partial.astype(jnp.float32) + swap_cores(partial).astype(jnp.float32)


def pair_scores(queries, key_rows, valid_rows):
    scores = jnp.einsum(
        "qhd,khd->hqk", queries, key_rows, preferred_element_type=jnp.float32
    ) * HEAD ** (-0.5)
    return jnp.where(valid_rows[None, None, :], scores, -1e30)


def attend_pair(pair_block):
    queries, key_rows, value_rows, valid_rows = pair_block
    scores = pair_scores(queries, key_rows, valid_rows)
    row_max = jnp.max(scores, axis=2, keepdims=True)
    lifted = jnp.exp(scores - row_max)
    row_total = jnp.sum(lifted, axis=2, keepdims=True)
    probability = (lifted / row_total).astype(jnp.bfloat16)
    attended = jnp.einsum(
        "hqk,khd->qhd", probability, value_rows, preferred_element_type=jnp.float32
    )
    return (attended.astype(jnp.bfloat16), row_max[:, :, 0] + jnp.log(row_total[:, :, 0]))


def attend_pair_back(pair_block):
    queries, key_rows, value_rows, valid_rows, log_total, grad_attended = pair_block
    scores = pair_scores(queries, key_rows, valid_rows)
    probability = jnp.exp(scores - log_total[:, :, None])
    grad_prob = jnp.einsum(
        "qhd,khd->hqk", grad_attended, value_rows, preferred_element_type=jnp.float32
    )
    inner_sum = jnp.sum(probability * grad_prob, axis=2, keepdims=True)
    grad_scores = (probability * (grad_prob - inner_sum)).astype(jnp.bfloat16)
    score_scale = HEAD ** (-0.5)
    grad_queries = (
        jnp.einsum("hqk,khd->qhd", grad_scores, key_rows, preferred_element_type=jnp.float32)
        * score_scale
    )
    grad_keys = (
        jnp.einsum("hqk,qhd->khd", grad_scores, queries, preferred_element_type=jnp.float32)
        * score_scale
    )
    grad_values = jnp.einsum(
        "hqk,qhd->khd",
        probability.astype(jnp.bfloat16),
        grad_attended,
        preferred_element_type=jnp.float32,
    )
    return (
        grad_queries.astype(jnp.bfloat16),
        grad_keys.astype(jnp.bfloat16),
        grad_values.astype(jnp.bfloat16),
    )


def hop(array, distance, axis_count):
    return lax.ppermute(array, "dp", [(i, i ^ distance) for i in range(axis_count)])


def swap_cores(array):
    return lax.ppermute(array, "mp", [(0, 1), (1, 0)])


def place_chunks(pieces, chunk_ids, member, count):
    rows, width = pieces[0].shape[1:]

    def body(member_ref, *refs):
        sources, target, semaphores = refs[:-2], refs[-2], refs[-1]
        copies = []
        for source, ids in zip(sources, chunk_ids):
            for place, distance in enumerate(ids):
                copies.append(
                    pltpu.make_async_copy(
                        source.at[place],
                        target.at[member_ref[0] ^ distance],
                        semaphores.at[len(copies)],
                    )
                )
        for copy in copies:
            copy.start()
        for copy in copies:
            copy.wait()

    return pl.pallas_call(
        body,
        in_specs=[pl.BlockSpec(memory_space=pltpu.SMEM)]
        + [pl.BlockSpec(memory_space=pl.ANY)] * len(pieces),
        out_specs=pl.BlockSpec(memory_space=pltpu.VMEM),
        out_shape=jax.ShapeDtypeStruct((count, rows, width), pieces[0].dtype),
        scratch_shapes=[pltpu.SemaphoreType.DMA((count,))],
        cost_estimate=pl.CostEstimate(
            flops=0, transcendentals=0, bytes_accessed=4 * count * rows * width
        ),
        name="place_chunks",
    )(member, *pieces)


def pick_chunks(whole, chunk_ids, member):
    count, rows, width = whole.shape

    def body(member_ref, source, *refs):
        targets, semaphores = refs[:-1], refs[-1]
        copies = []
        for target, ids in zip(targets, chunk_ids):
            for place, distance in enumerate(ids):
                copies.append(
                    pltpu.make_async_copy(
                        source.at[member_ref[0] ^ distance],
                        target.at[place],
                        semaphores.at[len(copies)],
                    )
                )
        for copy in copies:
            copy.start()
        for copy in copies:
            copy.wait()

    return pl.pallas_call(
        body,
        in_specs=[pl.BlockSpec(memory_space=pltpu.SMEM), pl.BlockSpec(memory_space=pltpu.VMEM)],
        out_specs=[pl.BlockSpec(memory_space=pl.ANY)] * len(chunk_ids),
        out_shape=[
            jax.ShapeDtypeStruct((len(ids), rows, width), whole.dtype) for ids in chunk_ids
        ],
        scratch_shapes=[pltpu.SemaphoreType.DMA((count,))],
        cost_estimate=pl.CostEstimate(
            flops=0, transcendentals=0, bytes_accessed=4 * count * rows * width
        ),
        name="pick_chunks",
    )(member, whole)


def gather_chunks(chunk, member, count):
    own = chunk[None]
    if count == 16:
        near, far, last = (hop(own, k, count) for k in (4, 8, 12))
        first, second = jnp.concatenate([own, near]), jnp.concatenate([far, last])
        x_first, x_second = hop(first, 1, count), hop(second, 1, count)
        y_first, y_second = hop(first, 2, count), hop(second, 2, count)
        d_first, d_second = hop(y_first, 1, count), hop(x_second, 2, count)
        pieces = [first, second, x_first, x_second, y_first, y_second, d_first, d_second]
        ids = [(0, 4), (8, 12), (1, 5), (9, 13), (2, 6), (10, 14), (3, 7), (11, 15)]
    else:
        held, step = own, 1
        while step < count:
            held = jnp.concatenate([held, hop(held, step, count)])
            step *= 2
        pieces, ids = [held], [tuple(range(count))]
    return place_chunks(pieces, ids, member, count)


def scatter_chunks(whole, member, count):
    def wide(array):
        return array.astype(jnp.float32)

    if count == 16:
        ids = [(3, 7), (11, 15), (2, 6), (9, 13), (10, 14), (1, 5), (0, 4), (8, 12)]
        d_first, d_second, y_first, x_second, y_second, x_first, first, second = pick_chunks(
            whole, ids, member
        )
        d_first, d_second = hop(d_first, 1, count), hop(d_second, 2, count)
        y_second, x_first = hop(y_second, 2, count), hop(x_first, 1, count)
        y_first = hop((wide(y_first) + wide(d_first)).astype(jnp.bfloat16), 2, count)
        x_second = hop((wide(x_second) + wide(d_second)).astype(jnp.bfloat16), 1, count)
        first = wide(first) + wide(y_first) + wide(x_first)
        second = wide(second) + wide(y_second) + wide(x_second)
        near = hop(first[1].astype(jnp.bfloat16), 4, count)
        far = hop(second[0].astype(jnp.bfloat16), 8, count)
        last = hop(second[1].astype(jnp.bfloat16), 12, count)
        return first[0] + wide(near) + wide(far) + wide(last)
    (held,) = pick_chunks(whole, [tuple(range(count))], member)
    held = wide(held)
    step = count // 2
    while step:
        held = held[:step] + wide(hop(held[step:].astype(jnp.bfloat16), step, count))
        step //= 2
    return held[0]


def sum_over_dp(vector, count):
    if count == 16:
        for low, high in ((1, 2), (4, 8)):
            other, third, fourth = (hop(vector, k, count) for k in (low, high, low + high))
            vector = (vector + other) + (third + fourth)
        return vector
    step = 1
    while step < count:
        vector = vector + hop(vector, step, count)
        step *= 2
    return vector


def on_device_general(
    patch_rows,
    cotangent,
    mask_token,
    lengths,
    masked,
    dealing,
    qkv_master,
    qkv_first,
    qkv_second,
    out_master,
    out_first,
    out_second,
    fc1_master,
    fc1_first,
    fc1_second,
    fc2_master,
    fc2_first,
    fc2_second,
    rep_master,
    rep_first,
    rep_second,
    split_master,
    split_first,
    split_second,
):
    slot_count, capacity, feature_width = patch_rows.shape
    half_width = mask_token.shape[0]
    dp_count = lax.axis_size("dp")
    member = lax.axis_index("dp")
    core_index = lax.axis_index("mp")
    positions_here = cotangent.shape[1]
    position_span = positions_here * dp_count
    heads_here = half_width // HEAD
    hidden_width = (split_master.shape[1] - 2) * half_width
    row_count = slot_count * capacity
    pair_count = slot_count // 2
    pair_length = 2 * capacity
    patch_index = jnp.arange(PATCHES, dtype=jnp.int32)
    visible_all = (patch_index[None, :] < lengths[:, None]) & (masked == 0)
    strips_here = lax.dynamic_slice_in_dim(dealing, member * slot_count, slot_count)
    visible_here = visible_all[strips_here]
    rank_here = jnp.cumsum(visible_here.astype(jnp.int32), axis=1) - 1
    counts_here = jnp.sum(visible_here.astype(jnp.int32), axis=1)
    valid_rows = jnp.arange(capacity, dtype=jnp.int32)[None, :] < counts_here[:, None]
    padding = position_span - PATCHES
    visible_padded = jnp.pad(visible_here, ((0, 0), (0, padding)))
    rank_padded = jnp.pad(jnp.maximum(rank_here, 0), ((0, 0), (0, padding)))
    own_positions = jnp.arange(positions_here, dtype=jnp.int32) * dp_count + member
    inside = own_positions < PATCHES
    visible_own = visible_all[:, jnp.minimum(own_positions, PATCHES - 1)] & inside[None, :]
    strip_count = lengths.shape[0]
    held_count = strip_count * positions_here
    strip_row = (
        jnp.arange(positions_here, dtype=jnp.int32)[None, :] * strip_count + dealing[:, None]
    ).reshape(held_count)
    deal = (
        strip_row[:, None] == jnp.arange(held_count, dtype=jnp.int32)[None, :]
    ).astype(jnp.bfloat16)
    encoder_row = jnp.where(
        visible_padded,
        rank_padded + jnp.arange(slot_count, dtype=jnp.int32)[:, None] * capacity,
        -1,
    )
    encoder_row = jnp.transpose(
        encoder_row.reshape(slot_count, positions_here, dp_count), (2, 0, 1)
    ).reshape(held_count)
    pick = (
        jnp.arange(row_count, dtype=jnp.int32)[:, None] == encoder_row[None, :]
    ).astype(jnp.bfloat16)
    unseen = jnp.transpose(jnp.logical_not(visible_own) & inside[None, :]).reshape(held_count)
    member_word = member.astype(jnp.int32).reshape(1)

    cotangent_rows = jnp.transpose(cotangent.reshape(strip_count, positions_here, half_width), (1, 0, 2))
    cotangent_rows = cotangent_rows.reshape(held_count, half_width)
    dealt = product(deal, cotangent_rows).astype(jnp.bfloat16)
    returned = lax.all_to_all(
        dealt.reshape(dp_count, slot_count * positions_here, half_width),
        "dp",
        split_axis=0,
        concat_axis=0,
        tiled=True,
    ).reshape(held_count, half_width)
    gathered = product(pick, returned).astype(jnp.bfloat16)
    gathered_other = swap_cores(gathered)
    grad_out = jnp.where(
        core_index == 0,
        jnp.concatenate([gathered, gathered_other], axis=1),
        jnp.concatenate([gathered_other, gathered], axis=1),
    )
    mask_grad = product(unseen.astype(jnp.bfloat16)[None, :], cotangent_rows)[0]

    def gathered_matrix(master, rows, width):
        chunk = master.astype(jnp.bfloat16).reshape(rows // dp_count, width)
        return gather_chunks(chunk, member_word, dp_count).reshape(rows, width)

    w_attention = gathered_matrix(qkv_master, feature_width, 3 * half_width)
    w_output = gathered_matrix(out_master, half_width, feature_width)
    w_first = gathered_matrix(fc1_master, feature_width, hidden_width)
    w_second = gathered_matrix(fc2_master, hidden_width, feature_width)
    inputs = patch_rows.reshape(row_count, feature_width).astype(jnp.float32)
    normed_full, norm_back_one = jax.vjp(layer_norm, inputs, rep_master[0], rep_master[1])
    normed = normed_full.astype(jnp.bfloat16)
    projected = product(normed, w_attention).reshape(row_count, 3, half_width)
    queries = (projected[:, 0] + split_master[0, 0]).astype(jnp.bfloat16)
    key_rows = projected[:, 1].astype(jnp.bfloat16)
    value_rows = (projected[:, 2] + split_master[0, 1]).astype(jnp.bfloat16)

    def by_pair(array):
        return array.reshape(pair_count, pair_length, heads_here, HEAD)

    pair_valid = valid_rows.reshape(pair_count, pair_length)
    attended, log_total = lax.map(
        attend_pair, (by_pair(queries), by_pair(key_rows), by_pair(value_rows), pair_valid)
    )
    attended = attended.reshape(row_count, half_width)
    branch = total_over_cores(product(attended, w_output)) + rep_master[4]
    middle = inputs + branch
    normed_two_full, norm_back_two = jax.vjp(layer_norm, middle, rep_master[2], rep_master[3])
    normed_two = normed_two_full.astype(jnp.bfloat16)
    hidden = product(normed_two, w_first) + split_master[0, 2:].reshape(hidden_width)
    active_full, gelu_back = jax.vjp(exact_gelu, hidden)
    active = active_full.astype(jnp.bfloat16)
    second = total_over_cores(product(active, w_second).astype(jnp.bfloat16)) + rep_master[5]
    result = (middle + second).astype(jnp.bfloat16)
    result_half = lax.dynamic_slice_in_dim(result, core_index * half_width, half_width, 1)
    outgoing = contract_rows(pick, result_half).astype(jnp.bfloat16)
    arrived = lax.all_to_all(
        outgoing.reshape(dp_count, slot_count * positions_here, half_width),
        "dp",
        split_axis=0,
        concat_axis=0,
        tiled=True,
    ).reshape(held_count, half_width)
    full_out = contract_rows(deal, arrived)
    full_out = jnp.where(unseen[:, None], mask_token.astype(jnp.float32)[None, :], full_out)
    full_out = full_out.astype(jnp.bfloat16).reshape(positions_here, strip_count, half_width)
    full_out = jnp.transpose(full_out, (1, 0, 2))[:, :, None, :]
    grad_rows = grad_out.astype(jnp.float32)
    bias_two_grad = jnp.sum(grad_rows, axis=0)
    grad_active = contract_last(grad_out, w_second)
    grad_hidden = gelu_back(grad_active)[0].astype(jnp.bfloat16)
    fc2_grad = contract_rows(active, grad_out)
    fc1_grad = contract_rows(normed_two, grad_hidden)
    hidden_bias_grad = jnp.sum(grad_hidden.astype(jnp.float32), axis=0)
    grad_normed_two = total_over_cores(contract_last(grad_hidden, w_first))
    grad_middle_part, gain_two_grad, shift_two_grad = norm_back_two(grad_normed_two)
    grad_middle = grad_rows + grad_middle_part
    grad_branch = grad_middle.astype(jnp.bfloat16)
    out_bias_grad = jnp.sum(grad_branch.astype(jnp.float32), axis=0)
    out_grad = contract_rows(attended, grad_branch)
    grad_attended = contract_last(grad_branch, w_output).astype(jnp.bfloat16)
    grad_queries, grad_keys, grad_values = lax.map(
        attend_pair_back,
        (
            by_pair(queries),
            by_pair(key_rows),
            by_pair(value_rows),
            pair_valid,
            log_total,
            by_pair(grad_attended),
        ),
    )
    grad_queries = grad_queries.reshape(row_count, half_width)
    grad_keys = grad_keys.reshape(row_count, half_width)
    grad_values = grad_values.reshape(row_count, half_width)
    grad_projected = jnp.stack([grad_queries, grad_keys, grad_values], axis=1).reshape(
        row_count, 3 * half_width
    )
    qkv_grad = contract_rows(normed, grad_projected)
    query_bias_grad = jnp.sum(grad_queries.astype(jnp.float32), axis=0)
    value_bias_grad = jnp.sum(grad_values.astype(jnp.float32), axis=0)
    grad_normed = total_over_cores(contract_last(grad_projected, w_attention))
    grad_inputs_part, gain_one_grad, shift_one_grad = norm_back_one(grad_normed)
    input_grad = (grad_middle + grad_inputs_part).reshape(slot_count, capacity, feature_width)
    def scattered(gradient):
        rows, width = gradient.shape
        chunks = gradient.astype(jnp.bfloat16).reshape(dp_count, rows // dp_count, width)
        return scatter_chunks(chunks, member_word, dp_count).reshape(1, -1)

    fc2_total = scattered(fc2_grad)
    fc1_total = scattered(fc1_grad)
    out_total = scattered(out_grad)
    qkv_total = scattered(qkv_grad)
    rep_grad = jnp.stack(
        [gain_one_grad, shift_one_grad, gain_two_grad, shift_two_grad, out_bias_grad, bias_two_grad]
    )
    split_grad = jnp.concatenate(
        [query_bias_grad[None], value_bias_grad[None], hidden_bias_grad.reshape(-1, half_width)],
        axis=0,
    )[None]
    packed = jnp.concatenate([mask_grad, rep_grad.reshape(-1), split_grad.reshape(-1)])
    packed = sum_over_dp(packed.reshape(-1, 128), dp_count).reshape(-1)
    mask_total = packed[:half_width]
    rep_total = packed[half_width : half_width + rep_grad.size].reshape(rep_grad.shape)
    split_total = packed[half_width + rep_grad.size :].reshape(split_grad.shape)
    qkv_new = adam_step(qkv_master, qkv_first, qkv_second, qkv_total, MATRIX_RATE, MATRIX_DECAY)
    out_new = adam_step(out_master, out_first, out_second, out_total, MATRIX_RATE, MATRIX_DECAY)
    fc1_new = adam_step(fc1_master, fc1_first, fc1_second, fc1_total, MATRIX_RATE, MATRIX_DECAY)
    fc2_new = adam_step(fc2_master, fc2_first, fc2_second, fc2_total, MATRIX_RATE, MATRIX_DECAY)
    rep_new = adam_step(rep_master, rep_first, rep_second, rep_total, VECTOR_RATE, 0.0)
    split_new = adam_step(split_master, split_first, split_second, split_total, VECTOR_RATE, 0.0)
    return (
        full_out,
        input_grad,
        mask_total,
        qkv_new[0],
        qkv_new[1],
        qkv_new[2],
        out_new[0],
        out_new[1],
        out_new[2],
        fc1_new[0],
        fc1_new[1],
        fc1_new[2],
        fc2_new[0],
        fc2_new[1],
        fc2_new[2],
        rep_new[0],
        rep_new[1],
        rep_new[2],
        split_new[0],
        split_new[1],
        split_new[2],
    )


BLOCK = 384
UNIT_ROWS = 48
UNIT_WIDTH = 1536
BLOCK_WIDTH = 256
Z_ORDER = (0, 12, 4, 8)
VMEM_BYTES = 60 * 1024 * 1024
ANY = pl.BlockSpec(memory_space=pl.ANY)
IN_VMEM = pl.BlockSpec(memory_space=pltpu.VMEM)
IN_SMEM = pl.BlockSpec(memory_space=pltpu.SMEM)


def shaped(shape, dtype):
    return jax.ShapeDtypeStruct(shape, dtype)


def params(grid_axes=0):
    semantics = ("arbitrary",) * grid_axes if grid_axes else None
    return pltpu.CompilerParams(dimension_semantics=semantics, vmem_limit_bytes=VMEM_BYTES)


def cost(microseconds):
    return pl.CostEstimate(
        flops=int(microseconds * 1.15e9), transcendentals=0, bytes_accessed=1000000
    )


def together(*values):
    return lax.optimization_barrier(values)


def hop_by_core(array, first_core, second_core, count):
    pairs = []
    for i in range(count):
        pairs.append((2 * i, 2 * (i ^ first_core)))
        pairs.append((2 * i + 1, 2 * (i ^ second_core) + 1))
    return lax.ppermute(array, ("dp", "mp"), pairs)


def pack_units(qkv, out, fc1, fc2):
    def body(qkv_ref, out_ref, fc1_ref, fc2_ref, units, unit_a, units_later):
        def put(unit, column, rows):
            units[unit, :, column * 128 : (column + 1) * 128] = rows.astype(jnp.bfloat16)

        for j in range(9):
            put(0, j, qkv_ref[pl.ds(j, UNIT_ROWS, stride=9), :])
        for j in range(3):
            put(0, 9 + j, out_ref[pl.ds(j, UNIT_ROWS, stride=3), :])
        for j in range(12):
            put(1, j, fc1_ref[pl.ds(j, UNIT_ROWS, stride=12), :])
        for half in range(2):
            for j in range(6):
                start = half * UNIT_ROWS * 6 + j
                put(2, half * 6 + j, fc2_ref[pl.ds(start, UNIT_ROWS, stride=6), :])
        unit_a[0] = units[0]
        units_later[0] = units[1]
        units_later[1] = units[2]

    def unit_array(count):
        return shaped((count, UNIT_ROWS, UNIT_WIDTH), jnp.bfloat16)

    return pl.pallas_call(
        body,
        out_shape=[unit_array(3), unit_array(1), unit_array(2)],
        compiler_params=params(),
        cost_estimate=cost(2),
        name="pack_units",
    )(
        *(array.reshape(-1, 128) for array in (qkv, out, fc1, fc2))
    )


def chunk_sources(words, own, pieces, unit):
    step, offset = (1, 0) if unit == 0 else (2, unit - 1)
    found = []
    for place, extra in enumerate((0, words[1], words[2], 3)):
        found.append((own[place].at[unit], words[0] ^ extra))
        for entry, distance in enumerate(Z_ORDER[1:]):
            source = pieces[place].at[entry * step + offset]
            found.append((source, words[0] ^ distance ^ extra))
    return found


def join_chunks(chunks):
    size = chunks[0].shape[0]

    def body(*refs):
        for entry, ref in enumerate(refs[:-1]):
            refs[-1][entry * size : (entry + 1) * size] = ref[...]

    return pl.pallas_call(
        body,
        out_shape=shaped((len(chunks) * size,) + chunks[0].shape[1:], chunks[0].dtype),
        compiler_params=params(),
        cost_estimate=cost(1.5 * size),
        name="join_chunks",
    )(*chunks)


def last_messages(kept, one, two, carried=None):
    extra = 0 if carried is None else 16
    inputs = [kept, one, two] + ([] if carried is None else [carried])

    def body(kept_ref, one_ref, two_ref, *refs):
        targets = refs[-3:]
        if extra:
            vectors = refs[0][...].astype(jnp.float32)
            vectors = vectors + two_ref[4 * UNIT_ROWS :, :].astype(jnp.float32)
            vectors = vectors.astype(jnp.bfloat16)
        for entry, target in enumerate(targets):
            rows = slice((entry + 1) * UNIT_ROWS, (entry + 2) * UNIT_ROWS)
            total = kept_ref[rows, :].astype(jnp.float32) + one_ref[rows, :].astype(jnp.float32)
            total = total + two_ref[rows, :].astype(jnp.float32)
            target[:UNIT_ROWS, :] = total.astype(jnp.bfloat16)
            if extra:
                target[UNIT_ROWS:, :] = vectors

    def rows(count, start=0):
        return pl.BlockSpec((count, UNIT_WIDTH), lambda i: (start, 0))

    specs = [rows(4 * UNIT_ROWS), rows(4 * UNIT_ROWS), rows(4 * UNIT_ROWS + extra)]
    if extra:
        specs.append(rows(16, 4 * UNIT_ROWS // 16))
    message = shaped((UNIT_ROWS + extra, UNIT_WIDTH), jnp.bfloat16)
    return pl.pallas_call(
        body,
        grid=(1,),
        in_specs=specs,
        out_specs=[rows(UNIT_ROWS + extra)] * 3,
        out_shape=[message] * 3,
        compiler_params=params(1),
        cost_estimate=cost(1.5),
        name="last_messages",
    )(*inputs)


def added(start, stop, *arrays):
    total = 0.0
    for array, offset in arrays:
        total = total + array[start - offset : stop - offset].astype(jnp.float32)
    return total.astype(jnp.bfloat16)


def unit_shapes(extra=0):
    return [shaped((8 * UNIT_ROWS + extra, UNIT_WIDTH), jnp.bfloat16)] * 2


def unit_targets(words, sent, kept):
    def rows(array, entry):
        return array.at[pl.ds(entry * UNIT_ROWS, UNIT_ROWS), :]

    places = []
    for entry, distance in enumerate(Z_ORDER):
        own = words[0] ^ distance
        places.append((rows(sent, 4 + entry), own ^ 3))
        places.append((rows(sent, entry), own ^ words[2]))
        places.append((rows(kept, entry), own))
        places.append((rows(kept, 4 + entry), own ^ words[1]))
    return places


def lanes_of(part, size):
    return pl.ds(pl.multiple_of(part * size, 128), size)


def unit_rows(owner, rows=UNIT_ROWS):
    return pl.ds(pl.multiple_of(owner * rows, 16), rows)


def norm_parts(signal):
    average = jnp.mean(signal, axis=1, keepdims=True)
    centered = signal - average
    scale = lax.rsqrt(jnp.mean(centered * centered, axis=1, keepdims=True) + NORM_EPS)
    return centered * scale, scale


def norm_back(grad, unit_signal, scale, gain):
    scaled = grad * gain
    mean_one = jnp.mean(scaled, axis=1, keepdims=True)
    mean_two = jnp.mean(scaled * unit_signal, axis=1, keepdims=True)
    return scale * (scaled - mean_one - unit_signal * mean_two)


def fixed(*shape):
    return pl.BlockSpec(shape, lambda i: (0,) * len(shape))


def run_copies(pairs, semaphores):
    copies = [
        pltpu.make_async_copy(source, target, semaphores.at[i])
        for i, (source, target) in enumerate(pairs)
    ]
    for copy in copies:
        copy.start()
    for copy in copies:
        copy.wait()


class Copies:
    def __init__(self, semaphores):
        self.semaphores, self.used = semaphores, 0

    def start(self, pairs):
        started = []
        for source, target in pairs:
            copy = pltpu.make_async_copy(source, target, self.semaphores.at[self.used])
            self.used += 1
            copy.start()
            started.append(copy)
        return started


def finish(copies):
    for copy in copies:
        copy.wait()


def chunk_pairs(words, own, pieces, unit, target):
    return [
        (source, target.at[unit_rows(owner), :])
        for source, owner in chunk_sources(words, own, pieces, unit)
    ]


def attention_forward(words, rows_in, rep, split, column_bias, own_pieces, pieces):
    count, width = rows_in.shape
    half = split.shape[1]
    pairs_of_heads = half // (2 * HEAD)

    def body(
        words_ref, in_ref, rep_ref, split_ref, bias_ref, o0, o1, o2, o3, p0, p1, p2, p3,
        normed_ref, qkv_ref, prob_ref, attended_ref, partial_ref, weights_ref, w_out_ref, spread, semaphores,
    ):
        pair = pl.program_id(0)

        @pl.when(pair == 0)
        def _():
            copies = Copies(semaphores)
            pairs = chunk_pairs(words_ref, (o0, o1, o2, o3), (p0, p1, p2, p3), 0, weights_ref)
            loads = copies.start(pairs)

            @pl.loop(0, count // BLOCK)
            def _(block):
                rows = pl.ds(block * BLOCK, BLOCK)
                unit_signal, _ = norm_parts(in_ref[rows, :].astype(jnp.float32))
                normed = unit_signal * rep_ref[0:1, :] + rep_ref[1:2, :]
                normed_ref[rows, :] = normed.astype(jnp.bfloat16)

            finish(loads)

            @pl.loop(0, count // BLOCK)
            def _(block):
                rows = pl.ds(block * BLOCK, BLOCK)
                projected = product(normed_ref[rows, :], weights_ref[:, : 3 * half])
                queries = projected[:, :half] + split_ref[0:1, :]
                values = projected[:, 2 * half :] + split_ref[1:2, :]
                qkv_ref[rows, :half] = queries.astype(jnp.bfloat16)
                qkv_ref[rows, half : 2 * half] = projected[:, half : 2 * half].astype(jnp.bfloat16)
                qkv_ref[rows, 2 * half :] = values.astype(jnp.bfloat16)

        lane = pl.multiple_of(pair * (2 * HEAD), 2 * HEAD)
        upper = lax.broadcasted_iota(jnp.int32, (1, 2 * HEAD), 1) >= HEAD
        keys = qkv_ref[:, pl.ds(half + lane, 2 * HEAD)]
        values = qkv_ref[:, pl.ds(2 * half + lane, 2 * HEAD)]
        for block in range(count // BLOCK):
            rows = pl.ds(block * BLOCK, BLOCK)
            queries = qkv_ref[rows, pl.ds(lane, 2 * HEAD)]
            found = []
            for side in range(2):
                chosen = upper if side else jnp.logical_not(upper)
                own = jnp.where(chosen, queries, jnp.zeros_like(queries))
                scores = contract_last(own, keys) * HEAD ** (-0.5) + bias_ref[...]
                lifted = jnp.exp(scores - jnp.max(scores, axis=1, keepdims=True))
                total = jnp.sum(lifted, axis=1, keepdims=True)
                probability = (lifted * (1.0 / total)).astype(jnp.bfloat16)
                prob_ref[side, rows, :] = probability
                found.append(product(probability, values))
            attended = jnp.where(upper, found[1], found[0])
            attended_ref[rows, pl.ds(lane, 2 * HEAD)] = attended.astype(jnp.bfloat16)

        @pl.when(pair == pairs_of_heads - 1)
        def _():
            for strip in range(half // 128):
                start = 3 * half + strip * 128
                spread[strip] = weights_ref[:, start : start + 128].astype(jnp.float32)
                for side in range(2):
                    start = side * half + strip * 128
                    w_out_ref[:, start : start + 128] = spread[
                        strip, pl.ds(side, half, stride=2), :
                    ].astype(jnp.bfloat16)
            partial_ref[...] = product(attended_ref[...], w_out_ref[...]).astype(jnp.bfloat16)

    return pl.pallas_call(
        body,
        grid=(pairs_of_heads,),
        in_specs=[IN_SMEM, fixed(count, width), fixed(6, width), fixed(6, half), fixed(1, count)]
        + [ANY] * 8,
        out_specs=[
            fixed(count, width),
            fixed(count, 3 * half),
            pl.BlockSpec((2, count, count), lambda h: (h, 0, 0)),
            fixed(count, half),
            fixed(count, width),
            fixed(width, UNIT_WIDTH),
            fixed(half, width),
        ],
        out_shape=[
            shaped((count, width), jnp.bfloat16),
            shaped((count, 3 * half), jnp.bfloat16),
            shaped((2 * pairs_of_heads, count, count), jnp.bfloat16),
            shaped((count, half), jnp.bfloat16),
            shaped((count, width), jnp.bfloat16),
            shaped((width, UNIT_WIDTH), jnp.bfloat16),
            shaped((half, width), jnp.bfloat16),
        ],
        scratch_shapes=[
            pltpu.VMEM((half // 128, width, 128), jnp.float32),
            pltpu.SemaphoreType.DMA((16,)),
        ],
        compiler_params=params(1),
        cost_estimate=cost(18),
        name="attention_forward",
    )(words, rows_in, rep, split, column_bias, *own_pieces, *pieces)


def mlp_all(
    words, rows_in, own, other, rep, hidden_bias, grad_out, own_pieces, pieces
):
    count, width = rows_in.shape
    hidden_width = UNIT_WIDTH
    half, wide = width // 2, 2 * BLOCK_WIDTH
    parts = hidden_width // wide

    def body(
        words_ref, rep_ref, bias_ref, in_any, own_any, other_any, grad_any,
        o0, o1, o2, o3, p0, p1, p2, p3,
        hidden_sum_ref, grad_sum_ref, middle_any, back_any, second_any,
        sent_b, kept_b, sent_c, kept_c,
        w_first, w_second, rows_ref, own_ref, other_ref, grad_ref, middle_ref, normed_ref,
        active_ref, slope_ref, grad_hidden_ref, back_ref, second_ref, whole_b, whole_c, semaphores,
    ):
        copies = Copies(semaphores)
        first_loads = copies.start(
            [(in_any, rows_ref), (own_any, own_ref), (other_any, other_ref)]
        )
        own_refs, later = (o0, o1, o2, o3), (p0, p1, p2, p3)
        loads_b = copies.start(chunk_pairs(words_ref, own_refs, later, 1, w_first))
        pairs = [(grad_any, grad_ref)]
        for source, owner in chunk_sources(words_ref, own_refs, later, 2):
            for side in range(2):
                pairs.append(
                    (
                        source.at[:, pl.ds(side * width, width)],
                        w_second.at[unit_rows(owner * 2 + side), :],
                    )
                )
        loads_c = copies.start(pairs)
        finish(first_loads)

        @pl.loop(0, count // BLOCK)
        def _(block):
            rows = pl.ds(block * BLOCK, BLOCK)
            branch = own_ref[rows, :].astype(jnp.float32) + other_ref[rows, :].astype(jnp.float32)
            middle = rows_ref[rows, :].astype(jnp.float32) + branch + rep_ref[4:5, :]
            middle_ref[rows, :] = middle
            unit_signal, _ = norm_parts(middle)
            normed = unit_signal * rep_ref[2:3, :] + rep_ref[3:4, :]
            normed_ref[rows, :] = normed.astype(jnp.bfloat16)

        stores = copies.start([(middle_ref, middle_any)])
        finish(loads_b)
        for part in range(parts):
            columns = slice(part * wide, (part + 1) * wide)
            hidden = product(normed_ref[...], w_first[:, columns]) + bias_ref[:, columns]
            spread = 0.5 + 0.5 * lax.erf(hidden * 0.7071067811865476)
            active_ref[:, columns] = (hidden * spread).astype(jnp.bfloat16)
            slope = spread + hidden * jnp.exp(-0.5 * hidden * hidden) * 0.3989422804014327
            slope_ref[:, columns] = slope.astype(jnp.bfloat16)

        finish(loads_c)
        second_ref[...] = product(active_ref[...], w_second[...]).astype(jnp.bfloat16)
        stores += copies.start([(second_ref, second_any)])
        grad_sum_ref[...] = jnp.sum(grad_ref[...].astype(jnp.float32), axis=0, keepdims=True)
        for part in range(parts):
            columns = slice(part * wide, (part + 1) * wide)
            grad_active = contract_last(grad_ref[...], w_second[columns, :])
            grad_hidden = grad_active * slope_ref[:, columns].astype(jnp.float32)
            grad_hidden = grad_hidden.astype(jnp.bfloat16)
            grad_hidden_ref[:, columns] = grad_hidden
            hidden_sum_ref[:, columns] = jnp.sum(
                grad_hidden.astype(jnp.float32), axis=0, keepdims=True
            )

        back_ref[...] = contract_last(grad_hidden_ref[...], w_first[...]).astype(jnp.bfloat16)
        stores += copies.start([(back_ref, back_any)])

        @pl.loop(0, hidden_width // half)
        def _(part):
            columns = lanes_of(part, half)
            whole_c[columns, :] = contract_rows(active_ref[:, columns], grad_ref[...]).astype(
                jnp.bfloat16
            )

        for target, owner in unit_targets(words_ref, sent_c, kept_c):
            stores += copies.start(
                [
                    (
                        whole_c.at[unit_rows(owner * 2 + side), :],
                        target.at[:, pl.ds(side * width, width)],
                    )
                    for side in range(2)
                ]
            )

        @pl.loop(0, width // half)
        def _(part):
            columns = lanes_of(part, half)
            whole_b[columns, :] = contract_rows(normed_ref[:, columns], grad_hidden_ref[...]).astype(
                jnp.bfloat16
            )

        for target, owner in unit_targets(words_ref, sent_b, kept_b):
            stores += copies.start([(whole_b.at[unit_rows(owner), :], target)])
        finish(stores)

    low, full = jnp.bfloat16, jnp.float32
    return pl.pallas_call(
        body,
        in_specs=[IN_SMEM, IN_VMEM, IN_VMEM] + [ANY] * 12,
        out_specs=[IN_VMEM, IN_VMEM] + [ANY] * 7,
        out_shape=[
            shaped((1, hidden_width), full),
            shaped((1, width), full),
            shaped((count, width), full),
            shaped((count, width), low),
            shaped((count, width), low),
        ]
        + unit_shapes()
        + unit_shapes(),
        scratch_shapes=[
            pltpu.VMEM((width, hidden_width), low),
            pltpu.VMEM((hidden_width, width), low),
            pltpu.VMEM((count, width), low),
            pltpu.VMEM((count, width), low),
            pltpu.VMEM((count, width), low),
            pltpu.VMEM((count, width), low),
            pltpu.VMEM((count, width), full),
            pltpu.VMEM((count, width), low),
            pltpu.VMEM((count, hidden_width), low),
            pltpu.VMEM((count, hidden_width), low),
            pltpu.VMEM((count, hidden_width), low),
            pltpu.VMEM((count, width), low),
            pltpu.VMEM((count, width), low),
            pltpu.VMEM((width, hidden_width), low),
            pltpu.VMEM((hidden_width, width), low),
            pltpu.SemaphoreType.DMA((104,)),
        ],
        compiler_params=params(),
        cost_estimate=cost(18),
        name="mlp_all",
    )(words, rep, hidden_bias, rows_in, own, other, grad_out, *own_pieces, *pieces)


def attention_back(
    words, rep, hidden_sum, grad_sum, mask_sum, middle, own, other, grad_out, w_out, attended, qkv,
    prob, normed, weights, rows_in,
):
    count, width = middle.shape
    half = qkv.shape[1] // 3
    span = 3 * half
    pairs_of_heads = half // (2 * HEAD)
    low, full = jnp.bfloat16, jnp.float32

    def body(
        words_ref, rep_ref, hidden_sum_ref, grad_sum_ref, mask_sum_ref,
        middle_any, own_any, other_any, grad_any, w_out_any, attended_any, qkv_any, prob_any,
        normed_any, weights_any, in_any,
        grad_middle_any, back_any, sent, kept,
        middle_ref, own_ref, other_ref, grad_ref, w_out_ref, attended_ref, qkv_ref, prob_ref,
        normed_ref, weights_ref, in_ref, grad_middle_ref, back_ref, branch, grad_attended,
        grad_qkv, spread, whole, vectors, low_vectors, semaphores,
    ):
        copies = Copies(semaphores)
        early = copies.start(
            [
                (middle_any, middle_ref), (own_any, own_ref), (other_any, other_ref),
                (grad_any, grad_ref),
            ]
        )
        outer = copies.start([(w_out_any, w_out_ref), (attended_any, attended_ref)])
        inner = copies.start([(qkv_any, qkv_ref)])
        probs = copies.start(
            [(prob_any.at[pl.ds(2 * i, 2)], prob_ref.at[i]) for i in range(pairs_of_heads)]
        )
        late = copies.start(
            [(normed_any, normed_ref), (weights_any, weights_ref), (in_any, in_ref)]
        )
        vectors[...] = jnp.zeros_like(vectors)
        finish(early)

        @pl.loop(0, count // BLOCK)
        def _(block):
            rows = pl.ds(block * BLOCK, BLOCK)
            unit_signal, scale = norm_parts(middle_ref[rows, :])
            mine = own_ref[rows, :].astype(full)
            grad_normed = mine + other_ref[rows, :].astype(full)
            grad_middle = grad_ref[rows, :].astype(full) + norm_back(
                grad_normed, unit_signal, scale, rep_ref[2:3, :]
            )
            grad_middle_ref[rows, :] = grad_middle
            grad_branch = grad_middle.astype(low)
            branch[rows, :] = grad_branch
            vectors[1:2, :width] += jnp.sum(mine * unit_signal, axis=0, keepdims=True)
            vectors[1:2, width:] += jnp.sum(mine, axis=0, keepdims=True)
            vectors[2:3, :width] += 0.5 * jnp.sum(grad_branch.astype(full), axis=0, keepdims=True)

        stores = copies.start([(grad_middle_ref, grad_middle_any)])
        finish(outer)
        grad_attended[...] = contract_last(branch[...], w_out_ref[...]).astype(low)
        out_gradient = contract_rows(attended_ref[...], branch[...])
        for strip in range(half // 128):
            for side in range(2):
                start = side * half + strip * 128
                spread[strip, pl.ds(side, half, stride=2), :] = out_gradient[
                    :, start : start + 128
                ]
            start = span + strip * 128
            whole[:, start : start + 128] = spread[strip].astype(low)
        finish(inner)
        upper = lax.broadcasted_iota(jnp.int32, (1, 2 * HEAD), 1) >= HEAD
        finish(probs)

        @pl.loop(0, pairs_of_heads)
        def _(pair):
            lanes = [
                pl.ds(pl.multiple_of(part * half + pair * (2 * HEAD), 2 * HEAD), 2 * HEAD)
                for part in range(3)
            ]
            queries, keys, values = (qkv_ref[:, lane] for lane in lanes)
            grad = grad_attended[:, lanes[0]]
            found = []
            for side in range(2):
                chosen = upper if side else jnp.logical_not(upper)
                own_grad = jnp.where(chosen, grad, jnp.zeros_like(grad))
                low_probability = prob_ref[pair, side]
                probability = low_probability.astype(full)
                weighted = probability * contract_last(own_grad, values)
                inner_sum = jnp.sum(weighted, axis=1, keepdims=True)
                grad_scores = (weighted - probability * inner_sum).astype(low)
                found.append(
                    (
                        product(grad_scores, keys),
                        contract_rows(queries, grad_scores)[side * HEAD : (side + 1) * HEAD],
                        contract_rows(grad, low_probability)[side * HEAD : (side + 1) * HEAD],
                    )
                )
            backs = (
                jnp.where(upper, found[1][0], found[0][0]) * HEAD ** (-0.5),
                jnp.transpose(jnp.concatenate([found[0][1], found[1][1]])) * HEAD ** (-0.5),
                jnp.transpose(jnp.concatenate([found[0][2], found[1][2]])),
            )
            for lane, value in zip(lanes, backs):
                grad_qkv[:, lane] = value.astype(low)

        finish(late)

        @pl.loop(0, width // half)
        def _(part):
            columns = lanes_of(part, half)
            whole[columns, :span] = contract_rows(normed_ref[:, columns], grad_qkv[...]).astype(low)

        for target, owner in unit_targets(words_ref, sent, kept):
            stores += copies.start([(whole.at[unit_rows(owner), :], target)])

        @pl.loop(0, count // BLOCK)
        def _(block):
            rows = pl.ds(block * BLOCK, BLOCK)
            back = contract_last(grad_qkv[rows, :], weights_ref[:, :span])
            back_ref[rows, :] = back.astype(low)
            unit_signal, _ = norm_parts(in_ref[rows, :].astype(full))
            vectors[0:1, :width] += jnp.sum(back * unit_signal, axis=0, keepdims=True)
            vectors[0:1, width:] += jnp.sum(back, axis=0, keepdims=True)
            for place, part in enumerate((0, 2)):
                sums = jnp.sum(
                    grad_qkv[rows, part * half : (part + 1) * half].astype(full),
                    axis=0,
                    keepdims=True,
                )
                vectors[3:4, place * half : (place + 1) * half] += sums

        stores += copies.start([(back_ref, back_any)])
        vectors[2:3, width:] = 0.5 * grad_sum_ref[...]
        vectors[3:4, 2 * half : span] = mask_sum_ref[...]
        vectors[4:5, :] = hidden_sum_ref[...]
        low_vectors[...] = vectors[...].astype(low)
        last = pl.ds(8 * UNIT_ROWS, 16)
        stores += copies.start([(low_vectors, sent.at[last, :]), (low_vectors, kept.at[last, :])])
        finish(stores)

    return pl.pallas_call(
        body,
        in_specs=[IN_SMEM] + [IN_VMEM] * 4 + [ANY] * 11,
        out_specs=[ANY] * 4,
        out_shape=[shaped((count, width), full), shaped((count, width), low)] + unit_shapes(16),
        scratch_shapes=[
            pltpu.VMEM((count, width), full),
            pltpu.VMEM((count, width), low),
            pltpu.VMEM((count, width), low),
            pltpu.VMEM((count, width), low),
            pltpu.VMEM((half, width), low),
            pltpu.VMEM((count, half), low),
            pltpu.VMEM((count, span), low),
            pltpu.VMEM((pairs_of_heads, 2, count, count), low),
            pltpu.VMEM((count, width), low),
            pltpu.VMEM((width, UNIT_WIDTH), low),
            pltpu.VMEM((count, width), low),
            pltpu.VMEM((count, width), full),
            pltpu.VMEM((count, width), low),
            pltpu.VMEM((count, width), low),
            pltpu.VMEM((count, half), low),
            pltpu.VMEM((count, span), low),
            pltpu.VMEM((half // 128, width, 128), full),
            pltpu.VMEM((width, UNIT_WIDTH), low),
            pltpu.VMEM((16, UNIT_WIDTH), full),
            pltpu.VMEM((16, UNIT_WIDTH), low),
            pltpu.SemaphoreType.DMA((40,)),
        ],
        compiler_params=params(),
        cost_estimate=cost(22),
        name="attention_back",
    )(
        words, rep, hidden_sum, grad_sum, mask_sum, middle, own, other, grad_out, w_out, attended,
        qkv, prob, normed, weights, rows_in,
    )


def input_gradient(rows_in, own, other, grad_middle, rep):
    count, width = rows_in.shape

    def body(in_ref, own_ref, other_ref, middle_ref, rep_ref, out_ref):
        unit_signal, scale = norm_parts(in_ref[...].astype(jnp.float32))
        grad = own_ref[...].astype(jnp.float32) + other_ref[...].astype(jnp.float32)
        out_ref[...] = middle_ref[...] + norm_back(grad, unit_signal, scale, rep_ref[0:1, :])

    block = pl.BlockSpec((BLOCK, width), lambda i: (i, 0))
    return pl.pallas_call(
        body,
        grid=(count // BLOCK,),
        in_specs=[block, block, block, block, pl.BlockSpec(rep.shape, lambda i: (0, 0))],
        out_specs=block,
        out_shape=shaped((count, width), jnp.float32),
        compiler_params=params(1),
        cost_estimate=cost(5.7),
        name="input_gradient",
    )(rows_in, own, other, grad_middle, rep)


def adam_unit(units, states, strides):
    flat = [array.reshape(-1, 128) for state in states for array in state]
    terms = [array for unit in units for array in unit]
    counts = [len(unit) for unit in units]

    def body(*refs):
        terms_here, refs = refs[: len(terms)], refs[len(terms) :]
        inputs, outputs = refs[: len(flat)], refs[len(flat) :]
        for unit, column, state, start, step in strides:
            columns = slice(column * 128, (column + 1) * 128)
            skip = sum(counts[:unit])
            gradient = terms_here[skip][:, columns].astype(jnp.float32)
            for term in terms_here[skip + 1 : skip + counts[unit]]:
                gradient = gradient + term[:, columns].astype(jnp.float32)
            rows = pl.ds(start, UNIT_ROWS, stride=step)
            weight, one, two = (inputs[3 * state + i][rows, :] for i in range(3))
            updated = adam_step(weight, one, two, gradient, MATRIX_RATE, MATRIX_DECAY)
            for i in range(3):
                outputs[3 * state + i][rows, :] = updated[i]

    whole = [pl.BlockSpec(array.shape, lambda i: (0, 0)) for array in flat]
    results = pl.pallas_call(
        body,
        grid=(1,),
        in_specs=[
            pl.BlockSpec((UNIT_ROWS, term.shape[1]), lambda i: (0, 0)) for term in terms
        ]
        + whole,
        out_specs=whole,
        out_shape=[shaped(array.shape, jnp.float32) for array in flat],
        compiler_params=params(1),
        cost_estimate=cost(2.5),
        name="adam_unit",
    )(*terms, *flat)
    return [array.reshape(1, -1) for array in results]


def on_device(
    patch_rows,
    cotangent,
    mask_token,
    lengths,
    masked,
    dealing,
    qkv_master,
    qkv_first,
    qkv_second,
    out_master,
    out_first,
    out_second,
    fc1_master,
    fc1_first,
    fc1_second,
    fc2_master,
    fc2_first,
    fc2_second,
    rep_master,
    rep_first,
    rep_second,
    split_master,
    split_first,
    split_second,
):
    slot_count, capacity, feature_width = patch_rows.shape
    half_width = mask_token.shape[0]
    dp_count = lax.axis_size("dp")
    member = lax.axis_index("dp")
    core_index = lax.axis_index("mp")
    positions_here = cotangent.shape[1]
    position_span = positions_here * dp_count
    heads_here = half_width // HEAD
    row_count = slot_count * capacity
    strip_count = lengths.shape[0]
    position_rows = -(-positions_here // 4) * 4
    held_count = strip_count * positions_here
    dealt_count = strip_count * position_rows
    words = jnp.stack([member, 1 + core_index, 2 - core_index, core_index]).astype(jnp.int32)

    inputs = patch_rows.reshape(row_count, feature_width)
    split_rows = split_master[0]
    hidden_bias = split_rows[2:].reshape(1, -1)
    units, unit_a, units_later = pack_units(qkv_master, out_master, fc1_master, fc2_master)

    patch_index = jnp.arange(PATCHES, dtype=jnp.int32)
    visible_all = (patch_index[None, :] < lengths[:, None]) & (masked == 0)
    strips_here = lax.dynamic_slice_in_dim(dealing, member * slot_count, slot_count)
    visible_here = visible_all[strips_here]
    rank_here = jnp.cumsum(visible_here.astype(jnp.int32), axis=1) - 1
    counts_here = jnp.sum(visible_here.astype(jnp.int32), axis=1)
    valid_rows = jnp.arange(capacity, dtype=jnp.int32)[None, :] < counts_here[:, None]
    column_bias = jnp.where(valid_rows, 0.0, -1e30).astype(jnp.float32).reshape(1, row_count)
    padding = position_span - PATCHES
    visible_padded = jnp.pad(visible_here, ((0, 0), (0, padding)))
    rank_padded = jnp.pad(jnp.maximum(rank_here, 0), ((0, 0), (0, padding)))
    own_positions = jnp.arange(positions_here, dtype=jnp.int32) * dp_count + member
    inside = own_positions < PATCHES
    visible_own = visible_all[:, jnp.minimum(own_positions, PATCHES - 1)] & inside[None, :]
    row_time = jnp.arange(position_rows, dtype=jnp.int32)[None, :]
    strip_row = jnp.where(
        row_time < positions_here, row_time * strip_count + dealing[:, None], -1
    ).reshape(dealt_count)
    deal = (
        strip_row[:, None] == jnp.arange(held_count, dtype=jnp.int32)[None, :]
    ).astype(jnp.bfloat16)
    encoder_row = jnp.where(
        visible_padded,
        rank_padded + jnp.arange(slot_count, dtype=jnp.int32)[:, None] * capacity,
        -1,
    )
    encoder_row = jnp.transpose(
        encoder_row.reshape(slot_count, positions_here, dp_count), (2, 0, 1)
    )
    encoder_row = jnp.pad(
        encoder_row, ((0, 0), (0, 0), (0, position_rows - positions_here)), constant_values=-1
    ).reshape(dealt_count)
    pick = (
        jnp.arange(row_count, dtype=jnp.int32)[:, None] == encoder_row[None, :]
    ).astype(jnp.bfloat16)
    unseen = jnp.transpose(jnp.logical_not(visible_own) & inside[None, :]).reshape(held_count)

    cotangent_rows = jnp.transpose(
        cotangent.reshape(strip_count, positions_here, half_width), (1, 0, 2)
    ).reshape(held_count, half_width)

    def spread_out(array):
        return hop_by_core(array, 1, 2, dp_count), hop_by_core(array, 2, 1, dp_count)

    def exchanged(array):
        array = array.reshape(dp_count, slot_count * position_rows, half_width)
        array = lax.all_to_all(array, "dp", split_axis=0, concat_axis=0, tiled=True)
        return array.reshape(dealt_count, half_width)

    def columns_of(unit):
        return [hop(unit, distance, dp_count) for distance in Z_ORDER[1:]]

    def along_z(messages):
        return [hop(message, k, dp_count) for message, k in zip(messages, Z_ORDER[1:])]

    own_first, own_second = spread_out(units)
    column_a = columns_of(unit_a)
    column_a, own_first, own_second, units_later, cotangent_rows, deal, unseen = together(
        column_a, own_first, own_second, units_later, cotangent_rows, deal, unseen
    )

    column_a = join_chunks(column_a)
    first_a, second_a = spread_out(column_a)
    own_third = hop_by_core(own_first, 2, 1, dp_count)
    column_far = hop(units_later, 12, dp_count)
    dealt = product(deal, cotangent_rows).astype(jnp.bfloat16)
    mask_sum = product(unseen.astype(jnp.bfloat16)[None, :], cotangent_rows)
    first_a, second_a, own_third, dealt, mask_sum, column_bias, pick, column_far, units_later = (
        together(
            first_a, second_a, own_third, dealt, mask_sum, column_bias, pick, column_far,
            units_later,
        )
    )

    third_a = hop_by_core(first_a, 2, 1, dp_count)
    column = [hop(units_later, distance, dp_count) for distance in (4, 8)]
    third_a, column, inputs_here, dealt = together(third_a, column, inputs, dealt)

    column = join_chunks([column_far, *column])
    first, last = spread_out(column)
    returned = exchanged(dealt)
    own_pieces = (units, own_first, own_second, own_third)
    normed, qkv, prob, attended, branch, weights_a, w_output = attention_forward(
        words, inputs_here, rep_master, split_rows, column_bias, own_pieces,
        (column_a, first_a, second_a, third_a),
    )
    first, last = together(first, last)

    third = hop_by_core(first, 2, 1, dp_count)
    branch_other = swap_cores(branch)
    gathered = product(pick, returned).astype(jnp.bfloat16)
    gathered_other = swap_cores(gathered)
    grad_out = jnp.where(
        core_index == 0,
        jnp.concatenate([gathered, gathered_other], axis=1),
        jnp.concatenate([gathered_other, gathered], axis=1),
    )
    third, branch_other, grad_out = together(third, branch_other, grad_out)

    hidden_sum, grad_sum, middle, back_two, second, sent_b, kept_b, sent_c, kept_c = mlp_all(
        words, inputs, branch, branch_other, rep_master, hidden_bias, grad_out, own_pieces,
        (column, first, last, third),
    )
    middle, back_two, second, sent_b, kept_b, sent_c, kept_c = together(
        middle, back_two, second, sent_b, kept_b, sent_c, kept_c
    )

    one_c = hop_by_core(sent_c, 2, 1, dp_count)
    back_two_other = swap_cores(back_two)
    second_other = swap_cores(second)
    total = second.astype(jnp.float32) + second_other.astype(jnp.float32) + rep_master[5]
    result = (middle + total).astype(jnp.bfloat16)
    result_half = lax.dynamic_slice_in_dim(result, core_index * half_width, half_width, 1)
    outgoing = contract_rows(pick, result_half).astype(jnp.bfloat16)
    one_c, back_two_other, outgoing = together(one_c, back_two_other, outgoing)

    half_unit = 4 * UNIT_ROWS
    one_b = hop_by_core(sent_b, 2, 1, dp_count)
    two_c = hop_by_core(
        added(half_unit, 2 * half_unit, (kept_c, 0), (one_c, 0)), 1, 2, dp_count
    )
    arrived = exchanged(outgoing)
    grad_middle, back_one, sent_a, kept_a = attention_back(
        words, rep_master, hidden_sum, grad_sum, mask_sum, middle, back_two, back_two_other,
        grad_out, w_output, attended, qkv, prob, normed, weights_a, inputs,
    )
    two_c, one_b, back_one, sent_a, kept_a, arrived = together(
        two_c, one_b, back_one, sent_a, kept_a, arrived
    )

    one_a = hop_by_core(sent_a, 2, 1, dp_count)
    two_b = hop_by_core(
        added(half_unit, 2 * half_unit, (kept_b, 0), (one_b, 0)), 1, 2, dp_count
    )
    arrivals_c = along_z(last_messages(kept_c, one_c, two_c))
    full_out = contract_rows(deal, arrived)
    full_out = jnp.where(unseen[:, None], mask_token.astype(jnp.float32)[None, :], full_out)
    full_out = full_out.astype(jnp.bfloat16)
    one_a, arrivals_c, two_b, full_out, back_one = together(
        one_a, arrivals_c, two_b, full_out, back_one
    )

    two_a_sent = added(half_unit, 2 * half_unit + 16, (kept_a, 0), (one_a, 0))
    two_a = hop_by_core(two_a_sent, 1, 2, dp_count)
    arrivals_b = along_z(last_messages(kept_b, one_b, two_b))
    fc2_new = adam_unit(
        [(kept_c, one_c, two_c, *arrivals_c)],
        [(fc2_master, fc2_first, fc2_second)],
        [(0, side * 6 + j, 0, side * UNIT_ROWS * 6 + j, 6) for side in range(2) for j in range(6)],
    )
    back_one_other = swap_cores(back_one)
    two_a_sent, two_a, arrivals_b, back_one_other, *fc2_new = together(
        two_a_sent, two_a, arrivals_b, back_one_other, *fc2_new
    )

    messages = last_messages(kept_a, one_a, two_a, two_a_sent)
    arrivals = along_z(messages)
    fc1_new = adam_unit(
        [(kept_b, one_b, two_b, *arrivals_b)],
        [(fc1_master, fc1_first, fc1_second)],
        [(0, j, 0, j, 12) for j in range(12)],
    )
    input_grad = input_gradient(inputs, back_one, back_one_other, grad_middle, rep_master)
    arrivals, message, input_grad, *fc1_new = together(
        arrivals, messages[0], input_grad, *fc1_new
    )

    vectors = [array[UNIT_ROWS:].astype(jnp.float32) for array in (message, *arrivals)]
    vectors = (vectors[0] + vectors[1]) + (vectors[2] + vectors[3])
    rep_total = (vectors[:3] + swap_cores(vectors[:3])).reshape(rep_master.shape)
    split_total = jnp.concatenate(
        [vectors[3, : 2 * half_width], vectors[4]]
    ).reshape(split_master.shape)
    mask_total = vectors[3, 2 * half_width : 3 * half_width]
    qkv_out_new = adam_unit(
        [(kept_a, one_a, two_a, *arrivals)],
        [(qkv_master, qkv_first, qkv_second), (out_master, out_first, out_second)],
        [(0, j, 0, j, 9) for j in range(9)] + [(0, 9 + j, 1, j, 3) for j in range(3)],
    )
    full_out = full_out.reshape(positions_here, strip_count, half_width)
    full_out = jnp.transpose(full_out, (1, 0, 2))[:, :, None, :]
    input_grad = input_grad.reshape(slot_count, capacity, feature_width)
    rep_new = adam_step(rep_master, rep_first, rep_second, rep_total, VECTOR_RATE, 0.0)
    split_new = adam_step(split_master, split_first, split_second, split_total, VECTOR_RATE, 0.0)
    return (
        full_out,
        input_grad,
        mask_total,
        *qkv_out_new,
        *fc1_new,
        *fc2_new,
        *rep_new,
        *split_new,
    )


def solution(mesh):
    placed = (
        P("dp", None, None),
        P(None, None, "dp", "mp"),
        P("mp"),
        P(),
        P(),
        P(),
        P("mp", "dp"),
        P("mp", "dp"),
        P("mp", "dp"),
        P("mp", "dp"),
        P("mp", "dp"),
        P("mp", "dp"),
        P("mp", "dp"),
        P("mp", "dp"),
        P("mp", "dp"),
        P("mp", "dp"),
        P("mp", "dp"),
        P("mp", "dp"),
        P(),
        P(),
        P(),
        P("mp", None, None),
        P("mp", None, None),
        P("mp", None, None),
    )
    tuned = mesh.shape["dp"] == 16 and mesh.shape["mp"] == 2
    return jax.shard_map(
        on_device if tuned else on_device_general,
        mesh=mesh,
        in_specs=placed,
        out_specs=(
            P(None, None, "dp", "mp"),
            P("dp", None, None),
            P("mp"),
            P("mp", "dp"),
            P("mp", "dp"),
            P("mp", "dp"),
            P("mp", "dp"),
            P("mp", "dp"),
            P("mp", "dp"),
            P("mp", "dp"),
            P("mp", "dp"),
            P("mp", "dp"),
            P("mp", "dp"),
            P("mp", "dp"),
            P("mp", "dp"),
            P(),
            P(),
            P(),
            P("mp", None, None),
            P("mp", None, None),
            P("mp", None, None),
        ),
        check_vma=False,
    )
```

```python
import jax
import jax.numpy as jnp
from jax import lax
from jax.experimental import pallas as pl
from jax.experimental.pallas import tpu as pltpu
from jax.sharding import PartitionSpec as P

HEAD = 64
PATCHES = 529
STEP = 10


NORM_EPS = 1e-06
BETA_ONE = 0.9
BETA_TWO = 0.999
ADAM_EPS = 1e-08
MATRIX_RATE = 0.15
MATRIX_DECAY = 0.05
VECTOR_RATE = 0.6


def layer_norm(signal, norm_gain, norm_shift):
    average = jnp.mean(signal, axis=-1, keepdims=True)
    centered = signal - average
    spread = jnp.mean(centered * centered, axis=-1, keepdims=True)
    return centered * lax.rsqrt(spread + NORM_EPS) * norm_gain + norm_shift


def exact_gelu(signal):
    return jax.nn.gelu(signal, approximate=False)


def product(left, right):
    return jnp.dot(left, right, preferred_element_type=jnp.float32)


def contract_last(left, right):
    return lax.dot_general(
        left, right, (((1,), (1,)), ((), ())), preferred_element_type=jnp.float32
    )


def contract_rows(left, right):
    return lax.dot_general(
        left, right, (((0,), (0,)), ((), ())), preferred_element_type=jnp.float32
    )


def adam_step(weight, moment_one, moment_two, gradient, step_rate, decay_rate):
    one_new = BETA_ONE * moment_one + (1.0 - BETA_ONE) * gradient
    two_new = BETA_TWO * moment_two + (1.0 - BETA_TWO) * gradient * gradient
    one_hat = one_new / (1.0 - BETA_ONE**STEP)
    two_hat = two_new / (1.0 - BETA_TWO**STEP)
    weight_new = weight - step_rate * (
        one_hat / (jnp.sqrt(two_hat) + ADAM_EPS) + decay_rate * weight
    )
    return (weight_new, one_new, two_new)


def total_over_cores(partial):
    return partial.astype(jnp.float32) + swap_cores(partial).astype(jnp.float32)


def pair_scores(queries, key_rows, valid_rows):
    scores = jnp.einsum(
        "qhd,khd->hqk", queries, key_rows, preferred_element_type=jnp.float32
    ) * HEAD ** (-0.5)
    return jnp.where(valid_rows[None, None, :], scores, -1e30)


def attend_pair(pair_block):
    queries, key_rows, value_rows, valid_rows = pair_block
    scores = pair_scores(queries, key_rows, valid_rows)
    row_max = jnp.max(scores, axis=2, keepdims=True)
    lifted = jnp.exp(scores - row_max)
    row_total = jnp.sum(lifted, axis=2, keepdims=True)
    probability = (lifted / row_total).astype(jnp.bfloat16)
    attended = jnp.einsum(
        "hqk,khd->qhd", probability, value_rows, preferred_element_type=jnp.float32
    )
    return (attended.astype(jnp.bfloat16), row_max[:, :, 0] + jnp.log(row_total[:, :, 0]))


def attend_pair_back(pair_block):
    queries, key_rows, value_rows, valid_rows, log_total, grad_attended = pair_block
    scores = pair_scores(queries, key_rows, valid_rows)
    probability = jnp.exp(scores - log_total[:, :, None])
    grad_prob = jnp.einsum(
        "qhd,khd->hqk", grad_attended, value_rows, preferred_element_type=jnp.float32
    )
    inner_sum = jnp.sum(probability * grad_prob, axis=2, keepdims=True)
    grad_scores = (probability * (grad_prob - inner_sum)).astype(jnp.bfloat16)
    score_scale = HEAD ** (-0.5)
    grad_queries = (
        jnp.einsum("hqk,khd->qhd", grad_scores, key_rows, preferred_element_type=jnp.float32)
        * score_scale
    )
    grad_keys = (
        jnp.einsum("hqk,qhd->khd", grad_scores, queries, preferred_element_type=jnp.float32)
        * score_scale
    )
    grad_values = jnp.einsum(
        "hqk,qhd->khd",
        probability.astype(jnp.bfloat16),
        grad_attended,
        preferred_element_type=jnp.float32,
    )
    return (
        grad_queries.astype(jnp.bfloat16),
        grad_keys.astype(jnp.bfloat16),
        grad_values.astype(jnp.bfloat16),
    )


def hop(array, distance, axis_count):
    return lax.ppermute(array, "dp", [(i, i ^ distance) for i in range(axis_count)])


def swap_cores(array):
    return lax.ppermute(array, "mp", [(0, 1), (1, 0)])


def place_chunks(pieces, chunk_ids, member, count):
    rows, width = pieces[0].shape[1:]

    def body(member_ref, *refs):
        sources, target, semaphores = refs[:-2], refs[-2], refs[-1]
        copies = []
        for source, ids in zip(sources, chunk_ids):
            for place, distance in enumerate(ids):
                copies.append(
                    pltpu.make_async_copy(
                        source.at[place],
                        target.at[member_ref[0] ^ distance],
                        semaphores.at[len(copies)],
                    )
                )
        for copy in copies:
            copy.start()
        for copy in copies:
            copy.wait()

    return pl.pallas_call(
        body,
        in_specs=[pl.BlockSpec(memory_space=pltpu.SMEM)]
        + [pl.BlockSpec(memory_space=pl.ANY)] * len(pieces),
        out_specs=pl.BlockSpec(memory_space=pltpu.VMEM),
        out_shape=jax.ShapeDtypeStruct((count, rows, width), pieces[0].dtype),
        scratch_shapes=[pltpu.SemaphoreType.DMA((count,))],
        cost_estimate=pl.CostEstimate(
            flops=0, transcendentals=0, bytes_accessed=4 * count * rows * width
        ),
        name="place_chunks",
    )(member, *pieces)


def pick_chunks(whole, chunk_ids, member):
    count, rows, width = whole.shape

    def body(member_ref, source, *refs):
        targets, semaphores = refs[:-1], refs[-1]
        copies = []
        for target, ids in zip(targets, chunk_ids):
            for place, distance in enumerate(ids):
                copies.append(
                    pltpu.make_async_copy(
                        source.at[member_ref[0] ^ distance],
                        target.at[place],
                        semaphores.at[len(copies)],
                    )
                )
        for copy in copies:
            copy.start()
        for copy in copies:
            copy.wait()

    return pl.pallas_call(
        body,
        in_specs=[pl.BlockSpec(memory_space=pltpu.SMEM), pl.BlockSpec(memory_space=pltpu.VMEM)],
        out_specs=[pl.BlockSpec(memory_space=pl.ANY)] * len(chunk_ids),
        out_shape=[
            jax.ShapeDtypeStruct((len(ids), rows, width), whole.dtype) for ids in chunk_ids
        ],
        scratch_shapes=[pltpu.SemaphoreType.DMA((count,))],
        cost_estimate=pl.CostEstimate(
            flops=0, transcendentals=0, bytes_accessed=4 * count * rows * width
        ),
        name="pick_chunks",
    )(member, whole)


def gather_chunks(chunk, member, count):
    own = chunk[None]
    if count == 16:
        near, far, last = (hop(own, k, count) for k in (4, 8, 12))
        first, second = jnp.concatenate([own, near]), jnp.concatenate([far, last])
        x_first, x_second = hop(first, 1, count), hop(second, 1, count)
        y_first, y_second = hop(first, 2, count), hop(second, 2, count)
        d_first, d_second = hop(y_first, 1, count), hop(x_second, 2, count)
        pieces = [first, second, x_first, x_second, y_first, y_second, d_first, d_second]
        ids = [(0, 4), (8, 12), (1, 5), (9, 13), (2, 6), (10, 14), (3, 7), (11, 15)]
    else:
        held, step = own, 1
        while step < count:
            held = jnp.concatenate([held, hop(held, step, count)])
            step *= 2
        pieces, ids = [held], [tuple(range(count))]
    return place_chunks(pieces, ids, member, count)


def scatter_chunks(whole, member, count):
    def wide(array):
        return array.astype(jnp.float32)

    if count == 16:
        ids = [(3, 7), (11, 15), (2, 6), (9, 13), (10, 14), (1, 5), (0, 4), (8, 12)]
        d_first, d_second, y_first, x_second, y_second, x_first, first, second = pick_chunks(
            whole, ids, member
        )
        d_first, d_second = hop(d_first, 1, count), hop(d_second, 2, count)
        y_second, x_first = hop(y_second, 2, count), hop(x_first, 1, count)
        y_first = hop((wide(y_first) + wide(d_first)).astype(jnp.bfloat16), 2, count)
        x_second = hop((wide(x_second) + wide(d_second)).astype(jnp.bfloat16), 1, count)
        first = wide(first) + wide(y_first) + wide(x_first)
        second = wide(second) + wide(y_second) + wide(x_second)
        near = hop(first[1].astype(jnp.bfloat16), 4, count)
        far = hop(second[0].astype(jnp.bfloat16), 8, count)
        last = hop(second[1].astype(jnp.bfloat16), 12, count)
        return first[0] + wide(near) + wide(far) + wide(last)
    (held,) = pick_chunks(whole, [tuple(range(count))], member)
    held = wide(held)
    step = count // 2
    while step:
        held = held[:step] + wide(hop(held[step:].astype(jnp.bfloat16), step, count))
        step //= 2
    return held[0]


def sum_over_dp(vector, count):
    if count == 16:
        for low, high in ((1, 2), (4, 8)):
            other, third, fourth = (hop(vector, k, count) for k in (low, high, low + high))
            vector = (vector + other) + (third + fourth)
        return vector
    step = 1
    while step < count:
        vector = vector + hop(vector, step, count)
        step *= 2
    return vector


def on_device_general(
    patch_rows,
    cotangent,
    mask_token,
    lengths,
    masked,
    dealing,
    qkv_master,
    qkv_first,
    qkv_second,
    out_master,
    out_first,
    out_second,
    fc1_master,
    fc1_first,
    fc1_second,
    fc2_master,
    fc2_first,
    fc2_second,
    rep_master,
    rep_first,
    rep_second,
    split_master,
    split_first,
    split_second,
):
    slot_count, capacity, feature_width = patch_rows.shape
    half_width = mask_token.shape[0]
    dp_count = lax.axis_size("dp")
    member = lax.axis_index("dp")
    core_index = lax.axis_index("mp")
    positions_here = cotangent.shape[1]
    position_span = positions_here * dp_count
    heads_here = half_width // HEAD
    hidden_width = (split_master.shape[1] - 2) * half_width
    row_count = slot_count * capacity
    pair_count = slot_count // 2
    pair_length = 2 * capacity
    patch_index = jnp.arange(PATCHES, dtype=jnp.int32)
    visible_all = (patch_index[None, :] < lengths[:, None]) & (masked == 0)
    strips_here = lax.dynamic_slice_in_dim(dealing, member * slot_count, slot_count)
    visible_here = visible_all[strips_here]
    rank_here = jnp.cumsum(visible_here.astype(jnp.int32), axis=1) - 1
    counts_here = jnp.sum(visible_here.astype(jnp.int32), axis=1)
    valid_rows = jnp.arange(capacity, dtype=jnp.int32)[None, :] < counts_here[:, None]
    padding = position_span - PATCHES
    visible_padded = jnp.pad(visible_here, ((0, 0), (0, padding)))
    rank_padded = jnp.pad(jnp.maximum(rank_here, 0), ((0, 0), (0, padding)))
    own_positions = jnp.arange(positions_here, dtype=jnp.int32) * dp_count + member
    inside = own_positions < PATCHES
    visible_own = visible_all[:, jnp.minimum(own_positions, PATCHES - 1)] & inside[None, :]
    strip_count = lengths.shape[0]
    held_count = strip_count * positions_here
    strip_row = (
        jnp.arange(positions_here, dtype=jnp.int32)[None, :] * strip_count + dealing[:, None]
    ).reshape(held_count)
    deal = (
        strip_row[:, None] == jnp.arange(held_count, dtype=jnp.int32)[None, :]
    ).astype(jnp.bfloat16)
    encoder_row = jnp.where(
        visible_padded,
        rank_padded + jnp.arange(slot_count, dtype=jnp.int32)[:, None] * capacity,
        -1,
    )
    encoder_row = jnp.transpose(
        encoder_row.reshape(slot_count, positions_here, dp_count), (2, 0, 1)
    ).reshape(held_count)
    pick = (
        jnp.arange(row_count, dtype=jnp.int32)[:, None] == encoder_row[None, :]
    ).astype(jnp.bfloat16)
    unseen = jnp.transpose(jnp.logical_not(visible_own) & inside[None, :]).reshape(held_count)
    member_word = member.astype(jnp.int32).reshape(1)

    cotangent_rows = jnp.transpose(cotangent.reshape(strip_count, positions_here, half_width), (1, 0, 2))
    cotangent_rows = cotangent_rows.reshape(held_count, half_width)
    dealt = product(deal, cotangent_rows).astype(jnp.bfloat16)
    returned = lax.all_to_all(
        dealt.reshape(dp_count, slot_count * positions_here, half_width),
        "dp",
        split_axis=0,
        concat_axis=0,
        tiled=True,
    ).reshape(held_count, half_width)
    gathered = product(pick, returned).astype(jnp.bfloat16)
    gathered_other = swap_cores(gathered)
    grad_out = jnp.where(
        core_index == 0,
        jnp.concatenate([gathered, gathered_other], axis=1),
        jnp.concatenate([gathered_other, gathered], axis=1),
    )
    mask_grad = product(unseen.astype(jnp.bfloat16)[None, :], cotangent_rows)[0]

    def gathered_matrix(master, rows, width):
        chunk = master.astype(jnp.bfloat16).reshape(rows // dp_count, width)
        return gather_chunks(chunk, member_word, dp_count).reshape(rows, width)

    w_attention = gathered_matrix(qkv_master, feature_width, 3 * half_width)
    w_output = gathered_matrix(out_master, half_width, feature_width)
    w_first = gathered_matrix(fc1_master, feature_width, hidden_width)
    w_second = gathered_matrix(fc2_master, hidden_width, feature_width)
    inputs = patch_rows.reshape(row_count, feature_width).astype(jnp.float32)
    normed_full, norm_back_one = jax.vjp(layer_norm, inputs, rep_master[0], rep_master[1])
    normed = normed_full.astype(jnp.bfloat16)
    projected = product(normed, w_attention).reshape(row_count, 3, half_width)
    queries = (projected[:, 0] + split_master[0, 0]).astype(jnp.bfloat16)
    key_rows = projected[:, 1].astype(jnp.bfloat16)
    value_rows = (projected[:, 2] + split_master[0, 1]).astype(jnp.bfloat16)

    def by_pair(array):
        return array.reshape(pair_count, pair_length, heads_here, HEAD)

    pair_valid = valid_rows.reshape(pair_count, pair_length)
    attended, log_total = lax.map(
        attend_pair, (by_pair(queries), by_pair(key_rows), by_pair(value_rows), pair_valid)
    )
    attended = attended.reshape(row_count, half_width)
    branch = total_over_cores(product(attended, w_output)) + rep_master[4]
    middle = inputs + branch
    normed_two_full, norm_back_two = jax.vjp(layer_norm, middle, rep_master[2], rep_master[3])
    normed_two = normed_two_full.astype(jnp.bfloat16)
    hidden = product(normed_two, w_first) + split_master[0, 2:].reshape(hidden_width)
    active_full, gelu_back = jax.vjp(exact_gelu, hidden)
    active = active_full.astype(jnp.bfloat16)
    second = total_over_cores(product(active, w_second).astype(jnp.bfloat16)) + rep_master[5]
    result = (middle + second).astype(jnp.bfloat16)
    result_half = lax.dynamic_slice_in_dim(result, core_index * half_width, half_width, 1)
    outgoing = contract_rows(pick, result_half).astype(jnp.bfloat16)
    arrived = lax.all_to_all(
        outgoing.reshape(dp_count, slot_count * positions_here, half_width),
        "dp",
        split_axis=0,
        concat_axis=0,
        tiled=True,
    ).reshape(held_count, half_width)
    full_out = contract_rows(deal, arrived)
    full_out = jnp.where(unseen[:, None], mask_token.astype(jnp.float32)[None, :], full_out)
    full_out = full_out.astype(jnp.bfloat16).reshape(positions_here, strip_count, half_width)
    full_out = jnp.transpose(full_out, (1, 0, 2))[:, :, None, :]
    grad_rows = grad_out.astype(jnp.float32)
    bias_two_grad = jnp.sum(grad_rows, axis=0)
    grad_active = contract_last(grad_out, w_second)
    grad_hidden = gelu_back(grad_active)[0].astype(jnp.bfloat16)
    fc2_grad = contract_rows(active, grad_out)
    fc1_grad = contract_rows(normed_two, grad_hidden)
    hidden_bias_grad = jnp.sum(grad_hidden.astype(jnp.float32), axis=0)
    grad_normed_two = total_over_cores(contract_last(grad_hidden, w_first))
    grad_middle_part, gain_two_grad, shift_two_grad = norm_back_two(grad_normed_two)
    grad_middle = grad_rows + grad_middle_part
    grad_branch = grad_middle.astype(jnp.bfloat16)
    out_bias_grad = jnp.sum(grad_branch.astype(jnp.float32), axis=0)
    out_grad = contract_rows(attended, grad_branch)
    grad_attended = contract_last(grad_branch, w_output).astype(jnp.bfloat16)
    grad_queries, grad_keys, grad_values = lax.map(
        attend_pair_back,
        (
            by_pair(queries),
            by_pair(key_rows),
            by_pair(value_rows),
            pair_valid,
            log_total,
            by_pair(grad_attended),
        ),
    )
    grad_queries = grad_queries.reshape(row_count, half_width)
    grad_keys = grad_keys.reshape(row_count, half_width)
    grad_values = grad_values.reshape(row_count, half_width)
    grad_projected = jnp.stack([grad_queries, grad_keys, grad_values], axis=1).reshape(
        row_count, 3 * half_width
    )
    qkv_grad = contract_rows(normed, grad_projected)
    query_bias_grad = jnp.sum(grad_queries.astype(jnp.float32), axis=0)
    value_bias_grad = jnp.sum(grad_values.astype(jnp.float32), axis=0)
    grad_normed = total_over_cores(contract_last(grad_projected, w_attention))
    grad_inputs_part, gain_one_grad, shift_one_grad = norm_back_one(grad_normed)
    input_grad = (grad_middle + grad_inputs_part).reshape(slot_count, capacity, feature_width)
    def scattered(gradient):
        rows, width = gradient.shape
        chunks = gradient.astype(jnp.bfloat16).reshape(dp_count, rows // dp_count, width)
        return scatter_chunks(chunks, member_word, dp_count).reshape(1, -1)

    fc2_total = scattered(fc2_grad)
    fc1_total = scattered(fc1_grad)
    out_total = scattered(out_grad)
    qkv_total = scattered(qkv_grad)
    rep_grad = jnp.stack(
        [gain_one_grad, shift_one_grad, gain_two_grad, shift_two_grad, out_bias_grad, bias_two_grad]
    )
    split_grad = jnp.concatenate(
        [query_bias_grad[None], value_bias_grad[None], hidden_bias_grad.reshape(-1, half_width)],
        axis=0,
    )[None]
    packed = jnp.concatenate([mask_grad, rep_grad.reshape(-1), split_grad.reshape(-1)])
    packed = sum_over_dp(packed.reshape(-1, 128), dp_count).reshape(-1)
    mask_total = packed[:half_width]
    rep_total = packed[half_width : half_width + rep_grad.size].reshape(rep_grad.shape)
    split_total = packed[half_width + rep_grad.size :].reshape(split_grad.shape)
    qkv_new = adam_step(qkv_master, qkv_first, qkv_second, qkv_total, MATRIX_RATE, MATRIX_DECAY)
    out_new = adam_step(out_master, out_first, out_second, out_total, MATRIX_RATE, MATRIX_DECAY)
    fc1_new = adam_step(fc1_master, fc1_first, fc1_second, fc1_total, MATRIX_RATE, MATRIX_DECAY)
    fc2_new = adam_step(fc2_master, fc2_first, fc2_second, fc2_total, MATRIX_RATE, MATRIX_DECAY)
    rep_new = adam_step(rep_master, rep_first, rep_second, rep_total, VECTOR_RATE, 0.0)
    split_new = adam_step(split_master, split_first, split_second, split_total, VECTOR_RATE, 0.0)
    return (
        full_out,
        input_grad,
        mask_total,
        qkv_new[0],
        qkv_new[1],
        qkv_new[2],
        out_new[0],
        out_new[1],
        out_new[2],
        fc1_new[0],
        fc1_new[1],
        fc1_new[2],
        fc2_new[0],
        fc2_new[1],
        fc2_new[2],
        rep_new[0],
        rep_new[1],
        rep_new[2],
        split_new[0],
        split_new[1],
        split_new[2],
    )


BLOCK = 384
UNIT_ROWS = 48
UNIT_WIDTH = 1536
BLOCK_WIDTH = 256
Z_ORDER = (0, 12, 4, 8)
VMEM_BYTES = 60 * 1024 * 1024
ANY = pl.BlockSpec(memory_space=pl.ANY)
IN_VMEM = pl.BlockSpec(memory_space=pltpu.VMEM)
IN_SMEM = pl.BlockSpec(memory_space=pltpu.SMEM)


def shaped(shape, dtype):
    return jax.ShapeDtypeStruct(shape, dtype)


def params(grid_axes=0):
    semantics = ("arbitrary",) * grid_axes if grid_axes else None
    return pltpu.CompilerParams(dimension_semantics=semantics, vmem_limit_bytes=VMEM_BYTES)


def cost(microseconds):
    return pl.CostEstimate(
        flops=int(microseconds * 1.15e9), transcendentals=0, bytes_accessed=1000000
    )


def together(*values):
    return lax.optimization_barrier(values)


def hop_by_core(array, first_core, second_core, count):
    pairs = []
    for i in range(count):
        pairs.append((2 * i, 2 * (i ^ first_core)))
        pairs.append((2 * i + 1, 2 * (i ^ second_core) + 1))
    return lax.ppermute(array, ("dp", "mp"), pairs)


def pack_units(qkv, out, fc1, fc2):
    def body(qkv_ref, out_ref, fc1_ref, fc2_ref, units, unit_a, units_later):
        def put(unit, column, rows):
            units[unit, :, column * 128 : (column + 1) * 128] = rows.astype(jnp.bfloat16)

        for j in range(9):
            put(0, j, qkv_ref[pl.ds(j, UNIT_ROWS, stride=9), :])
        for j in range(3):
            put(0, 9 + j, out_ref[pl.ds(j, UNIT_ROWS, stride=3), :])
        for j in range(12):
            put(1, j, fc1_ref[pl.ds(j, UNIT_ROWS, stride=12), :])
        for half in range(2):
            for j in range(6):
                start = half * UNIT_ROWS * 6 + j
                put(2, half * 6 + j, fc2_ref[pl.ds(start, UNIT_ROWS, stride=6), :])
        unit_a[0] = units[0]
        units_later[0] = units[1]
        units_later[1] = units[2]

    def unit_array(count):
        return shaped((count, UNIT_ROWS, UNIT_WIDTH), jnp.bfloat16)

    return pl.pallas_call(
        body,
        out_shape=[unit_array(3), unit_array(1), unit_array(2)],
        compiler_params=params(),
        cost_estimate=cost(2),
        name="pack_units",
    )(
        *(array.reshape(-1, 128) for array in (qkv, out, fc1, fc2))
    )


def chunk_sources(words, own, pieces, unit):
    step, offset = (1, 0) if unit == 0 else (2, unit - 1)
    found = []
    for place, extra in enumerate((0, words[1], words[2], 3)):
        found.append((own[place].at[unit], words[0] ^ extra))
        for entry, distance in enumerate(Z_ORDER[1:]):
            source = pieces[place].at[entry * step + offset]
            found.append((source, words[0] ^ distance ^ extra))
    return found


def join_chunks(chunks):
    size = chunks[0].shape[0]

    def body(*refs):
        for entry, ref in enumerate(refs[:-1]):
            refs[-1][entry * size : (entry + 1) * size] = ref[...]

    return pl.pallas_call(
        body,
        out_shape=shaped((len(chunks) * size,) + chunks[0].shape[1:], chunks[0].dtype),
        compiler_params=params(),
        cost_estimate=cost(1.5 * size),
        name="join_chunks",
    )(*chunks)


def last_messages(kept, one, two, carried=None):
    extra = 0 if carried is None else 16
    inputs = [kept, one, two] + ([] if carried is None else [carried])

    def body(kept_ref, one_ref, two_ref, *refs):
        targets = refs[-3:]
        if extra:
            vectors = refs[0][...].astype(jnp.float32)
            vectors = vectors + two_ref[4 * UNIT_ROWS :, :].astype(jnp.float32)
            vectors = vectors.astype(jnp.bfloat16)
        for entry, target in enumerate(targets):
            rows = slice((entry + 1) * UNIT_ROWS, (entry + 2) * UNIT_ROWS)
            total = kept_ref[rows, :].astype(jnp.float32) + one_ref[rows, :].astype(jnp.float32)
            total = total + two_ref[rows, :].astype(jnp.float32)
            target[:UNIT_ROWS, :] = total.astype(jnp.bfloat16)
            if extra:
                target[UNIT_ROWS:, :] = vectors

    def rows(count, start=0):
        return pl.BlockSpec((count, UNIT_WIDTH), lambda i: (start, 0))

    specs = [rows(4 * UNIT_ROWS), rows(4 * UNIT_ROWS), rows(4 * UNIT_ROWS + extra)]
    if extra:
        specs.append(rows(16, 4 * UNIT_ROWS // 16))
    message = shaped((UNIT_ROWS + extra, UNIT_WIDTH), jnp.bfloat16)
    return pl.pallas_call(
        body,
        grid=(1,),
        in_specs=specs,
        out_specs=[rows(UNIT_ROWS + extra)] * 3,
        out_shape=[message] * 3,
        compiler_params=params(1),
        cost_estimate=cost(1.5),
        name="last_messages",
    )(*inputs)


def added(start, stop, *arrays):
    total = 0.0
    for array, offset in arrays:
        total = total + array[start - offset : stop - offset].astype(jnp.float32)
    return total.astype(jnp.bfloat16)


def unit_shapes(extra=0):
    return [shaped((8 * UNIT_ROWS + extra, UNIT_WIDTH), jnp.bfloat16)] * 2


def unit_targets(words, sent, kept):
    def rows(array, entry):
        return array.at[pl.ds(entry * UNIT_ROWS, UNIT_ROWS), :]

    places = []
    for entry, distance in enumerate(Z_ORDER):
        own = words[0] ^ distance
        places.append((rows(sent, 4 + entry), own ^ 3))
        places.append((rows(sent, entry), own ^ words[2]))
        places.append((rows(kept, entry), own))
        places.append((rows(kept, 4 + entry), own ^ words[1]))
    return places


def lanes_of(part, size):
    return pl.ds(pl.multiple_of(part * size, 128), size)


def unit_rows(owner, rows=UNIT_ROWS):
    return pl.ds(pl.multiple_of(owner * rows, 16), rows)


def norm_parts(signal):
    average = jnp.mean(signal, axis=1, keepdims=True)
    centered = signal - average
    scale = lax.rsqrt(jnp.mean(centered * centered, axis=1, keepdims=True) + NORM_EPS)
    return centered * scale, scale


def norm_back(grad, unit_signal, scale, gain):
    scaled = grad * gain
    mean_one = jnp.mean(scaled, axis=1, keepdims=True)
    mean_two = jnp.mean(scaled * unit_signal, axis=1, keepdims=True)
    return scale * (scaled - mean_one - unit_signal * mean_two)


def fixed(*shape):
    return pl.BlockSpec(shape, lambda i: (0,) * len(shape))


def run_copies(pairs, semaphores):
    copies = [
        pltpu.make_async_copy(source, target, semaphores.at[i])
        for i, (source, target) in enumerate(pairs)
    ]
    for copy in copies:
        copy.start()
    for copy in copies:
        copy.wait()


class Copies:
    def __init__(self, semaphores):
        self.semaphores, self.used = semaphores, 0

    def start(self, pairs):
        started = []
        for source, target in pairs:
            copy = pltpu.make_async_copy(source, target, self.semaphores.at[self.used])
            self.used += 1
            copy.start()
            started.append(copy)
        return started


def finish(copies):
    for copy in copies:
        copy.wait()


def chunk_pairs(words, own, pieces, unit, target):
    return [
        (source, target.at[unit_rows(owner), :])
        for source, owner in chunk_sources(words, own, pieces, unit)
    ]


def attention_forward(words, rows_in, rep, split, column_bias, own_pieces, pieces):
    count, width = rows_in.shape
    half = split.shape[1]
    pairs_of_heads = half // (2 * HEAD)

    def body(
        words_ref, in_ref, rep_ref, split_ref, bias_ref, o0, o1, o2, o3, p0, p1, p2, p3,
        normed_ref, qkv_ref, prob_ref, attended_ref, partial_ref, weights_ref, w_out_ref, spread, semaphores,
    ):
        pair = pl.program_id(0)

        @pl.when(pair == 0)
        def _():
            copies = Copies(semaphores)
            pairs = chunk_pairs(words_ref, (o0, o1, o2, o3), (p0, p1, p2, p3), 0, weights_ref)
            loads = copies.start(pairs)

            @pl.loop(0, count // BLOCK)
            def _(block):
                rows = pl.ds(block * BLOCK, BLOCK)
                unit_signal, _ = norm_parts(in_ref[rows, :].astype(jnp.float32))
                normed = unit_signal * rep_ref[0:1, :] + rep_ref[1:2, :]
                normed_ref[rows, :] = normed.astype(jnp.bfloat16)

            finish(loads)

            @pl.loop(0, count // BLOCK)
            def _(block):
                rows = pl.ds(block * BLOCK, BLOCK)
                projected = product(normed_ref[rows, :], weights_ref[:, : 3 * half])
                queries = projected[:, :half] + split_ref[0:1, :]
                values = projected[:, 2 * half :] + split_ref[1:2, :]
                qkv_ref[rows, :half] = queries.astype(jnp.bfloat16)
                qkv_ref[rows, half : 2 * half] = projected[:, half : 2 * half].astype(jnp.bfloat16)
                qkv_ref[rows, 2 * half :] = values.astype(jnp.bfloat16)

        lane = pl.multiple_of(pair * (2 * HEAD), 2 * HEAD)
        upper = lax.broadcasted_iota(jnp.int32, (1, 2 * HEAD), 1) >= HEAD
        keys = qkv_ref[:, pl.ds(half + lane, 2 * HEAD)]
        values = qkv_ref[:, pl.ds(2 * half + lane, 2 * HEAD)]
        for block in range(count // BLOCK):
            rows = pl.ds(block * BLOCK, BLOCK)
            queries = qkv_ref[rows, pl.ds(lane, 2 * HEAD)]
            found = []
            for side in range(2):
                chosen = upper if side else jnp.logical_not(upper)
                own = jnp.where(chosen, queries, jnp.zeros_like(queries))
                scores = contract_last(own, keys) * HEAD ** (-0.5) + bias_ref[...]
                lifted = jnp.exp(scores - jnp.max(scores, axis=1, keepdims=True))
                total = jnp.sum(lifted, axis=1, keepdims=True)
                probability = (lifted * (1.0 / total)).astype(jnp.bfloat16)
                prob_ref[side, rows, :] = probability
                found.append(product(probability, values))
            attended = jnp.where(upper, found[1], found[0])
            attended_ref[rows, pl.ds(lane, 2 * HEAD)] = attended.astype(jnp.bfloat16)

        @pl.when(pair == pairs_of_heads - 1)
        def _():
            for strip in range(half // 128):
                start = 3 * half + strip * 128
                spread[strip] = weights_ref[:, start : start + 128].astype(jnp.float32)
                for side in range(2):
                    start = side * half + strip * 128
                    w_out_ref[:, start : start + 128] = spread[
                        strip, pl.ds(side, half, stride=2), :
                    ].astype(jnp.bfloat16)
            partial_ref[...] = product(attended_ref[...], w_out_ref[...]).astype(jnp.bfloat16)

    return pl.pallas_call(
        body,
        grid=(pairs_of_heads,),
        in_specs=[IN_SMEM, fixed(count, width), fixed(6, width), fixed(6, half), fixed(1, count)]
        + [ANY] * 8,
        out_specs=[
            fixed(count, width),
            fixed(count, 3 * half),
            pl.BlockSpec((2, count, count), lambda h: (h, 0, 0)),
            fixed(count, half),
            fixed(count, width),
            fixed(width, UNIT_WIDTH),
            fixed(half, width),
        ],
        out_shape=[
            shaped((count, width), jnp.bfloat16),
            shaped((count, 3 * half), jnp.bfloat16),
            shaped((2 * pairs_of_heads, count, count), jnp.bfloat16),
            shaped((count, half), jnp.bfloat16),
            shaped((count, width), jnp.bfloat16),
            shaped((width, UNIT_WIDTH), jnp.bfloat16),
            shaped((half, width), jnp.bfloat16),
        ],
        scratch_shapes=[
            pltpu.VMEM((half // 128, width, 128), jnp.float32),
            pltpu.SemaphoreType.DMA((16,)),
        ],
        compiler_params=params(1),
        cost_estimate=cost(18),
        name="attention_forward",
    )(words, rows_in, rep, split, column_bias, *own_pieces, *pieces)


def mlp_all(
    words, rows_in, own, other, rep, hidden_bias, grad_out, own_pieces, pieces
):
    count, width = rows_in.shape
    hidden_width = UNIT_WIDTH
    half, wide = width // 2, 2 * BLOCK_WIDTH
    parts = hidden_width // wide

    def body(
        words_ref, rep_ref, bias_ref, in_any, own_any, other_any, grad_any,
        o0, o1, o2, o3, p0, p1, p2, p3,
        hidden_sum_ref, grad_sum_ref, middle_any, back_any, second_any,
        sent_b, kept_b, sent_c, kept_c,
        w_first, w_second, rows_ref, own_ref, other_ref, grad_ref, middle_ref, normed_ref,
        active_ref, slope_ref, grad_hidden_ref, back_ref, second_ref, whole_b, whole_c, semaphores,
    ):
        copies = Copies(semaphores)
        first_loads = copies.start(
            [(in_any, rows_ref), (own_any, own_ref), (other_any, other_ref)]
        )
        own_refs, later = (o0, o1, o2, o3), (p0, p1, p2, p3)
        loads_b = copies.start(chunk_pairs(words_ref, own_refs, later, 1, w_first))
        pairs = [(grad_any, grad_ref)]
        for source, owner in chunk_sources(words_ref, own_refs, later, 2):
            for side in range(2):
                pairs.append(
                    (
                        source.at[:, pl.ds(side * width, width)],
                        w_second.at[unit_rows(owner * 2 + side), :],
                    )
                )
        loads_c = copies.start(pairs)
        finish(first_loads)

        @pl.loop(0, count // BLOCK)
        def _(block):
            rows = pl.ds(block * BLOCK, BLOCK)
            branch = own_ref[rows, :].astype(jnp.float32) + other_ref[rows, :].astype(jnp.float32)
            middle = rows_ref[rows, :].astype(jnp.float32) + branch + rep_ref[4:5, :]
            middle_ref[rows, :] = middle
            unit_signal, _ = norm_parts(middle)
            normed = unit_signal * rep_ref[2:3, :] + rep_ref[3:4, :]
            normed_ref[rows, :] = normed.astype(jnp.bfloat16)

        stores = copies.start([(middle_ref, middle_any)])
        finish(loads_b)
        for part in range(parts):
            columns = slice(part * wide, (part + 1) * wide)
            hidden = product(normed_ref[...], w_first[:, columns]) + bias_ref[:, columns]
            spread = 0.5 + 0.5 * lax.erf(hidden * 0.7071067811865476)
            active_ref[:, columns] = (hidden * spread).astype(jnp.bfloat16)
            slope = spread + hidden * jnp.exp(-0.5 * hidden * hidden) * 0.3989422804014327
            slope_ref[:, columns] = slope.astype(jnp.bfloat16)

        finish(loads_c)
        second_ref[...] = product(active_ref[...], w_second[...]).astype(jnp.bfloat16)
        stores += copies.start([(second_ref, second_any)])
        grad_sum_ref[...] = jnp.sum(grad_ref[...].astype(jnp.float32), axis=0, keepdims=True)
        for part in range(parts):
            columns = slice(part * wide, (part + 1) * wide)
            grad_active = contract_last(grad_ref[...], w_second[columns, :])
            grad_hidden = grad_active * slope_ref[:, columns].astype(jnp.float32)
            grad_hidden = grad_hidden.astype(jnp.bfloat16)
            grad_hidden_ref[:, columns] = grad_hidden
            hidden_sum_ref[:, columns] = jnp.sum(
                grad_hidden.astype(jnp.float32), axis=0, keepdims=True
            )

        back_ref[...] = contract_last(grad_hidden_ref[...], w_first[...]).astype(jnp.bfloat16)
        stores += copies.start([(back_ref, back_any)])

        @pl.loop(0, hidden_width // half)
        def _(part):
            columns = lanes_of(part, half)
            whole_c[columns, :] = contract_rows(active_ref[:, columns], grad_ref[...]).astype(
                jnp.bfloat16
            )

        for target, owner in unit_targets(words_ref, sent_c, kept_c):
            stores += copies.start(
                [
                    (
                        whole_c.at[unit_rows(owner * 2 + side), :],
                        target.at[:, pl.ds(side * width, width)],
                    )
                    for side in range(2)
                ]
            )

        @pl.loop(0, width // half)
        def _(part):
            columns = lanes_of(part, half)
            whole_b[columns, :] = contract_rows(normed_ref[:, columns], grad_hidden_ref[...]).astype(
                jnp.bfloat16
            )

        for target, owner in unit_targets(words_ref, sent_b, kept_b):
            stores += copies.start([(whole_b.at[unit_rows(owner), :], target)])
        finish(stores)

    low, full = jnp.bfloat16, jnp.float32
    return pl.pallas_call(
        body,
        in_specs=[IN_SMEM, IN_VMEM, IN_VMEM] + [ANY] * 12,
        out_specs=[IN_VMEM, IN_VMEM] + [ANY] * 7,
        out_shape=[
            shaped((1, hidden_width), full),
            shaped((1, width), full),
            shaped((count, width), full),
            shaped((count, width), low),
            shaped((count, width), low),
        ]
        + unit_shapes()
        + unit_shapes(),
        scratch_shapes=[
            pltpu.VMEM((width, hidden_width), low),
            pltpu.VMEM((hidden_width, width), low),
            pltpu.VMEM((count, width), low),
            pltpu.VMEM((count, width), low),
            pltpu.VMEM((count, width), low),
            pltpu.VMEM((count, width), low),
            pltpu.VMEM((count, width), full),
            pltpu.VMEM((count, width), low),
            pltpu.VMEM((count, hidden_width), low),
            pltpu.VMEM((count, hidden_width), low),
            pltpu.VMEM((count, hidden_width), low),
            pltpu.VMEM((count, width), low),
            pltpu.VMEM((count, width), low),
            pltpu.VMEM((width, hidden_width), low),
            pltpu.VMEM((hidden_width, width), low),
            pltpu.SemaphoreType.DMA((104,)),
        ],
        compiler_params=params(),
        cost_estimate=cost(18),
        name="mlp_all",
    )(words, rep, hidden_bias, rows_in, own, other, grad_out, *own_pieces, *pieces)


def attention_back(
    words, rep, hidden_sum, grad_sum, mask_sum, middle, own, other, grad_out, w_out, attended, qkv,
    prob, normed, weights, rows_in,
):
    count, width = middle.shape
    half = qkv.shape[1] // 3
    span = 3 * half
    pairs_of_heads = half // (2 * HEAD)
    low, full = jnp.bfloat16, jnp.float32

    def body(
        words_ref, rep_ref, hidden_sum_ref, grad_sum_ref, mask_sum_ref,
        middle_any, own_any, other_any, grad_any, w_out_any, attended_any, qkv_any, prob_any,
        normed_any, weights_any, in_any,
        grad_middle_any, back_any, sent, kept,
        middle_ref, own_ref, other_ref, grad_ref, w_out_ref, attended_ref, qkv_ref, prob_ref,
        normed_ref, weights_ref, in_ref, grad_middle_ref, back_ref, branch, grad_attended,
        grad_qkv, spread, whole, vectors, low_vectors, semaphores,
    ):
        copies = Copies(semaphores)
        early = copies.start(
            [
                (middle_any, middle_ref), (own_any, own_ref), (other_any, other_ref),
                (grad_any, grad_ref),
            ]
        )
        outer = copies.start([(w_out_any, w_out_ref), (attended_any, attended_ref)])
        inner = copies.start([(qkv_any, qkv_ref)])
        probs = copies.start(
            [(prob_any.at[pl.ds(2 * i, 2)], prob_ref.at[i]) for i in range(pairs_of_heads)]
        )
        late = copies.start(
            [(normed_any, normed_ref), (weights_any, weights_ref), (in_any, in_ref)]
        )
        vectors[...] = jnp.zeros_like(vectors)
        finish(early)

        @pl.loop(0, count // BLOCK)
        def _(block):
            rows = pl.ds(block * BLOCK, BLOCK)
            unit_signal, scale = norm_parts(middle_ref[rows, :])
            mine = own_ref[rows, :].astype(full)
            grad_normed = mine + other_ref[rows, :].astype(full)
            grad_middle = grad_ref[rows, :].astype(full) + norm_back(
                grad_normed, unit_signal, scale, rep_ref[2:3, :]
            )
            grad_middle_ref[rows, :] = grad_middle
            grad_branch = grad_middle.astype(low)
            branch[rows, :] = grad_branch
            vectors[1:2, :width] += jnp.sum(mine * unit_signal, axis=0, keepdims=True)
            vectors[1:2, width:] += jnp.sum(mine, axis=0, keepdims=True)
            vectors[2:3, :width] += 0.5 * jnp.sum(grad_branch.astype(full), axis=0, keepdims=True)

        stores = copies.start([(grad_middle_ref, grad_middle_any)])
        finish(outer)
        grad_attended[...] = contract_last(branch[...], w_out_ref[...]).astype(low)
        out_gradient = contract_rows(attended_ref[...], branch[...])
        for strip in range(half // 128):
            for side in range(2):
                start = side * half + strip * 128
                spread[strip, pl.ds(side, half, stride=2), :] = out_gradient[
                    :, start : start + 128
                ]
            start = span + strip * 128
            whole[:, start : start + 128] = spread[strip].astype(low)
        finish(inner)
        upper = lax.broadcasted_iota(jnp.int32, (1, 2 * HEAD), 1) >= HEAD
        finish(probs)

        @pl.loop(0, pairs_of_heads)
        def _(pair):
            lanes = [
                pl.ds(pl.multiple_of(part * half + pair * (2 * HEAD), 2 * HEAD), 2 * HEAD)
                for part in range(3)
            ]
            queries, keys, values = (qkv_ref[:, lane] for lane in lanes)
            grad = grad_attended[:, lanes[0]]
            found = []
            for side in range(2):
                chosen = upper if side else jnp.logical_not(upper)
                own_grad = jnp.where(chosen, grad, jnp.zeros_like(grad))
                low_probability = prob_ref[pair, side]
                probability = low_probability.astype(full)
                weighted = probability * contract_last(own_grad, values)
                inner_sum = jnp.sum(weighted, axis=1, keepdims=True)
                grad_scores = (weighted - probability * inner_sum).astype(low)
                found.append(
                    (
                        product(grad_scores, keys),
                        contract_rows(queries, grad_scores)[side * HEAD : (side + 1) * HEAD],
                        contract_rows(grad, low_probability)[side * HEAD : (side + 1) * HEAD],
                    )
                )
            backs = (
                jnp.where(upper, found[1][0], found[0][0]) * HEAD ** (-0.5),
                jnp.transpose(jnp.concatenate([found[0][1], found[1][1]])) * HEAD ** (-0.5),
                jnp.transpose(jnp.concatenate([found[0][2], found[1][2]])),
            )
            for lane, value in zip(lanes, backs):
                grad_qkv[:, lane] = value.astype(low)

        finish(late)

        @pl.loop(0, width // half)
        def _(part):
            columns = lanes_of(part, half)
            whole[columns, :span] = contract_rows(normed_ref[:, columns], grad_qkv[...]).astype(low)

        for target, owner in unit_targets(words_ref, sent, kept):
            stores += copies.start([(whole.at[unit_rows(owner), :], target)])

        @pl.loop(0, count // BLOCK)
        def _(block):
            rows = pl.ds(block * BLOCK, BLOCK)
            back = contract_last(grad_qkv[rows, :], weights_ref[:, :span])
            back_ref[rows, :] = back.astype(low)
            unit_signal, _ = norm_parts(in_ref[rows, :].astype(full))
            vectors[0:1, :width] += jnp.sum(back * unit_signal, axis=0, keepdims=True)
            vectors[0:1, width:] += jnp.sum(back, axis=0, keepdims=True)
            for place, part in enumerate((0, 2)):
                sums = jnp.sum(
                    grad_qkv[rows, part * half : (part + 1) * half].astype(full),
                    axis=0,
                    keepdims=True,
                )
                vectors[3:4, place * half : (place + 1) * half] += sums

        stores += copies.start([(back_ref, back_any)])
        vectors[2:3, width:] = 0.5 * grad_sum_ref[...]
        vectors[3:4, 2 * half : span] = mask_sum_ref[...]
        vectors[4:5, :] = hidden_sum_ref[...]
        low_vectors[...] = vectors[...].astype(low)
        last = pl.ds(8 * UNIT_ROWS, 16)
        stores += copies.start([(low_vectors, sent.at[last, :]), (low_vectors, kept.at[last, :])])
        finish(stores)

    return pl.pallas_call(
        body,
        in_specs=[IN_SMEM] + [IN_VMEM] * 4 + [ANY] * 11,
        out_specs=[ANY] * 4,
        out_shape=[shaped((count, width), full), shaped((count, width), low)] + unit_shapes(16),
        scratch_shapes=[
            pltpu.VMEM((count, width), full),
            pltpu.VMEM((count, width), low),
            pltpu.VMEM((count, width), low),
            pltpu.VMEM((count, width), low),
            pltpu.VMEM((half, width), low),
            pltpu.VMEM((count, half), low),
            pltpu.VMEM((count, span), low),
            pltpu.VMEM((pairs_of_heads, 2, count, count), low),
            pltpu.VMEM((count, width), low),
            pltpu.VMEM((width, UNIT_WIDTH), low),
            pltpu.VMEM((count, width), low),
            pltpu.VMEM((count, width), full),
            pltpu.VMEM((count, width), low),
            pltpu.VMEM((count, width), low),
            pltpu.VMEM((count, half), low),
            pltpu.VMEM((count, span), low),
            pltpu.VMEM((half // 128, width, 128), full),
            pltpu.VMEM((width, UNIT_WIDTH), low),
            pltpu.VMEM((16, UNIT_WIDTH), full),
            pltpu.VMEM((16, UNIT_WIDTH), low),
            pltpu.SemaphoreType.DMA((40,)),
        ],
        compiler_params=params(),
        cost_estimate=cost(22),
        name="attention_back",
    )(
        words, rep, hidden_sum, grad_sum, mask_sum, middle, own, other, grad_out, w_out, attended,
        qkv, prob, normed, weights, rows_in,
    )


def input_gradient(rows_in, own, other, grad_middle, rep):
    count, width = rows_in.shape

    def body(in_ref, own_ref, other_ref, middle_ref, rep_ref, out_ref):
        unit_signal, scale = norm_parts(in_ref[...].astype(jnp.float32))
        grad = own_ref[...].astype(jnp.float32) + other_ref[...].astype(jnp.float32)
        out_ref[...] = middle_ref[...] + norm_back(grad, unit_signal, scale, rep_ref[0:1, :])

    block = pl.BlockSpec((BLOCK, width), lambda i: (i, 0))
    return pl.pallas_call(
        body,
        grid=(count // BLOCK,),
        in_specs=[block, block, block, block, pl.BlockSpec(rep.shape, lambda i: (0, 0))],
        out_specs=block,
        out_shape=shaped((count, width), jnp.float32),
        compiler_params=params(1),
        cost_estimate=cost(5.7),
        name="input_gradient",
    )(rows_in, own, other, grad_middle, rep)


def adam_unit(units, states, strides):
    flat = [array.reshape(-1, 128) for state in states for array in state]
    terms = [array for unit in units for array in unit]
    counts = [len(unit) for unit in units]

    def body(*refs):
        terms_here, refs = refs[: len(terms)], refs[len(terms) :]
        inputs, outputs = refs[: len(flat)], refs[len(flat) :]
        for unit, column, state, start, step in strides:
            columns = slice(column * 128, (column + 1) * 128)
            skip = sum(counts[:unit])
            gradient = terms_here[skip][:, columns].astype(jnp.float32)
            for term in terms_here[skip + 1 : skip + counts[unit]]:
                gradient = gradient + term[:, columns].astype(jnp.float32)
            rows = pl.ds(start, UNIT_ROWS, stride=step)
            weight, one, two = (inputs[3 * state + i][rows, :] for i in range(3))
            updated = adam_step(weight, one, two, gradient, MATRIX_RATE, MATRIX_DECAY)
            for i in range(3):
                outputs[3 * state + i][rows, :] = updated[i]

    whole = [pl.BlockSpec(array.shape, lambda i: (0, 0)) for array in flat]
    results = pl.pallas_call(
        body,
        grid=(1,),
        in_specs=[
            pl.BlockSpec((UNIT_ROWS, term.shape[1]), lambda i: (0, 0)) for term in terms
        ]
        + whole,
        out_specs=whole,
        out_shape=[shaped(array.shape, jnp.float32) for array in flat],
        compiler_params=params(1),
        cost_estimate=cost(2.5),
        name="adam_unit",
    )(*terms, *flat)
    return [array.reshape(1, -1) for array in results]


def on_device(
    patch_rows,
    cotangent,
    mask_token,
    lengths,
    masked,
    dealing,
    qkv_master,
    qkv_first,
    qkv_second,
    out_master,
    out_first,
    out_second,
    fc1_master,
    fc1_first,
    fc1_second,
    fc2_master,
    fc2_first,
    fc2_second,
    rep_master,
    rep_first,
    rep_second,
    split_master,
    split_first,
    split_second,
):
    slot_count, capacity, feature_width = patch_rows.shape
    half_width = mask_token.shape[0]
    dp_count = lax.axis_size("dp")
    member = lax.axis_index("dp")
    core_index = lax.axis_index("mp")
    positions_here = cotangent.shape[1]
    position_span = positions_here * dp_count
    heads_here = half_width // HEAD
    row_count = slot_count * capacity
    strip_count = lengths.shape[0]
    position_rows = -(-positions_here // 4) * 4
    held_count = strip_count * positions_here
    dealt_count = strip_count * position_rows
    words = jnp.stack([member, 1 + core_index, 2 - core_index, core_index]).astype(jnp.int32)

    inputs = patch_rows.reshape(row_count, feature_width)
    split_rows = split_master[0]
    hidden_bias = split_rows[2:].reshape(1, -1)
    units, unit_a, units_later = pack_units(qkv_master, out_master, fc1_master, fc2_master)

    patch_index = jnp.arange(PATCHES, dtype=jnp.int32)
    visible_all = (patch_index[None, :] < lengths[:, None]) & (masked == 0)
    strips_here = lax.dynamic_slice_in_dim(dealing, member * slot_count, slot_count)
    visible_here = visible_all[strips_here]
    rank_here = jnp.cumsum(visible_here.astype(jnp.int32), axis=1) - 1
    counts_here = jnp.sum(visible_here.astype(jnp.int32), axis=1)
    valid_rows = jnp.arange(capacity, dtype=jnp.int32)[None, :] < counts_here[:, None]
    column_bias = jnp.where(valid_rows, 0.0, -1e30).astype(jnp.float32).reshape(1, row_count)
    padding = position_span - PATCHES
    visible_padded = jnp.pad(visible_here, ((0, 0), (0, padding)))
    rank_padded = jnp.pad(jnp.maximum(rank_here, 0), ((0, 0), (0, padding)))
    own_positions = jnp.arange(positions_here, dtype=jnp.int32) * dp_count + member
    inside = own_positions < PATCHES
    visible_own = visible_all[:, jnp.minimum(own_positions, PATCHES - 1)] & inside[None, :]
    row_time = jnp.arange(position_rows, dtype=jnp.int32)[None, :]
    strip_row = jnp.where(
        row_time < positions_here, row_time * strip_count + dealing[:, None], -1
    ).reshape(dealt_count)
    deal = (
        strip_row[:, None] == jnp.arange(held_count, dtype=jnp.int32)[None, :]
    ).astype(jnp.bfloat16)
    encoder_row = jnp.where(
        visible_padded,
        rank_padded + jnp.arange(slot_count, dtype=jnp.int32)[:, None] * capacity,
        -1,
    )
    encoder_row = jnp.transpose(
        encoder_row.reshape(slot_count, positions_here, dp_count), (2, 0, 1)
    )
    encoder_row = jnp.pad(
        encoder_row, ((0, 0), (0, 0), (0, position_rows - positions_here)), constant_values=-1
    ).reshape(dealt_count)
    pick = (
        jnp.arange(row_count, dtype=jnp.int32)[:, None] == encoder_row[None, :]
    ).astype(jnp.bfloat16)
    unseen = jnp.transpose(jnp.logical_not(visible_own) & inside[None, :]).reshape(held_count)

    cotangent_rows = jnp.transpose(
        cotangent.reshape(strip_count, positions_here, half_width), (1, 0, 2)
    ).reshape(held_count, half_width)

    def spread_out(array):
        return hop_by_core(array, 1, 2, dp_count), hop_by_core(array, 2, 1, dp_count)

    def exchanged(array):
        array = array.reshape(dp_count, slot_count * position_rows, half_width)
        array = lax.all_to_all(array, "dp", split_axis=0, concat_axis=0, tiled=True)
        return array.reshape(dealt_count, half_width)

    def columns_of(unit):
        return [hop(unit, distance, dp_count) for distance in Z_ORDER[1:]]

    def along_z(messages):
        return [hop(message, k, dp_count) for message, k in zip(messages, Z_ORDER[1:])]

    own_first, own_second = spread_out(units)
    column_a = columns_of(unit_a)
    column_a, own_first, own_second, units_later, cotangent_rows, deal, unseen = together(
        column_a, own_first, own_second, units_later, cotangent_rows, deal, unseen
    )

    column_a = join_chunks(column_a)
    first_a, second_a = spread_out(column_a)
    own_third = hop_by_core(own_first, 2, 1, dp_count)
    column_far = hop(units_later, 12, dp_count)
    dealt = product(deal, cotangent_rows).astype(jnp.bfloat16)
    mask_sum = product(unseen.astype(jnp.bfloat16)[None, :], cotangent_rows)
    first_a, second_a, own_third, dealt, mask_sum, column_bias, pick, column_far, units_later = (
        together(
            first_a, second_a, own_third, dealt, mask_sum, column_bias, pick, column_far,
            units_later,
        )
    )

    third_a = hop_by_core(first_a, 2, 1, dp_count)
    column = [hop(units_later, distance, dp_count) for distance in (4, 8)]
    third_a, column, inputs_here, dealt = together(third_a, column, inputs, dealt)

    column = join_chunks([column_far, *column])
    first, last = spread_out(column)
    returned = exchanged(dealt)
    own_pieces = (units, own_first, own_second, own_third)
    normed, qkv, prob, attended, branch, weights_a, w_output = attention_forward(
        words, inputs_here, rep_master, split_rows, column_bias, own_pieces,
        (column_a, first_a, second_a, third_a),
    )
    first, last = together(first, last)

    third = hop_by_core(first, 2, 1, dp_count)
    branch_other = swap_cores(branch)
    gathered = product(pick, returned).astype(jnp.bfloat16)
    gathered_other = swap_cores(gathered)
    grad_out = jnp.where(
        core_index == 0,
        jnp.concatenate([gathered, gathered_other], axis=1),
        jnp.concatenate([gathered_other, gathered], axis=1),
    )
    third, branch_other, grad_out = together(third, branch_other, grad_out)

    hidden_sum, grad_sum, middle, back_two, second, sent_b, kept_b, sent_c, kept_c = mlp_all(
        words, inputs, branch, branch_other, rep_master, hidden_bias, grad_out, own_pieces,
        (column, first, last, third),
    )
    middle, back_two, second, sent_b, kept_b, sent_c, kept_c = together(
        middle, back_two, second, sent_b, kept_b, sent_c, kept_c
    )

    one_c = hop_by_core(sent_c, 2, 1, dp_count)
    back_two_other = swap_cores(back_two)
    second_other = swap_cores(second)
    total = second.astype(jnp.float32) + second_other.astype(jnp.float32) + rep_master[5]
    result = (middle + total).astype(jnp.bfloat16)
    result_half = lax.dynamic_slice_in_dim(result, core_index * half_width, half_width, 1)
    outgoing = contract_rows(pick, result_half).astype(jnp.bfloat16)
    one_c, back_two_other, outgoing = together(one_c, back_two_other, outgoing)

    half_unit = 4 * UNIT_ROWS
    one_b = hop_by_core(sent_b, 2, 1, dp_count)
    two_c = hop_by_core(
        added(half_unit, 2 * half_unit, (kept_c, 0), (one_c, 0)), 1, 2, dp_count
    )
    arrived = exchanged(outgoing)
    grad_middle, back_one, sent_a, kept_a = attention_back(
        words, rep_master, hidden_sum, grad_sum, mask_sum, middle, back_two, back_two_other,
        grad_out, w_output, attended, qkv, prob, normed, weights_a, inputs,
    )
    two_c, one_b, back_one, sent_a, kept_a, arrived = together(
        two_c, one_b, back_one, sent_a, kept_a, arrived
    )

    one_a = hop_by_core(sent_a, 2, 1, dp_count)
    two_b = hop_by_core(
        added(half_unit, 2 * half_unit, (kept_b, 0), (one_b, 0)), 1, 2, dp_count
    )
    arrivals_c = along_z(last_messages(kept_c, one_c, two_c))
    full_out = contract_rows(deal, arrived)
    full_out = jnp.where(unseen[:, None], mask_token.astype(jnp.float32)[None, :], full_out)
    full_out = full_out.astype(jnp.bfloat16)
    one_a, arrivals_c, two_b, full_out, back_one = together(
        one_a, arrivals_c, two_b, full_out, back_one
    )

    two_a_sent = added(half_unit, 2 * half_unit + 16, (kept_a, 0), (one_a, 0))
    two_a = hop_by_core(two_a_sent, 1, 2, dp_count)
    arrivals_b = along_z(last_messages(kept_b, one_b, two_b))
    fc2_new = adam_unit(
        [(kept_c, one_c, two_c, *arrivals_c)],
        [(fc2_master, fc2_first, fc2_second)],
        [(0, side * 6 + j, 0, side * UNIT_ROWS * 6 + j, 6) for side in range(2) for j in range(6)],
    )
    back_one_other = swap_cores(back_one)
    two_a_sent, two_a, arrivals_b[0], back_one_other = together(
        two_a_sent, two_a, arrivals_b[0], back_one_other
    )

    messages = last_messages(kept_a, one_a, two_a, two_a_sent)
    arrivals = along_z(messages)
    fc1_new = adam_unit(
        [(kept_b, one_b, two_b, *arrivals_b)],
        [(fc1_master, fc1_first, fc1_second)],
        [(0, j, 0, j, 12) for j in range(12)],
    )
    input_grad = input_gradient(inputs, back_one, back_one_other, grad_middle, rep_master)
    arrivals, message, input_grad, *fc1_new = together(
        arrivals, messages[0], input_grad, *fc1_new
    )

    vectors = [array[UNIT_ROWS:].astype(jnp.float32) for array in (message, *arrivals)]
    vectors = (vectors[0] + vectors[1]) + (vectors[2] + vectors[3])
    rep_total = (vectors[:3] + swap_cores(vectors[:3])).reshape(rep_master.shape)
    split_total = jnp.concatenate(
        [vectors[3, : 2 * half_width], vectors[4]]
    ).reshape(split_master.shape)
    mask_total = vectors[3, 2 * half_width : 3 * half_width]
    qkv_out_new = adam_unit(
        [(kept_a, one_a, two_a, *arrivals)],
        [(qkv_master, qkv_first, qkv_second), (out_master, out_first, out_second)],
        [(0, j, 0, j, 9) for j in range(9)] + [(0, 9 + j, 1, j, 3) for j in range(3)],
    )
    full_out = full_out.reshape(positions_here, strip_count, half_width)
    full_out = jnp.transpose(full_out, (1, 0, 2))[:, :, None, :]
    input_grad = input_grad.reshape(slot_count, capacity, feature_width)
    rep_new = adam_step(rep_master, rep_first, rep_second, rep_total, VECTOR_RATE, 0.0)
    split_new = adam_step(split_master, split_first, split_second, split_total, VECTOR_RATE, 0.0)
    return (
        full_out,
        input_grad,
        mask_total,
        *qkv_out_new,
        *fc1_new,
        *fc2_new,
        *rep_new,
        *split_new,
    )


def solution(mesh):
    placed = (
        P("dp", None, None),
        P(None, None, "dp", "mp"),
        P("mp"),
        P(),
        P(),
        P(),
        P("mp", "dp"),
        P("mp", "dp"),
        P("mp", "dp"),
        P("mp", "dp"),
        P("mp", "dp"),
        P("mp", "dp"),
        P("mp", "dp"),
        P("mp", "dp"),
        P("mp", "dp"),
        P("mp", "dp"),
        P("mp", "dp"),
        P("mp", "dp"),
        P(),
        P(),
        P(),
        P("mp", None, None),
        P("mp", None, None),
        P("mp", None, None),
    )
    tuned = mesh.shape["dp"] == 16 and mesh.shape["mp"] == 2
    return jax.shard_map(
        on_device if tuned else on_device_general,
        mesh=mesh,
        in_specs=placed,
        out_specs=(
            P(None, None, "dp", "mp"),
            P("dp", None, None),
            P("mp"),
            P("mp", "dp"),
            P("mp", "dp"),
            P("mp", "dp"),
            P("mp", "dp"),
            P("mp", "dp"),
            P("mp", "dp"),
            P("mp", "dp"),
            P("mp", "dp"),
            P("mp", "dp"),
            P("mp", "dp"),
            P("mp", "dp"),
            P("mp", "dp"),
            P(),
            P(),
            P(),
            P("mp", None, None),
            P("mp", None, None),
            P("mp", None, None),
        ),
        check_vma=False,
    )
```

```python
import jax
import jax.numpy as jnp
from jax import lax
from jax.experimental import pallas as pl
from jax.experimental.pallas import tpu as pltpu
from jax.sharding import PartitionSpec as P

HEAD = 64
PATCHES = 529
STEP = 10


NORM_EPS = 1e-06
BETA_ONE = 0.9
BETA_TWO = 0.999
ADAM_EPS = 1e-08
MATRIX_RATE = 0.15
MATRIX_DECAY = 0.05
VECTOR_RATE = 0.6


def layer_norm(signal, norm_gain, norm_shift):
    average = jnp.mean(signal, axis=-1, keepdims=True)
    centered = signal - average
    spread = jnp.mean(centered * centered, axis=-1, keepdims=True)
    return centered * lax.rsqrt(spread + NORM_EPS) * norm_gain + norm_shift


def exact_gelu(signal):
    return jax.nn.gelu(signal, approximate=False)


def product(left, right):
    return jnp.dot(left, right, preferred_element_type=jnp.float32)


def contract_last(left, right):
    return lax.dot_general(
        left, right, (((1,), (1,)), ((), ())), preferred_element_type=jnp.float32
    )


def contract_rows(left, right):
    return lax.dot_general(
        left, right, (((0,), (0,)), ((), ())), preferred_element_type=jnp.float32
    )


def adam_step(weight, moment_one, moment_two, gradient, step_rate, decay_rate):
    one_new = BETA_ONE * moment_one + (1.0 - BETA_ONE) * gradient
    two_new = BETA_TWO * moment_two + (1.0 - BETA_TWO) * gradient * gradient
    one_hat = one_new / (1.0 - BETA_ONE**STEP)
    two_hat = two_new / (1.0 - BETA_TWO**STEP)
    weight_new = weight - step_rate * (
        one_hat / (jnp.sqrt(two_hat) + ADAM_EPS) + decay_rate * weight
    )
    return (weight_new, one_new, two_new)


def total_over_cores(partial):
    return partial.astype(jnp.float32) + swap_cores(partial).astype(jnp.float32)


def pair_scores(queries, key_rows, valid_rows):
    scores = jnp.einsum(
        "qhd,khd->hqk", queries, key_rows, preferred_element_type=jnp.float32
    ) * HEAD ** (-0.5)
    return jnp.where(valid_rows[None, None, :], scores, -1e30)


def attend_pair(pair_block):
    queries, key_rows, value_rows, valid_rows = pair_block
    scores = pair_scores(queries, key_rows, valid_rows)
    row_max = jnp.max(scores, axis=2, keepdims=True)
    lifted = jnp.exp(scores - row_max)
    row_total = jnp.sum(lifted, axis=2, keepdims=True)
    probability = (lifted / row_total).astype(jnp.bfloat16)
    attended = jnp.einsum(
        "hqk,khd->qhd", probability, value_rows, preferred_element_type=jnp.float32
    )
    return (attended.astype(jnp.bfloat16), row_max[:, :, 0] + jnp.log(row_total[:, :, 0]))


def attend_pair_back(pair_block):
    queries, key_rows, value_rows, valid_rows, log_total, grad_attended = pair_block
    scores = pair_scores(queries, key_rows, valid_rows)
    probability = jnp.exp(scores - log_total[:, :, None])
    grad_prob = jnp.einsum(
        "qhd,khd->hqk", grad_attended, value_rows, preferred_element_type=jnp.float32
    )
    inner_sum = jnp.sum(probability * grad_prob, axis=2, keepdims=True)
    grad_scores = (probability * (grad_prob - inner_sum)).astype(jnp.bfloat16)
    score_scale = HEAD ** (-0.5)
    grad_queries = (
        jnp.einsum("hqk,khd->qhd", grad_scores, key_rows, preferred_element_type=jnp.float32)
        * score_scale
    )
    grad_keys = (
        jnp.einsum("hqk,qhd->khd", grad_scores, queries, preferred_element_type=jnp.float32)
        * score_scale
    )
    grad_values = jnp.einsum(
        "hqk,qhd->khd",
        probability.astype(jnp.bfloat16),
        grad_attended,
        preferred_element_type=jnp.float32,
    )
    return (
        grad_queries.astype(jnp.bfloat16),
        grad_keys.astype(jnp.bfloat16),
        grad_values.astype(jnp.bfloat16),
    )


def hop(array, distance, axis_count):
    return lax.ppermute(array, "dp", [(i, i ^ distance) for i in range(axis_count)])


def swap_cores(array):
    return lax.ppermute(array, "mp", [(0, 1), (1, 0)])


def place_chunks(pieces, chunk_ids, member, count):
    rows, width = pieces[0].shape[1:]

    def body(member_ref, *refs):
        sources, target, semaphores = refs[:-2], refs[-2], refs[-1]
        copies = []
        for source, ids in zip(sources, chunk_ids):
            for place, distance in enumerate(ids):
                copies.append(
                    pltpu.make_async_copy(
                        source.at[place],
                        target.at[member_ref[0] ^ distance],
                        semaphores.at[len(copies)],
                    )
                )
        for copy in copies:
            copy.start()
        for copy in copies:
            copy.wait()

    return pl.pallas_call(
        body,
        in_specs=[pl.BlockSpec(memory_space=pltpu.SMEM)]
        + [pl.BlockSpec(memory_space=pl.ANY)] * len(pieces),
        out_specs=pl.BlockSpec(memory_space=pltpu.VMEM),
        out_shape=jax.ShapeDtypeStruct((count, rows, width), pieces[0].dtype),
        scratch_shapes=[pltpu.SemaphoreType.DMA((count,))],
        cost_estimate=pl.CostEstimate(
            flops=0, transcendentals=0, bytes_accessed=4 * count * rows * width
        ),
        name="place_chunks",
    )(member, *pieces)


def pick_chunks(whole, chunk_ids, member):
    count, rows, width = whole.shape

    def body(member_ref, source, *refs):
        targets, semaphores = refs[:-1], refs[-1]
        copies = []
        for target, ids in zip(targets, chunk_ids):
            for place, distance in enumerate(ids):
                copies.append(
                    pltpu.make_async_copy(
                        source.at[member_ref[0] ^ distance],
                        target.at[place],
                        semaphores.at[len(copies)],
                    )
                )
        for copy in copies:
            copy.start()
        for copy in copies:
            copy.wait()

    return pl.pallas_call(
        body,
        in_specs=[pl.BlockSpec(memory_space=pltpu.SMEM), pl.BlockSpec(memory_space=pltpu.VMEM)],
        out_specs=[pl.BlockSpec(memory_space=pl.ANY)] * len(chunk_ids),
        out_shape=[
            jax.ShapeDtypeStruct((len(ids), rows, width), whole.dtype) for ids in chunk_ids
        ],
        scratch_shapes=[pltpu.SemaphoreType.DMA((count,))],
        cost_estimate=pl.CostEstimate(
            flops=0, transcendentals=0, bytes_accessed=4 * count * rows * width
        ),
        name="pick_chunks",
    )(member, whole)


def gather_chunks(chunk, member, count):
    own = chunk[None]
    if count == 16:
        near, far, last = (hop(own, k, count) for k in (4, 8, 12))
        first, second = jnp.concatenate([own, near]), jnp.concatenate([far, last])
        x_first, x_second = hop(first, 1, count), hop(second, 1, count)
        y_first, y_second = hop(first, 2, count), hop(second, 2, count)
        d_first, d_second = hop(y_first, 1, count), hop(x_second, 2, count)
        pieces = [first, second, x_first, x_second, y_first, y_second, d_first, d_second]
        ids = [(0, 4), (8, 12), (1, 5), (9, 13), (2, 6), (10, 14), (3, 7), (11, 15)]
    else:
        held, step = own, 1
        while step < count:
            held = jnp.concatenate([held, hop(held, step, count)])
            step *= 2
        pieces, ids = [held], [tuple(range(count))]
    return place_chunks(pieces, ids, member, count)


def scatter_chunks(whole, member, count):
    def wide(array):
        return array.astype(jnp.float32)

    if count == 16:
        ids = [(3, 7), (11, 15), (2, 6), (9, 13), (10, 14), (1, 5), (0, 4), (8, 12)]
        d_first, d_second, y_first, x_second, y_second, x_first, first, second = pick_chunks(
            whole, ids, member
        )
        d_first, d_second = hop(d_first, 1, count), hop(d_second, 2, count)
        y_second, x_first = hop(y_second, 2, count), hop(x_first, 1, count)
        y_first = hop((wide(y_first) + wide(d_first)).astype(jnp.bfloat16), 2, count)
        x_second = hop((wide(x_second) + wide(d_second)).astype(jnp.bfloat16), 1, count)
        first = wide(first) + wide(y_first) + wide(x_first)
        second = wide(second) + wide(y_second) + wide(x_second)
        near = hop(first[1].astype(jnp.bfloat16), 4, count)
        far = hop(second[0].astype(jnp.bfloat16), 8, count)
        last = hop(second[1].astype(jnp.bfloat16), 12, count)
        return first[0] + wide(near) + wide(far) + wide(last)
    (held,) = pick_chunks(whole, [tuple(range(count))], member)
    held = wide(held)
    step = count // 2
    while step:
        held = held[:step] + wide(hop(held[step:].astype(jnp.bfloat16), step, count))
        step //= 2
    return held[0]


def sum_over_dp(vector, count):
    if count == 16:
        for low, high in ((1, 2), (4, 8)):
            other, third, fourth = (hop(vector, k, count) for k in (low, high, low + high))
            vector = (vector + other) + (third + fourth)
        return vector
    step = 1
    while step < count:
        vector = vector + hop(vector, step, count)
        step *= 2
    return vector


def on_device_general(
    patch_rows,
    cotangent,
    mask_token,
    lengths,
    masked,
    dealing,
    qkv_master,
    qkv_first,
    qkv_second,
    out_master,
    out_first,
    out_second,
    fc1_master,
    fc1_first,
    fc1_second,
    fc2_master,
    fc2_first,
    fc2_second,
    rep_master,
    rep_first,
    rep_second,
    split_master,
    split_first,
    split_second,
):
    slot_count, capacity, feature_width = patch_rows.shape
    half_width = mask_token.shape[0]
    dp_count = lax.axis_size("dp")
    member = lax.axis_index("dp")
    core_index = lax.axis_index("mp")
    positions_here = cotangent.shape[1]
    position_span = positions_here * dp_count
    heads_here = half_width // HEAD
    hidden_width = (split_master.shape[1] - 2) * half_width
    row_count = slot_count * capacity
    pair_count = slot_count // 2
    pair_length = 2 * capacity
    patch_index = jnp.arange(PATCHES, dtype=jnp.int32)
    visible_all = (patch_index[None, :] < lengths[:, None]) & (masked == 0)
    strips_here = lax.dynamic_slice_in_dim(dealing, member * slot_count, slot_count)
    visible_here = visible_all[strips_here]
    rank_here = jnp.cumsum(visible_here.astype(jnp.int32), axis=1) - 1
    counts_here = jnp.sum(visible_here.astype(jnp.int32), axis=1)
    valid_rows = jnp.arange(capacity, dtype=jnp.int32)[None, :] < counts_here[:, None]
    padding = position_span - PATCHES
    visible_padded = jnp.pad(visible_here, ((0, 0), (0, padding)))
    rank_padded = jnp.pad(jnp.maximum(rank_here, 0), ((0, 0), (0, padding)))
    own_positions = jnp.arange(positions_here, dtype=jnp.int32) * dp_count + member
    inside = own_positions < PATCHES
    visible_own = visible_all[:, jnp.minimum(own_positions, PATCHES - 1)] & inside[None, :]
    strip_count = lengths.shape[0]
    held_count = strip_count * positions_here
    strip_row = (
        jnp.arange(positions_here, dtype=jnp.int32)[None, :] * strip_count + dealing[:, None]
    ).reshape(held_count)
    deal = (
        strip_row[:, None] == jnp.arange(held_count, dtype=jnp.int32)[None, :]
    ).astype(jnp.bfloat16)
    encoder_row = jnp.where(
        visible_padded,
        rank_padded + jnp.arange(slot_count, dtype=jnp.int32)[:, None] * capacity,
        -1,
    )
    encoder_row = jnp.transpose(
        encoder_row.reshape(slot_count, positions_here, dp_count), (2, 0, 1)
    ).reshape(held_count)
    pick = (
        jnp.arange(row_count, dtype=jnp.int32)[:, None] == encoder_row[None, :]
    ).astype(jnp.bfloat16)
    unseen = jnp.transpose(jnp.logical_not(visible_own) & inside[None, :]).reshape(held_count)
    member_word = member.astype(jnp.int32).reshape(1)

    cotangent_rows = jnp.transpose(cotangent.reshape(strip_count, positions_here, half_width), (1, 0, 2))
    cotangent_rows = cotangent_rows.reshape(held_count, half_width)
    dealt = product(deal, cotangent_rows).astype(jnp.bfloat16)
    returned = lax.all_to_all(
        dealt.reshape(dp_count, slot_count * positions_here, half_width),
        "dp",
        split_axis=0,
        concat_axis=0,
        tiled=True,
    ).reshape(held_count, half_width)
    gathered = product(pick, returned).astype(jnp.bfloat16)
    gathered_other = swap_cores(gathered)
    grad_out = jnp.where(
        core_index == 0,
        jnp.concatenate([gathered, gathered_other], axis=1),
        jnp.concatenate([gathered_other, gathered], axis=1),
    )
    mask_grad = product(unseen.astype(jnp.bfloat16)[None, :], cotangent_rows)[0]

    def gathered_matrix(master, rows, width):
        chunk = master.astype(jnp.bfloat16).reshape(rows // dp_count, width)
        return gather_chunks(chunk, member_word, dp_count).reshape(rows, width)

    w_attention = gathered_matrix(qkv_master, feature_width, 3 * half_width)
    w_output = gathered_matrix(out_master, half_width, feature_width)
    w_first = gathered_matrix(fc1_master, feature_width, hidden_width)
    w_second = gathered_matrix(fc2_master, hidden_width, feature_width)
    inputs = patch_rows.reshape(row_count, feature_width).astype(jnp.float32)
    normed_full, norm_back_one = jax.vjp(layer_norm, inputs, rep_master[0], rep_master[1])
    normed = normed_full.astype(jnp.bfloat16)
    projected = product(normed, w_attention).reshape(row_count, 3, half_width)
    queries = (projected[:, 0] + split_master[0, 0]).astype(jnp.bfloat16)
    key_rows = projected[:, 1].astype(jnp.bfloat16)
    value_rows = (projected[:, 2] + split_master[0, 1]).astype(jnp.bfloat16)

    def by_pair(array):
        return array.reshape(pair_count, pair_length, heads_here, HEAD)

    pair_valid = valid_rows.reshape(pair_count, pair_length)
    attended, log_total = lax.map(
        attend_pair, (by_pair(queries), by_pair(key_rows), by_pair(value_rows), pair_valid)
    )
    attended = attended.reshape(row_count, half_width)
    branch = total_over_cores(product(attended, w_output)) + rep_master[4]
    middle = inputs + branch
    normed_two_full, norm_back_two = jax.vjp(layer_norm, middle, rep_master[2], rep_master[3])
    normed_two = normed_two_full.astype(jnp.bfloat16)
    hidden = product(normed_two, w_first) + split_master[0, 2:].reshape(hidden_width)
    active_full, gelu_back = jax.vjp(exact_gelu, hidden)
    active = active_full.astype(jnp.bfloat16)
    second = total_over_cores(product(active, w_second).astype(jnp.bfloat16)) + rep_master[5]
    result = (middle + second).astype(jnp.bfloat16)
    result_half = lax.dynamic_slice_in_dim(result, core_index * half_width, half_width, 1)
    outgoing = contract_rows(pick, result_half).astype(jnp.bfloat16)
    arrived = lax.all_to_all(
        outgoing.reshape(dp_count, slot_count * positions_here, half_width),
        "dp",
        split_axis=0,
        concat_axis=0,
        tiled=True,
    ).reshape(held_count, half_width)
    full_out = contract_rows(deal, arrived)
    full_out = jnp.where(unseen[:, None], mask_token.astype(jnp.float32)[None, :], full_out)
    full_out = full_out.astype(jnp.bfloat16).reshape(positions_here, strip_count, half_width)
    full_out = jnp.transpose(full_out, (1, 0, 2))[:, :, None, :]
    grad_rows = grad_out.astype(jnp.float32)
    bias_two_grad = jnp.sum(grad_rows, axis=0)
    grad_active = contract_last(grad_out, w_second)
    grad_hidden = gelu_back(grad_active)[0].astype(jnp.bfloat16)
    fc2_grad = contract_rows(active, grad_out)
    fc1_grad = contract_rows(normed_two, grad_hidden)
    hidden_bias_grad = jnp.sum(grad_hidden.astype(jnp.float32), axis=0)
    grad_normed_two = total_over_cores(contract_last(grad_hidden, w_first))
    grad_middle_part, gain_two_grad, shift_two_grad = norm_back_two(grad_normed_two)
    grad_middle = grad_rows + grad_middle_part
    grad_branch = grad_middle.astype(jnp.bfloat16)
    out_bias_grad = jnp.sum(grad_branch.astype(jnp.float32), axis=0)
    out_grad = contract_rows(attended, grad_branch)
    grad_attended = contract_last(grad_branch, w_output).astype(jnp.bfloat16)
    grad_queries, grad_keys, grad_values = lax.map(
        attend_pair_back,
        (
            by_pair(queries),
            by_pair(key_rows),
            by_pair(value_rows),
            pair_valid,
            log_total,
            by_pair(grad_attended),
        ),
    )
    grad_queries = grad_queries.reshape(row_count, half_width)
    grad_keys = grad_keys.reshape(row_count, half_width)
    grad_values = grad_values.reshape(row_count, half_width)
    grad_projected = jnp.stack([grad_queries, grad_keys, grad_values], axis=1).reshape(
        row_count, 3 * half_width
    )
    qkv_grad = contract_rows(normed, grad_projected)
    query_bias_grad = jnp.sum(grad_queries.astype(jnp.float32), axis=0)
    value_bias_grad = jnp.sum(grad_values.astype(jnp.float32), axis=0)
    grad_normed = total_over_cores(contract_last(grad_projected, w_attention))
    grad_inputs_part, gain_one_grad, shift_one_grad = norm_back_one(grad_normed)
    input_grad = (grad_middle + grad_inputs_part).reshape(slot_count, capacity, feature_width)
    def scattered(gradient):
        rows, width = gradient.shape
        chunks = gradient.astype(jnp.bfloat16).reshape(dp_count, rows // dp_count, width)
        return scatter_chunks(chunks, member_word, dp_count).reshape(1, -1)

    fc2_total = scattered(fc2_grad)
    fc1_total = scattered(fc1_grad)
    out_total = scattered(out_grad)
    qkv_total = scattered(qkv_grad)
    rep_grad = jnp.stack(
        [gain_one_grad, shift_one_grad, gain_two_grad, shift_two_grad, out_bias_grad, bias_two_grad]
    )
    split_grad = jnp.concatenate(
        [query_bias_grad[None], value_bias_grad[None], hidden_bias_grad.reshape(-1, half_width)],
        axis=0,
    )[None]
    packed = jnp.concatenate([mask_grad, rep_grad.reshape(-1), split_grad.reshape(-1)])
    packed = sum_over_dp(packed.reshape(-1, 128), dp_count).reshape(-1)
    mask_total = packed[:half_width]
    rep_total = packed[half_width : half_width + rep_grad.size].reshape(rep_grad.shape)
    split_total = packed[half_width + rep_grad.size :].reshape(split_grad.shape)
    qkv_new = adam_step(qkv_master, qkv_first, qkv_second, qkv_total, MATRIX_RATE, MATRIX_DECAY)
    out_new = adam_step(out_master, out_first, out_second, out_total, MATRIX_RATE, MATRIX_DECAY)
    fc1_new = adam_step(fc1_master, fc1_first, fc1_second, fc1_total, MATRIX_RATE, MATRIX_DECAY)
    fc2_new = adam_step(fc2_master, fc2_first, fc2_second, fc2_total, MATRIX_RATE, MATRIX_DECAY)
    rep_new = adam_step(rep_master, rep_first, rep_second, rep_total, VECTOR_RATE, 0.0)
    split_new = adam_step(split_master, split_first, split_second, split_total, VECTOR_RATE, 0.0)
    return (
        full_out,
        input_grad,
        mask_total,
        qkv_new[0],
        qkv_new[1],
        qkv_new[2],
        out_new[0],
        out_new[1],
        out_new[2],
        fc1_new[0],
        fc1_new[1],
        fc1_new[2],
        fc2_new[0],
        fc2_new[1],
        fc2_new[2],
        rep_new[0],
        rep_new[1],
        rep_new[2],
        split_new[0],
        split_new[1],
        split_new[2],
    )


BLOCK = 384
UNIT_ROWS = 48
UNIT_WIDTH = 1536
BLOCK_WIDTH = 256
Z_ORDER = (0, 12, 4, 8)
VMEM_BYTES = 60 * 1024 * 1024
ANY = pl.BlockSpec(memory_space=pl.ANY)
IN_VMEM = pl.BlockSpec(memory_space=pltpu.VMEM)
IN_SMEM = pl.BlockSpec(memory_space=pltpu.SMEM)


def shaped(shape, dtype):
    return jax.ShapeDtypeStruct(shape, dtype)


def params(grid_axes=0):
    semantics = ("arbitrary",) * grid_axes if grid_axes else None
    return pltpu.CompilerParams(dimension_semantics=semantics, vmem_limit_bytes=VMEM_BYTES)


def cost(microseconds):
    return pl.CostEstimate(
        flops=int(microseconds * 1.15e9), transcendentals=0, bytes_accessed=1000000
    )


def together(*values):
    return lax.optimization_barrier(values)


def hop_by_core(array, first_core, second_core, count):
    pairs = []
    for i in range(count):
        pairs.append((2 * i, 2 * (i ^ first_core)))
        pairs.append((2 * i + 1, 2 * (i ^ second_core) + 1))
    return lax.ppermute(array, ("dp", "mp"), pairs)


def pack_units(qkv, out, fc1, fc2):
    def body(qkv_ref, out_ref, fc1_ref, fc2_ref, units, unit_a, units_later):
        def put(unit, column, rows):
            units[unit, :, column * 128 : (column + 1) * 128] = rows.astype(jnp.bfloat16)

        for j in range(9):
            put(0, j, qkv_ref[pl.ds(j, UNIT_ROWS, stride=9), :])
        for j in range(3):
            put(0, 9 + j, out_ref[pl.ds(j, UNIT_ROWS, stride=3), :])
        for j in range(12):
            put(1, j, fc1_ref[pl.ds(j, UNIT_ROWS, stride=12), :])
        for half in range(2):
            for j in range(6):
                start = half * UNIT_ROWS * 6 + j
                put(2, half * 6 + j, fc2_ref[pl.ds(start, UNIT_ROWS, stride=6), :])
        unit_a[0] = units[0]
        units_later[0] = units[1]
        units_later[1] = units[2]

    def unit_array(count):
        return shaped((count, UNIT_ROWS, UNIT_WIDTH), jnp.bfloat16)

    return pl.pallas_call(
        body,
        out_shape=[unit_array(3), unit_array(1), unit_array(2)],
        compiler_params=params(),
        cost_estimate=cost(2),
        name="pack_units",
    )(
        *(array.reshape(-1, 128) for array in (qkv, out, fc1, fc2))
    )


def chunk_sources(words, own, pieces, unit):
    step, offset = (1, 0) if unit == 0 else (2, unit - 1)
    found = []
    for place, extra in enumerate((0, words[1], words[2], 3)):
        found.append((own[place].at[unit], words[0] ^ extra))
        for entry, distance in enumerate(Z_ORDER[1:]):
            source = pieces[place].at[entry * step + offset]
            found.append((source, words[0] ^ distance ^ extra))
    return found


def join_chunks(chunks):
    size = chunks[0].shape[0]

    def body(*refs):
        for entry, ref in enumerate(refs[:-1]):
            refs[-1][entry * size : (entry + 1) * size] = ref[...]

    return pl.pallas_call(
        body,
        out_shape=shaped((len(chunks) * size,) + chunks[0].shape[1:], chunks[0].dtype),
        compiler_params=params(),
        cost_estimate=cost(1.5 * size),
        name="join_chunks",
    )(*chunks)


def last_messages(kept, one, two, carried=None):
    extra = 0 if carried is None else 16
    inputs = [kept, one, two] + ([] if carried is None else [carried])

    def body(kept_ref, one_ref, two_ref, *refs):
        targets = refs[-3:]
        if extra:
            vectors = refs[0][...].astype(jnp.float32)
            vectors = vectors + two_ref[4 * UNIT_ROWS :, :].astype(jnp.float32)
            vectors = vectors.astype(jnp.bfloat16)
        for entry, target in enumerate(targets):
            rows = slice((entry + 1) * UNIT_ROWS, (entry + 2) * UNIT_ROWS)
            total = kept_ref[rows, :].astype(jnp.float32) + one_ref[rows, :].astype(jnp.float32)
            total = total + two_ref[rows, :].astype(jnp.float32)
            target[:UNIT_ROWS, :] = total.astype(jnp.bfloat16)
            if extra:
                target[UNIT_ROWS:, :] = vectors

    def rows(count, start=0):
        return pl.BlockSpec((count, UNIT_WIDTH), lambda i: (start, 0))

    specs = [rows(4 * UNIT_ROWS), rows(4 * UNIT_ROWS), rows(4 * UNIT_ROWS + extra)]
    if extra:
        specs.append(rows(16, 4 * UNIT_ROWS // 16))
    message = shaped((UNIT_ROWS + extra, UNIT_WIDTH), jnp.bfloat16)
    return pl.pallas_call(
        body,
        grid=(1,),
        in_specs=specs,
        out_specs=[rows(UNIT_ROWS + extra)] * 3,
        out_shape=[message] * 3,
        compiler_params=params(1),
        cost_estimate=cost(1.5),
        name="last_messages",
    )(*inputs)


def added(start, stop, *arrays):
    total = 0.0
    for array, offset in arrays:
        total = total + array[start - offset : stop - offset].astype(jnp.float32)
    return total.astype(jnp.bfloat16)


def unit_shapes(extra=0):
    return [shaped((8 * UNIT_ROWS + extra, UNIT_WIDTH), jnp.bfloat16)] * 2


def unit_targets(words, sent, kept):
    def rows(array, entry):
        return array.at[pl.ds(entry * UNIT_ROWS, UNIT_ROWS), :]

    places = []
    for entry, distance in enumerate(Z_ORDER):
        own = words[0] ^ distance
        places.append((rows(sent, 4 + entry), own ^ 3))
        places.append((rows(sent, entry), own ^ words[2]))
        places.append((rows(kept, entry), own))
        places.append((rows(kept, 4 + entry), own ^ words[1]))
    return places


def lanes_of(part, size):
    return pl.ds(pl.multiple_of(part * size, 128), size)


def unit_rows(owner, rows=UNIT_ROWS):
    return pl.ds(pl.multiple_of(owner * rows, 16), rows)


def norm_parts(signal):
    average = jnp.mean(signal, axis=1, keepdims=True)
    centered = signal - average
    scale = lax.rsqrt(jnp.mean(centered * centered, axis=1, keepdims=True) + NORM_EPS)
    return centered * scale, scale


def norm_back(grad, unit_signal, scale, gain):
    scaled = grad * gain
    mean_one = jnp.mean(scaled, axis=1, keepdims=True)
    mean_two = jnp.mean(scaled * unit_signal, axis=1, keepdims=True)
    return scale * (scaled - mean_one - unit_signal * mean_two)


def fixed(*shape):
    return pl.BlockSpec(shape, lambda i: (0,) * len(shape))


def run_copies(pairs, semaphores):
    copies = [
        pltpu.make_async_copy(source, target, semaphores.at[i])
        for i, (source, target) in enumerate(pairs)
    ]
    for copy in copies:
        copy.start()
    for copy in copies:
        copy.wait()


class Copies:
    def __init__(self, semaphores):
        self.semaphores, self.used = semaphores, 0

    def start(self, pairs):
        started = []
        for source, target in pairs:
            copy = pltpu.make_async_copy(source, target, self.semaphores.at[self.used])
            self.used += 1
            copy.start()
            started.append(copy)
        return started


def finish(copies):
    for copy in copies:
        copy.wait()


def chunk_pairs(words, own, pieces, unit, target):
    return [
        (source, target.at[unit_rows(owner), :])
        for source, owner in chunk_sources(words, own, pieces, unit)
    ]


def attention_forward(words, rows_in, rep, split, column_bias, own_pieces, pieces):
    count, width = rows_in.shape
    half = split.shape[1]
    pairs_of_heads = half // (2 * HEAD)

    def body(
        words_ref, in_ref, rep_ref, split_ref, bias_ref, o0, o1, o2, o3, p0, p1, p2, p3,
        normed_ref, qkv_ref, prob_ref, attended_ref, partial_ref, weights_ref, w_out_ref, spread, semaphores,
    ):
        pair = pl.program_id(0)

        @pl.when(pair == 0)
        def _():
            copies = Copies(semaphores)
            pairs = chunk_pairs(words_ref, (o0, o1, o2, o3), (p0, p1, p2, p3), 0, weights_ref)
            loads = copies.start(pairs)

            @pl.loop(0, count // BLOCK)
            def _(block):
                rows = pl.ds(block * BLOCK, BLOCK)
                unit_signal, _ = norm_parts(in_ref[rows, :].astype(jnp.float32))
                normed = unit_signal * rep_ref[0:1, :] + rep_ref[1:2, :]
                normed_ref[rows, :] = normed.astype(jnp.bfloat16)

            finish(loads)

            @pl.loop(0, count // BLOCK)
            def _(block):
                rows = pl.ds(block * BLOCK, BLOCK)
                projected = product(normed_ref[rows, :], weights_ref[:, : 3 * half])
                queries = projected[:, :half] + split_ref[0:1, :]
                values = projected[:, 2 * half :] + split_ref[1:2, :]
                qkv_ref[rows, :half] = queries.astype(jnp.bfloat16)
                qkv_ref[rows, half : 2 * half] = projected[:, half : 2 * half].astype(jnp.bfloat16)
                qkv_ref[rows, 2 * half :] = values.astype(jnp.bfloat16)

        lane = pl.multiple_of(pair * (2 * HEAD), 2 * HEAD)
        upper = lax.broadcasted_iota(jnp.int32, (1, 2 * HEAD), 1) >= HEAD
        keys = qkv_ref[:, pl.ds(half + lane, 2 * HEAD)]
        values = qkv_ref[:, pl.ds(2 * half + lane, 2 * HEAD)]
        for block in range(count // BLOCK):
            rows = pl.ds(block * BLOCK, BLOCK)
            queries = qkv_ref[rows, pl.ds(lane, 2 * HEAD)]
            found = []
            for side in range(2):
                chosen = upper if side else jnp.logical_not(upper)
                own = jnp.where(chosen, queries, jnp.zeros_like(queries))
                scores = contract_last(own, keys) * HEAD ** (-0.5) + bias_ref[...]
                lifted = jnp.exp(scores - jnp.max(scores, axis=1, keepdims=True))
                total = jnp.sum(lifted, axis=1, keepdims=True)
                probability = (lifted * (1.0 / total)).astype(jnp.bfloat16)
                prob_ref[side, rows, :] = probability
                found.append(product(probability, values))
            attended = jnp.where(upper, found[1], found[0])
            attended_ref[rows, pl.ds(lane, 2 * HEAD)] = attended.astype(jnp.bfloat16)

        @pl.when(pair == pairs_of_heads - 1)
        def _():
            for strip in range(half // 128):
                start = 3 * half + strip * 128
                spread[strip] = weights_ref[:, start : start + 128].astype(jnp.float32)
                for side in range(2):
                    start = side * half + strip * 128
                    w_out_ref[:, start : start + 128] = spread[
                        strip, pl.ds(side, half, stride=2), :
                    ].astype(jnp.bfloat16)
            partial_ref[...] = product(attended_ref[...], w_out_ref[...]).astype(jnp.bfloat16)

    return pl.pallas_call(
        body,
        grid=(pairs_of_heads,),
        in_specs=[IN_SMEM, fixed(count, width), fixed(6, width), fixed(6, half), fixed(1, count)]
        + [ANY] * 8,
        out_specs=[
            fixed(count, width),
            fixed(count, 3 * half),
            pl.BlockSpec((2, count, count), lambda h: (h, 0, 0)),
            fixed(count, half),
            fixed(count, width),
            fixed(width, UNIT_WIDTH),
            fixed(half, width),
        ],
        out_shape=[
            shaped((count, width), jnp.bfloat16),
            shaped((count, 3 * half), jnp.bfloat16),
            shaped((2 * pairs_of_heads, count, count), jnp.bfloat16),
            shaped((count, half), jnp.bfloat16),
            shaped((count, width), jnp.bfloat16),
            shaped((width, UNIT_WIDTH), jnp.bfloat16),
            shaped((half, width), jnp.bfloat16),
        ],
        scratch_shapes=[
            pltpu.VMEM((half // 128, width, 128), jnp.float32),
            pltpu.SemaphoreType.DMA((16,)),
        ],
        compiler_params=params(1),
        cost_estimate=cost(18),
        name="attention_forward",
    )(words, rows_in, rep, split, column_bias, *own_pieces, *pieces)


def mlp_all(
    words, rows_in, own, other, rep, hidden_bias, grad_out, own_pieces, pieces
):
    count, width = rows_in.shape
    hidden_width = UNIT_WIDTH
    half, wide = width // 2, 2 * BLOCK_WIDTH
    parts = hidden_width // wide

    def body(
        words_ref, rep_any, bias_any, in_any, own_any, other_any, grad_any,
        o0, o1, o2, o3, p0, p1, p2, p3,
        hidden_sum_any, grad_sum_any, middle_any, back_any, second_any,
        sent_b, kept_b, sent_c, kept_c,
        rep_ref, bias_ref, hidden_sum_ref, grad_sum_ref, w_first, w_second, rows_ref, own_ref, other_ref, grad_ref, middle_ref, normed_ref,
        active_ref, slope_ref, grad_hidden_ref, back_ref, second_ref, whole_b, whole_c, semaphores,
    ):
        copies = Copies(semaphores)
        first_loads = copies.start(
            [
                (in_any, rows_ref), (own_any, own_ref), (other_any, other_ref),
                (rep_any, rep_ref), (bias_any, bias_ref),
            ]
        )
        own_refs, later = (o0, o1, o2, o3), (p0, p1, p2, p3)
        loads_b = copies.start(chunk_pairs(words_ref, own_refs, later, 1, w_first))
        pairs = [(grad_any, grad_ref)]
        for source, owner in chunk_sources(words_ref, own_refs, later, 2):
            for side in range(2):
                pairs.append(
                    (
                        source.at[:, pl.ds(side * width, width)],
                        w_second.at[unit_rows(owner * 2 + side), :],
                    )
                )
        loads_c = copies.start(pairs)
        finish(first_loads)

        @pl.loop(0, count // BLOCK)
        def _(block):
            rows = pl.ds(block * BLOCK, BLOCK)
            branch = own_ref[rows, :].astype(jnp.float32) + other_ref[rows, :].astype(jnp.float32)
            middle = rows_ref[rows, :].astype(jnp.float32) + branch + rep_ref[4:5, :]
            middle_ref[rows, :] = middle
            unit_signal, _ = norm_parts(middle)
            normed = unit_signal * rep_ref[2:3, :] + rep_ref[3:4, :]
            normed_ref[rows, :] = normed.astype(jnp.bfloat16)

        stores = copies.start([(middle_ref, middle_any)])
        finish(loads_b)
        for part in range(parts):
            columns = slice(part * wide, (part + 1) * wide)
            hidden = product(normed_ref[...], w_first[:, columns]) + bias_ref[:, columns]
            spread = 0.5 + 0.5 * lax.erf(hidden * 0.7071067811865476)
            active_ref[:, columns] = (hidden * spread).astype(jnp.bfloat16)
            slope = spread + hidden * jnp.exp(-0.5 * hidden * hidden) * 0.3989422804014327
            slope_ref[:, columns] = slope.astype(jnp.bfloat16)

        finish(loads_c)
        second_ref[...] = product(active_ref[...], w_second[...]).astype(jnp.bfloat16)
        stores += copies.start([(second_ref, second_any)])
        grad_sum_ref[...] = jnp.sum(grad_ref[...].astype(jnp.float32), axis=0, keepdims=True)
        for part in range(parts):
            columns = slice(part * wide, (part + 1) * wide)
            grad_active = contract_last(grad_ref[...], w_second[columns, :])
            grad_hidden = grad_active * slope_ref[:, columns].astype(jnp.float32)
            grad_hidden = grad_hidden.astype(jnp.bfloat16)
            grad_hidden_ref[:, columns] = grad_hidden
            hidden_sum_ref[:, columns] = jnp.sum(
                grad_hidden.astype(jnp.float32), axis=0, keepdims=True
            )

        back_ref[...] = contract_last(grad_hidden_ref[...], w_first[...]).astype(jnp.bfloat16)
        stores += copies.start(
            [
                (back_ref, back_any), (hidden_sum_ref, hidden_sum_any),
                (grad_sum_ref, grad_sum_any),
            ]
        )

        @pl.loop(0, hidden_width // half)
        def _(part):
            columns = lanes_of(part, half)
            whole_c[columns, :] = contract_rows(active_ref[:, columns], grad_ref[...]).astype(
                jnp.bfloat16
            )

        for target, owner in unit_targets(words_ref, sent_c, kept_c):
            stores += copies.start(
                [
                    (
                        whole_c.at[unit_rows(owner * 2 + side), :],
                        target.at[:, pl.ds(side * width, width)],
                    )
                    for side in range(2)
                ]
            )

        @pl.loop(0, width // half)
        def _(part):
            columns = lanes_of(part, half)
            whole_b[columns, :] = contract_rows(normed_ref[:, columns], grad_hidden_ref[...]).astype(
                jnp.bfloat16
            )

        for target, owner in unit_targets(words_ref, sent_b, kept_b):
            stores += copies.start([(whole_b.at[unit_rows(owner), :], target)])
        finish(stores)

    low, full = jnp.bfloat16, jnp.float32
    return pl.pallas_call(
        body,
        in_specs=[IN_SMEM] + [ANY] * 14,
        out_specs=[ANY] * 9,
        out_shape=[
            shaped((1, hidden_width), full),
            shaped((1, width), full),
            shaped((count, width), full),
            shaped((count, width), low),
            shaped((count, width), low),
        ]
        + unit_shapes()
        + unit_shapes(),
        scratch_shapes=[
            pltpu.VMEM(rep.shape, full),
            pltpu.VMEM((1, hidden_width), full),
            pltpu.VMEM((1, hidden_width), full),
            pltpu.VMEM((1, width), full),
            pltpu.VMEM((width, hidden_width), low),
            pltpu.VMEM((hidden_width, width), low),
            pltpu.VMEM((count, width), low),
            pltpu.VMEM((count, width), low),
            pltpu.VMEM((count, width), low),
            pltpu.VMEM((count, width), low),
            pltpu.VMEM((count, width), full),
            pltpu.VMEM((count, width), low),
            pltpu.VMEM((count, hidden_width), low),
            pltpu.VMEM((count, hidden_width), low),
            pltpu.VMEM((count, hidden_width), low),
            pltpu.VMEM((count, width), low),
            pltpu.VMEM((count, width), low),
            pltpu.VMEM((width, hidden_width), low),
            pltpu.VMEM((hidden_width, width), low),
            pltpu.SemaphoreType.DMA((112,)),
        ],
        compiler_params=params(),
        cost_estimate=cost(18),
        name="mlp_all",
    )(words, rep, hidden_bias, rows_in, own, other, grad_out, *own_pieces, *pieces)


def attention_back(
    words, rep, hidden_sum, grad_sum, mask_sum, middle, own, other, grad_out, w_out, attended, qkv,
    prob, normed, weights, rows_in,
):
    count, width = middle.shape
    half = qkv.shape[1] // 3
    span = 3 * half
    pairs_of_heads = half // (2 * HEAD)
    low, full = jnp.bfloat16, jnp.float32

    def body(
        words_ref, rep_any, hidden_sum_any, grad_sum_any, mask_sum_any,
        middle_any, own_any, other_any, grad_any, w_out_any, attended_any, qkv_any, prob_any,
        normed_any, weights_any, in_any,
        grad_middle_any, back_any, sent, kept,
        rep_ref, hidden_sum_ref, grad_sum_ref, mask_sum_ref,
        middle_ref, own_ref, other_ref, grad_ref, w_out_ref, attended_ref, qkv_ref, prob_ref,
        normed_ref, weights_ref, in_ref, grad_middle_ref, back_ref, branch, grad_attended,
        grad_qkv, spread, whole, vectors, low_vectors, semaphores,
    ):
        copies = Copies(semaphores)
        early = copies.start(
            [
                (middle_any, middle_ref), (own_any, own_ref), (other_any, other_ref),
                (grad_any, grad_ref), (rep_any, rep_ref),
            ]
        )
        outer = copies.start([(w_out_any, w_out_ref), (attended_any, attended_ref)])
        inner = copies.start([(qkv_any, qkv_ref)])
        probs = copies.start(
            [(prob_any.at[pl.ds(2 * i, 2)], prob_ref.at[i]) for i in range(pairs_of_heads)]
        )
        late = copies.start(
            [(normed_any, normed_ref), (weights_any, weights_ref), (in_any, in_ref)]
            + [(hidden_sum_any, hidden_sum_ref), (grad_sum_any, grad_sum_ref)]
            + [(mask_sum_any, mask_sum_ref)]
        )
        vectors[...] = jnp.zeros_like(vectors)
        finish(early)

        @pl.loop(0, count // BLOCK)
        def _(block):
            rows = pl.ds(block * BLOCK, BLOCK)
            unit_signal, scale = norm_parts(middle_ref[rows, :])
            mine = own_ref[rows, :].astype(full)
            grad_normed = mine + other_ref[rows, :].astype(full)
            grad_middle = grad_ref[rows, :].astype(full) + norm_back(
                grad_normed, unit_signal, scale, rep_ref[2:3, :]
            )
            grad_middle_ref[rows, :] = grad_middle
            grad_branch = grad_middle.astype(low)
            branch[rows, :] = grad_branch
            vectors[1:2, :width] += jnp.sum(mine * unit_signal, axis=0, keepdims=True)
            vectors[1:2, width:] += jnp.sum(mine, axis=0, keepdims=True)
            vectors[2:3, :width] += 0.5 * jnp.sum(grad_branch.astype(full), axis=0, keepdims=True)

        stores = copies.start([(grad_middle_ref, grad_middle_any)])
        finish(outer)
        grad_attended[...] = contract_last(branch[...], w_out_ref[...]).astype(low)
        out_gradient = contract_rows(attended_ref[...], branch[...])
        for strip in range(half // 128):
            for side in range(2):
                start = side * half + strip * 128
                spread[strip, pl.ds(side, half, stride=2), :] = out_gradient[
                    :, start : start + 128
                ]
            start = span + strip * 128
            whole[:, start : start + 128] = spread[strip].astype(low)
        finish(inner)
        upper = lax.broadcasted_iota(jnp.int32, (1, 2 * HEAD), 1) >= HEAD
        finish(probs)

        @pl.loop(0, pairs_of_heads)
        def _(pair):
            lanes = [
                pl.ds(pl.multiple_of(part * half + pair * (2 * HEAD), 2 * HEAD), 2 * HEAD)
                for part in range(3)
            ]
            queries, keys, values = (qkv_ref[:, lane] for lane in lanes)
            grad = grad_attended[:, lanes[0]]
            found = []
            for side in range(2):
                chosen = upper if side else jnp.logical_not(upper)
                own_grad = jnp.where(chosen, grad, jnp.zeros_like(grad))
                low_probability = prob_ref[pair, side]
                probability = low_probability.astype(full)
                weighted = probability * contract_last(own_grad, values)
                inner_sum = jnp.sum(weighted, axis=1, keepdims=True)
                grad_scores = (weighted - probability * inner_sum).astype(low)
                found.append(
                    (
                        product(grad_scores, keys),
                        contract_rows(queries, grad_scores)[side * HEAD : (side + 1) * HEAD],
                        contract_rows(grad, low_probability)[side * HEAD : (side + 1) * HEAD],
                    )
                )
            backs = (
                jnp.where(upper, found[1][0], found[0][0]) * HEAD ** (-0.5),
                jnp.transpose(jnp.concatenate([found[0][1], found[1][1]])) * HEAD ** (-0.5),
                jnp.transpose(jnp.concatenate([found[0][2], found[1][2]])),
            )
            for lane, value in zip(lanes, backs):
                grad_qkv[:, lane] = value.astype(low)

        finish(late)

        @pl.loop(0, width // half)
        def _(part):
            columns = lanes_of(part, half)
            whole[columns, :span] = contract_rows(normed_ref[:, columns], grad_qkv[...]).astype(low)

        for target, owner in unit_targets(words_ref, sent, kept):
            stores += copies.start([(whole.at[unit_rows(owner), :], target)])

        @pl.loop(0, count // BLOCK)
        def _(block):
            rows = pl.ds(block * BLOCK, BLOCK)
            back = contract_last(grad_qkv[rows, :], weights_ref[:, :span])
            back_ref[rows, :] = back.astype(low)
            unit_signal, _ = norm_parts(in_ref[rows, :].astype(full))
            vectors[0:1, :width] += jnp.sum(back * unit_signal, axis=0, keepdims=True)
            vectors[0:1, width:] += jnp.sum(back, axis=0, keepdims=True)
            for place, part in enumerate((0, 2)):
                sums = jnp.sum(
                    grad_qkv[rows, part * half : (part + 1) * half].astype(full),
                    axis=0,
                    keepdims=True,
                )
                vectors[3:4, place * half : (place + 1) * half] += sums

        stores += copies.start([(back_ref, back_any)])
        vectors[2:3, width:] = 0.5 * grad_sum_ref[...]
        vectors[3:4, 2 * half : span] = mask_sum_ref[...]
        vectors[4:5, :] = hidden_sum_ref[...]
        low_vectors[...] = vectors[...].astype(low)
        last = pl.ds(8 * UNIT_ROWS, 16)
        stores += copies.start([(low_vectors, sent.at[last, :]), (low_vectors, kept.at[last, :])])
        finish(stores)

    return pl.pallas_call(
        body,
        in_specs=[IN_SMEM] + [ANY] * 15,
        out_specs=[ANY] * 4,
        out_shape=[shaped((count, width), full), shaped((count, width), low)] + unit_shapes(16),
        scratch_shapes=[
            pltpu.VMEM(rep.shape, full),
            pltpu.VMEM(hidden_sum.shape, full),
            pltpu.VMEM(grad_sum.shape, full),
            pltpu.VMEM(mask_sum.shape, full),
            pltpu.VMEM((count, width), full),
            pltpu.VMEM((count, width), low),
            pltpu.VMEM((count, width), low),
            pltpu.VMEM((count, width), low),
            pltpu.VMEM((half, width), low),
            pltpu.VMEM((count, half), low),
            pltpu.VMEM((count, span), low),
            pltpu.VMEM((pairs_of_heads, 2, count, count), low),
            pltpu.VMEM((count, width), low),
            pltpu.VMEM((width, UNIT_WIDTH), low),
            pltpu.VMEM((count, width), low),
            pltpu.VMEM((count, width), full),
            pltpu.VMEM((count, width), low),
            pltpu.VMEM((count, width), low),
            pltpu.VMEM((count, half), low),
            pltpu.VMEM((count, span), low),
            pltpu.VMEM((half // 128, width, 128), full),
            pltpu.VMEM((width, UNIT_WIDTH), low),
            pltpu.VMEM((16, UNIT_WIDTH), full),
            pltpu.VMEM((16, UNIT_WIDTH), low),
            pltpu.SemaphoreType.DMA((40,)),
        ],
        compiler_params=params(),
        cost_estimate=cost(22),
        name="attention_back",
    )(
        words, rep, hidden_sum, grad_sum, mask_sum, middle, own, other, grad_out, w_out, attended,
        qkv, prob, normed, weights, rows_in,
    )


def input_gradient(rows_in, own, other, grad_middle, rep):
    count, width = rows_in.shape

    def body(in_ref, own_ref, other_ref, middle_ref, rep_ref, out_ref):
        unit_signal, scale = norm_parts(in_ref[...].astype(jnp.float32))
        grad = own_ref[...].astype(jnp.float32) + other_ref[...].astype(jnp.float32)
        out_ref[...] = middle_ref[...] + norm_back(grad, unit_signal, scale, rep_ref[0:1, :])

    block = pl.BlockSpec((BLOCK, width), lambda i: (i, 0))
    return pl.pallas_call(
        body,
        grid=(count // BLOCK,),
        in_specs=[block, block, block, block, pl.BlockSpec(rep.shape, lambda i: (0, 0))],
        out_specs=block,
        out_shape=shaped((count, width), jnp.float32),
        compiler_params=params(1),
        cost_estimate=cost(5.7),
        name="input_gradient",
    )(rows_in, own, other, grad_middle, rep)


def adam_unit(units, states, strides):
    flat = [array.reshape(-1, 128) for state in states for array in state]
    terms = [array for unit in units for array in unit]
    counts = [len(unit) for unit in units]

    def body(*refs):
        terms_here, refs = refs[: len(terms)], refs[len(terms) :]
        inputs, outputs = refs[: len(flat)], refs[len(flat) :]
        for unit, column, state, start, step in strides:
            columns = slice(column * 128, (column + 1) * 128)
            skip = sum(counts[:unit])
            gradient = terms_here[skip][:, columns].astype(jnp.float32)
            for term in terms_here[skip + 1 : skip + counts[unit]]:
                gradient = gradient + term[:, columns].astype(jnp.float32)
            rows = pl.ds(start, UNIT_ROWS, stride=step)
            weight, one, two = (inputs[3 * state + i][rows, :] for i in range(3))
            updated = adam_step(weight, one, two, gradient, MATRIX_RATE, MATRIX_DECAY)
            for i in range(3):
                outputs[3 * state + i][rows, :] = updated[i]

    whole = [pl.BlockSpec(array.shape, lambda i: (0, 0)) for array in flat]
    results = pl.pallas_call(
        body,
        grid=(1,),
        in_specs=[
            pl.BlockSpec((UNIT_ROWS, term.shape[1]), lambda i: (0, 0)) for term in terms
        ]
        + whole,
        out_specs=whole,
        out_shape=[shaped(array.shape, jnp.float32) for array in flat],
        compiler_params=params(1),
        cost_estimate=cost(2.5),
        name="adam_unit",
    )(*terms, *flat)
    return [array.reshape(1, -1) for array in results]


def on_device(
    patch_rows,
    cotangent,
    mask_token,
    lengths,
    masked,
    dealing,
    qkv_master,
    qkv_first,
    qkv_second,
    out_master,
    out_first,
    out_second,
    fc1_master,
    fc1_first,
    fc1_second,
    fc2_master,
    fc2_first,
    fc2_second,
    rep_master,
    rep_first,
    rep_second,
    split_master,
    split_first,
    split_second,
):
    slot_count, capacity, feature_width = patch_rows.shape
    half_width = mask_token.shape[0]
    dp_count = lax.axis_size("dp")
    member = lax.axis_index("dp")
    core_index = lax.axis_index("mp")
    positions_here = cotangent.shape[1]
    position_span = positions_here * dp_count
    heads_here = half_width // HEAD
    row_count = slot_count * capacity
    strip_count = lengths.shape[0]
    position_rows = -(-positions_here // 4) * 4
    held_count = strip_count * positions_here
    dealt_count = strip_count * position_rows
    words = jnp.stack([member, 1 + core_index, 2 - core_index, core_index]).astype(jnp.int32)

    inputs = patch_rows.reshape(row_count, feature_width)
    split_rows = split_master[0]
    hidden_bias = split_rows[2:].reshape(1, -1)
    units, unit_a, units_later = pack_units(qkv_master, out_master, fc1_master, fc2_master)

    patch_index = jnp.arange(PATCHES, dtype=jnp.int32)
    visible_all = (patch_index[None, :] < lengths[:, None]) & (masked == 0)
    strips_here = lax.dynamic_slice_in_dim(dealing, member * slot_count, slot_count)
    visible_here = visible_all[strips_here]
    rank_here = jnp.cumsum(visible_here.astype(jnp.int32), axis=1) - 1
    counts_here = jnp.sum(visible_here.astype(jnp.int32), axis=1)
    valid_rows = jnp.arange(capacity, dtype=jnp.int32)[None, :] < counts_here[:, None]
    column_bias = jnp.where(valid_rows, 0.0, -1e30).astype(jnp.float32).reshape(1, row_count)
    padding = position_span - PATCHES
    visible_padded = jnp.pad(visible_here, ((0, 0), (0, padding)))
    rank_padded = jnp.pad(jnp.maximum(rank_here, 0), ((0, 0), (0, padding)))
    own_positions = jnp.arange(positions_here, dtype=jnp.int32) * dp_count + member
    inside = own_positions < PATCHES
    visible_own = visible_all[:, jnp.minimum(own_positions, PATCHES - 1)] & inside[None, :]
    row_time = jnp.arange(position_rows, dtype=jnp.int32)[None, :]
    strip_row = jnp.where(
        row_time < positions_here, row_time * strip_count + dealing[:, None], -1
    ).reshape(dealt_count)
    deal = (
        strip_row[:, None] == jnp.arange(held_count, dtype=jnp.int32)[None, :]
    ).astype(jnp.bfloat16)
    encoder_row = jnp.where(
        visible_padded,
        rank_padded + jnp.arange(slot_count, dtype=jnp.int32)[:, None] * capacity,
        -1,
    )
    encoder_row = jnp.transpose(
        encoder_row.reshape(slot_count, positions_here, dp_count), (2, 0, 1)
    )
    encoder_row = jnp.pad(
        encoder_row, ((0, 0), (0, 0), (0, position_rows - positions_here)), constant_values=-1
    ).reshape(dealt_count)
    pick = (
        jnp.arange(row_count, dtype=jnp.int32)[:, None] == encoder_row[None, :]
    ).astype(jnp.bfloat16)
    unseen = jnp.transpose(jnp.logical_not(visible_own) & inside[None, :]).reshape(held_count)

    cotangent_rows = jnp.transpose(
        cotangent.reshape(strip_count, positions_here, half_width), (1, 0, 2)
    ).reshape(held_count, half_width)

    def spread_out(array):
        return hop_by_core(array, 1, 2, dp_count), hop_by_core(array, 2, 1, dp_count)

    def exchanged(array):
        array = array.reshape(dp_count, slot_count * position_rows, half_width)
        array = lax.all_to_all(array, "dp", split_axis=0, concat_axis=0, tiled=True)
        return array.reshape(dealt_count, half_width)

    def columns_of(unit):
        return [hop(unit, distance, dp_count) for distance in Z_ORDER[1:]]

    def along_z(messages):
        return [hop(message, k, dp_count) for message, k in zip(messages, Z_ORDER[1:])]

    own_first, own_second = spread_out(units)
    column_a = columns_of(unit_a)
    column_a, own_first, own_second, units_later, cotangent_rows, deal, unseen = together(
        column_a, own_first, own_second, units_later, cotangent_rows, deal, unseen
    )

    column_a = join_chunks(column_a)
    first_a, second_a = spread_out(column_a)
    own_third = hop_by_core(own_first, 2, 1, dp_count)
    column_far = hop(units_later, 12, dp_count)
    dealt = product(deal, cotangent_rows).astype(jnp.bfloat16)
    mask_sum = product(unseen.astype(jnp.bfloat16)[None, :], cotangent_rows)
    first_a, second_a, own_third, dealt, mask_sum, column_bias, pick, column_far, units_later = (
        together(
            first_a, second_a, own_third, dealt, mask_sum, column_bias, pick, column_far,
            units_later,
        )
    )

    third_a = hop_by_core(first_a, 2, 1, dp_count)
    column = [hop(units_later, distance, dp_count) for distance in (4, 8)]
    third_a, column, inputs_here, dealt = together(third_a, column, inputs, dealt)

    column = join_chunks([column_far, *column])
    first, last = spread_out(column)
    returned = exchanged(dealt)
    own_pieces = (units, own_first, own_second, own_third)
    normed, qkv, prob, attended, branch, weights_a, w_output = attention_forward(
        words, inputs_here, rep_master, split_rows, column_bias, own_pieces,
        (column_a, first_a, second_a, third_a),
    )
    first, last = together(first, last)

    third = hop_by_core(first, 2, 1, dp_count)
    branch_other = swap_cores(branch)
    gathered = product(pick, returned).astype(jnp.bfloat16)
    gathered_other = swap_cores(gathered)
    grad_out = jnp.where(
        core_index == 0,
        jnp.concatenate([gathered, gathered_other], axis=1),
        jnp.concatenate([gathered_other, gathered], axis=1),
    )
    third, branch_other, grad_out = together(third, branch_other, grad_out)

    hidden_sum, grad_sum, middle, back_two, second, sent_b, kept_b, sent_c, kept_c = mlp_all(
        words, inputs, branch, branch_other, rep_master, hidden_bias, grad_out, own_pieces,
        (column, first, last, third),
    )
    middle, back_two, second, sent_b, kept_b, sent_c, kept_c = together(
        middle, back_two, second, sent_b, kept_b, sent_c, kept_c
    )

    one_c = hop_by_core(sent_c, 2, 1, dp_count)
    back_two_other = swap_cores(back_two)
    second_other = swap_cores(second)
    total = second.astype(jnp.float32) + second_other.astype(jnp.float32) + rep_master[5]
    result = (middle + total).astype(jnp.bfloat16)
    result_half = lax.dynamic_slice_in_dim(result, core_index * half_width, half_width, 1)
    outgoing = contract_rows(pick, result_half).astype(jnp.bfloat16)
    one_c, back_two_other, outgoing = together(one_c, back_two_other, outgoing)

    half_unit = 4 * UNIT_ROWS
    one_b = hop_by_core(sent_b, 2, 1, dp_count)
    two_c = hop_by_core(
        added(half_unit, 2 * half_unit, (kept_c, 0), (one_c, 0)), 1, 2, dp_count
    )
    arrived = exchanged(outgoing)
    grad_middle, back_one, sent_a, kept_a = attention_back(
        words, rep_master, hidden_sum, grad_sum, mask_sum, middle, back_two, back_two_other,
        grad_out, w_output, attended, qkv, prob, normed, weights_a, inputs,
    )
    two_c, one_b, back_one, sent_a, kept_a, arrived = together(
        two_c, one_b, back_one, sent_a, kept_a, arrived
    )

    one_a = hop_by_core(sent_a, 2, 1, dp_count)
    two_b = hop_by_core(
        added(half_unit, 2 * half_unit, (kept_b, 0), (one_b, 0)), 1, 2, dp_count
    )
    arrivals_c = along_z(last_messages(kept_c, one_c, two_c))
    full_out = contract_rows(deal, arrived)
    full_out = jnp.where(unseen[:, None], mask_token.astype(jnp.float32)[None, :], full_out)
    full_out = full_out.astype(jnp.bfloat16)
    one_a, arrivals_c, two_b, full_out, back_one = together(
        one_a, arrivals_c, two_b, full_out, back_one
    )

    two_a_sent = added(half_unit, 2 * half_unit + 16, (kept_a, 0), (one_a, 0))
    two_a = hop_by_core(two_a_sent, 1, 2, dp_count)
    arrivals_b = along_z(last_messages(kept_b, one_b, two_b))
    fc2_new = adam_unit(
        [(kept_c, one_c, two_c, *arrivals_c)],
        [(fc2_master, fc2_first, fc2_second)],
        [(0, side * 6 + j, 0, side * UNIT_ROWS * 6 + j, 6) for side in range(2) for j in range(6)],
    )
    back_one_other = swap_cores(back_one)
    two_a_sent, two_a, arrivals_b[0], back_one_other = together(
        two_a_sent, two_a, arrivals_b[0], back_one_other
    )

    messages = last_messages(kept_a, one_a, two_a, two_a_sent)
    arrivals = along_z(messages)
    fc1_new = adam_unit(
        [(kept_b, one_b, two_b, *arrivals_b)],
        [(fc1_master, fc1_first, fc1_second)],
        [(0, j, 0, j, 12) for j in range(12)],
    )
    input_grad = input_gradient(inputs, back_one, back_one_other, grad_middle, rep_master)
    arrivals, message, input_grad, *fc1_new = together(
        arrivals, messages[0], input_grad, *fc1_new
    )

    vectors = [array[UNIT_ROWS:].astype(jnp.float32) for array in (message, *arrivals)]
    vectors = (vectors[0] + vectors[1]) + (vectors[2] + vectors[3])
    rep_total = (vectors[:3] + swap_cores(vectors[:3])).reshape(rep_master.shape)
    split_total = jnp.concatenate(
        [vectors[3, : 2 * half_width], vectors[4]]
    ).reshape(split_master.shape)
    mask_total = vectors[3, 2 * half_width : 3 * half_width]
    qkv_out_new = adam_unit(
        [(kept_a, one_a, two_a, *arrivals)],
        [(qkv_master, qkv_first, qkv_second), (out_master, out_first, out_second)],
        [(0, j, 0, j, 9) for j in range(9)] + [(0, 9 + j, 1, j, 3) for j in range(3)],
    )
    full_out = full_out.reshape(positions_here, strip_count, half_width)
    full_out = jnp.transpose(full_out, (1, 0, 2))[:, :, None, :]
    input_grad = input_grad.reshape(slot_count, capacity, feature_width)
    rep_new = adam_step(rep_master, rep_first, rep_second, rep_total, VECTOR_RATE, 0.0)
    split_new = adam_step(split_master, split_first, split_second, split_total, VECTOR_RATE, 0.0)
    return (
        full_out,
        input_grad,
        mask_total,
        *qkv_out_new,
        *fc1_new,
        *fc2_new,
        *rep_new,
        *split_new,
    )


def solution(mesh):
    placed = (
        P("dp", None, None),
        P(None, None, "dp", "mp"),
        P("mp"),
        P(),
        P(),
        P(),
        P("mp", "dp"),
        P("mp", "dp"),
        P("mp", "dp"),
        P("mp", "dp"),
        P("mp", "dp"),
        P("mp", "dp"),
        P("mp", "dp"),
        P("mp", "dp"),
        P("mp", "dp"),
        P("mp", "dp"),
        P("mp", "dp"),
        P("mp", "dp"),
        P(),
        P(),
        P(),
        P("mp", None, None),
        P("mp", None, None),
        P("mp", None, None),
    )
    tuned = mesh.shape["dp"] == 16 and mesh.shape["mp"] == 2
    return jax.shard_map(
        on_device if tuned else on_device_general,
        mesh=mesh,
        in_specs=placed,
        out_specs=(
            P(None, None, "dp", "mp"),
            P("dp", None, None),
            P("mp"),
            P("mp", "dp"),
            P("mp", "dp"),
            P("mp", "dp"),
            P("mp", "dp"),
            P("mp", "dp"),
            P("mp", "dp"),
            P("mp", "dp"),
            P("mp", "dp"),
            P("mp", "dp"),
            P("mp", "dp"),
            P("mp", "dp"),
            P("mp", "dp"),
            P(),
            P(),
            P(),
            P("mp", None, None),
            P("mp", None, None),
            P("mp", None, None),
        ),
        check_vma=False,
    )
```
